32 devices in a mesh: dp: 4 (over y, x), tensor: 8 (over z, core).
Axes of the slice: x: 2, y: 2, z: 4, core: 2. Of those that a mesh axis runs over, the one named last changes fastest.
Arguments:
- inputs: bfloat16 [16384, 2048], P(('dp', 'tensor')), may hold values from -6 to 6
- block_ids: int32 [16, 1024], P('dp'), may hold values from 0 to 4, never falling along the last dimension, each value on 1 to 256 neighbouring positions
- norm_gain: bfloat16 [2048], replicated, may hold values from 0.5 to 1.5
- norm_bias: bfloat16 [2048], replicated, may hold values from -3 to 3
- query_weight: bfloat16 [2048, 2048], P('dp', 'tensor'), may hold values from -0.125 to 0.125
- query_bias: bfloat16 [2048], P('tensor'), may hold values from -3 to 3
- key_weight: bfloat16 [2048, 2048], P('dp', 'tensor'), may hold values from -0.125 to 0.125
- key_bias: bfloat16 [2048], P('tensor'), may hold values from -3 to 3
- value_weight: bfloat16 [2048, 2048], P('dp', 'tensor'), may hold values from -0.125 to 0.125
- value_bias: bfloat16 [2048], P('tensor'), may hold values from -3 to 3
- out_weight: bfloat16 [2048, 2048], P('tensor', 'dp'), may hold values from -3 to 3
- out_bias: bfloat16 [2048], replicated, may hold values from -3 to 3
- up_weight: bfloat16 [2048, 8192], P('dp', 'tensor'), may hold values from -0.125 to 0.125
- up_bias: bfloat16 [8192], P('tensor'), may hold values from -3 to 3
- down_weight: bfloat16 [8192, 2048], P('tensor', 'dp'), may hold values from -0.09375 to 0.09375
- down_bias: bfloat16 [2048], replicated, may hold values from -3 to 3
- grad_out: bfloat16 [16384, 2048], P(('dp', 'tensor')), may hold values from -6 to 6
Outputs:
- output: bfloat16 [16384, 2048], P(('dp', 'tensor'))
- input_grad: bfloat16 [16384, 2048], P(('dp', 'tensor'))
- norm_gain_grad: float32 [2048], replicated
- norm_bias_grad: float32 [2048], replicated
- query_weight_grad: float32 [2048, 2048], P('dp', 'tensor')
- query_bias_grad: float32 [2048], P('tensor')
- key_weight_grad: float32 [2048, 2048], P('dp', 'tensor')
- key_bias_grad: float32 [2048], P('tensor')
- value_weight_grad: float32 [2048, 2048], P('dp', 'tensor')
- value_bias_grad: float32 [2048], P('tensor')
- out_weight_grad: float32 [2048, 2048], P('tensor', 'dp')
- out_bias_grad: float32 [2048], replicated
- up_weight_grad: float32 [2048, 8192], P('dp', 'tensor')
- up_bias_grad: float32 [8192], P('tensor')
- down_weight_grad: float32 [8192, 2048], P('tensor', 'dp')
- down_bias_grad: float32 [2048], replicated
The draws below stay inside these ranges and needn't reach their ends.
Inputs may be any that keep to these rules, and one draw needn't show every extreme that they name: `block_ids`: in each sequence the block numbers never fall along the positions; a block spans 1 to 256 positions, and one block of each sequence spans exactly 256.
All inputs are finite; a program needn't handle non-finite values.
Results may differ from the reference program's by a relative error of at most 0.012.
The reference program's roundings to bfloat16 on the way count: a program that leaves them out, or rounds other values in their place, can miss the bound.
Values may be sent and summed in bfloat16 or wider, within the bound.
A program may use at most 320 MiB of HBM per device.

```python
import math
import jax
import jax.numpy as jnp
import numpy as np
from jax import lax

D = 2048
HEADS = 32
HEAD_DIM = 64
ROT = 32
FF = 8192
LENGTH = 1024
BLOCK = 256
NBLK = 5
SEQS = 16
TOKENS = 16384


def strengthened(array, stream_key, source, target, blocks, factor):
    def block_of(dim):
        return (jnp.arange(array.shape[dim]) // (array.shape[dim] // blocks)).reshape((-1,) + (1,) * (array.ndim - 1 - dim))

    near = jax.random.permutation(stream_key, blocks)[block_of(target)]
    second = (block_of(target) + blocks // 2) % blocks
    return jnp.where((block_of(source) == near) | (block_of(source) == second), factor * array, array)


def steps_of(own_key, shape, split, smallest, largest):
    gain = 1.0
    for dim, parts in split:
        steps = jax.random.uniform(jax.random.fold_in(jax.random.fold_in(own_key, 6), dim), (parts,), jnp.float32, smallest / len(split), largest / len(split))
        gain = gain * jnp.repeat(jnp.exp(steps), shape[dim] // parts).reshape((-1,) + (1,) * (len(shape) - 1 - dim))
    return gain


def length_profile(amount, total, most, skew):
    loads = [(1 << 20) // math.isqrt(standing ** skew) + 1 for standing in range(2, amount + 1)]
    spare, counts = total - most - (amount - 1), [1] * (amount - 1)
    while spare > 0:
        free = [i for i in range(amount - 1) if counts[i] < most]
        mass, left = sum([loads[i] for i in free]), spare
        for i in free:
            more = min(most - counts[i], max(1, left * loads[i] // mass), spare)
            counts[i] = counts[i] + more
            spare = spare - more
    return np.array([most] + counts)


def ragged_sizes(rng, number_of, total, most, skew):
    if number_of == 2:
        one = jax.random.randint(rng, (), max(1, total - most), min(most, total - 1) + 1)
        return jnp.stack([one, total - one])
    sizes = jnp.asarray(length_profile(number_of, total, most, skew), jnp.int32)
    couples = (number_of - 1) // 2
    donor, sink = sizes[1:1 + 2 * couples:2], sizes[2:2 + 2 * couples:2]
    slack = jnp.minimum(donor - 1, most - sink)
    moved = jax.random.randint(jax.random.fold_in(rng, 1), (couples,), 0, 1 << 20) % (slack + 1)
    sizes = sizes.at[1:1 + 2 * couples:2].set(donor - moved).at[2:2 + 2 * couples:2].set(sink + moved)
    return sizes[jax.random.permutation(jax.random.fold_in(rng, 2), number_of)]


def noise(stream_key, dims, width, bound, shards=(), kind=jnp.bfloat16):
    drawn = width * jax.random.normal(stream_key, dims, jnp.float32)
    if shards:
        drawn = drawn * steps_of(stream_key, dims, shards, -0.22, 0.18)
    return jnp.clip(drawn, -bound, bound).astype(kind)


def bell_draw_with(stream_key, shape, deviation, bound, split, heavy, held_as=jnp.bfloat16):
    array = deviation * jax.random.normal(stream_key, shape, jnp.float32)
    if split:
        array = array * steps_of(stream_key, shape, split, -0.22, 0.18)
    return jnp.clip(strengthened(array, jax.random.fold_in(stream_key, 3), *heavy), -bound, bound).astype(held_as)


def setup_inputs(seed: int = 0) -> dict:
    keys = jax.random.split(jax.random.key(seed), 18)
    inputs = bell_draw_with(keys[0], (TOKENS, D), 1.0, 6.0, ((0, 32),), (0, 1, 32, 2.75))
    block_ids = jax.vmap(lambda own: jnp.searchsorted(jnp.cumsum(ragged_sizes(own, NBLK, LENGTH, BLOCK, 1)), jnp.arange(LENGTH), side="right"))(jax.random.split(keys[1], SEQS)).reshape((SEQS, LENGTH)).astype(jnp.int32)
    norm_gain = jnp.clip(1.0 + 0.1 * jax.random.normal(keys[2], (D,), jnp.float32), 0.5, 1.5).astype(jnp.bfloat16)
    norm_bias = noise(keys[3], (D,), 0.5, 3.0)
    query_weight = noise(keys[4], (D, D), D ** -0.5, 0.125, ((0, 4), (1, 8)))
    query_bias = noise(keys[5], (D,), 0.5, 3.0, ((0, 8),))
    key_weight = noise(keys[6], (D, D), D ** -0.5, 0.125, ((0, 4), (1, 8)))
    key_bias = noise(keys[7], (D,), 0.5, 3.0, ((0, 8),))
    value_weight = noise(keys[8], (D, D), D ** -0.5, 0.125, ((0, 4), (1, 8)))
    value_bias = noise(keys[9], (D,), 0.5, 3.0, ((0, 8),))
    out_weight = bell_draw_with(keys[10], (D, D), (max(1, D * 4 // LENGTH)) ** -0.5, 3.0, ((0, 8), (1, 4)), (0, 1, 8, 2.0))
    out_bias = noise(keys[11], (D,), 0.5, 3.0)
    up_weight = noise(keys[12], (D, FF), D ** -0.5, 0.125, ((0, 4), (1, 8)))
    up_bias = noise(keys[13], (FF,), 0.5, 3.0, ((0, 8),))
    down_weight = bell_draw_with(keys[14], (FF, D), FF ** -0.5, 0.09375, ((0, 8), (1, 4)), (0, 1, 8, 2.0))
    down_bias = noise(keys[15], (D,), 0.5, 3.0)
    grad_out = bell_draw_with(keys[16], (TOKENS, D), 1.0, 6.0, ((0, 32),), (0, 1, 32, 2.75))
    return dict(inputs=inputs, block_ids=block_ids, norm_gain=norm_gain, norm_bias=norm_bias, query_weight=query_weight, query_bias=query_bias, key_weight=key_weight, key_bias=key_bias, value_weight=value_weight, value_bias=value_bias, out_weight=out_weight, out_bias=out_bias, up_weight=up_weight, up_bias=up_bias, down_weight=down_weight, down_bias=down_bias, grad_out=grad_out)


@jax.custom_vjp
def low(v):
    return lax.optimization_barrier(v.astype(jnp.bfloat16)).astype(jnp.float32)

@jax.custom_vjp
def low_back(v):
    return v

def low_keep(v):
    return (low(v), None)

def low_pass(kept, grad):
    return (grad,)

def back_keep(v):
    return (v, None)

def back_low(kept, grad):
    return (low(grad),)
low.defvjp(low_keep, low_pass)
low_back.defvjp(back_keep, back_low)
eps_norm = 1e-05

def matmul(left, right):
    return jnp.dot(left, right, precision=lax.Precision.HIGHEST, preferred_element_type=jnp.float32)

def normalize(values, gain_in, shift_in):
    center = lax.optimization_barrier(jnp.mean(values, axis=-1, keepdims=True))
    centered = values - center
    variance = lax.optimization_barrier(jnp.mean(centered * centered, axis=-1, keepdims=True))
    return centered * lax.rsqrt(variance + eps_norm) * gain_in + shift_in

def rotary_tables(length, rot_width):
    halves = rot_width // 2
    exponent = jnp.arange(halves, dtype=jnp.float32) * (2.0 / rot_width)
    frequency = jnp.power(10000.0, -exponent)
    angles = jnp.arange(length, dtype=jnp.float32)[:, None] * frequency[None, :]
    angles = jnp.concatenate([angles, angles], axis=1)
    return (jnp.cos(angles), jnp.sin(angles))

def rotate(per_head, cos_table, sin_table):
    rot_width = cos_table.shape[-1]
    halves = rot_width // 2
    first_half = per_head[..., :halves]
    second_half = per_head[..., halves:rot_width]
    turned = jnp.concatenate([-second_half, first_half], axis=-1)
    rotated = per_head[..., :rot_width] * cos_table[:, None, :] + turned * sin_table[:, None, :]
    return jnp.concatenate([rotated, per_head[..., rot_width:]], axis=-1)

def block_layer(seq_rows, params, block_row):
    norm_gain, norm_bias, query_weight, query_bias, key_weight, key_bias, value_weight, value_bias, out_weight, out_bias, up_weight, up_bias, down_weight, down_bias = params
    length = seq_rows.shape[0]
    normed = low(normalize(seq_rows, norm_gain, norm_bias))
    cos_table, sin_table = rotary_tables(length, ROT)
    query_pre = low_back(matmul(normed, query_weight) + query_bias).reshape(length, HEADS, HEAD_DIM)
    key_pre = low_back(matmul(normed, key_weight) + key_bias).reshape(length, HEADS, HEAD_DIM)
    queries = low(rotate(query_pre, cos_table, sin_table))
    key_rows = low(rotate(key_pre, cos_table, sin_table))
    value_rows = low(low_back(matmul(normed, value_weight) + value_bias)).reshape(length, HEADS, HEAD_DIM)
    scores = jnp.einsum('qhd,khd->hqk', queries, key_rows, precision=lax.Precision.HIGHEST) * HEAD_DIM ** (-0.5)
    allowed = block_row[None, :] <= block_row[:, None]
    scores = low_back(jnp.where(allowed[None, :, :], scores, -1000000000.0))
    probs_low = low(jax.nn.softmax(scores, axis=-1))
    attended = jnp.einsum('hqk,khd->qhd', probs_low, value_rows, precision=lax.Precision.HIGHEST).reshape(length, D)
    attended = low(low_back(attended))
    hidden = low_back(matmul(normed, up_weight) + up_bias)
    active = low(jax.nn.gelu(hidden, approximate=True))
    return seq_rows + matmul(attended, out_weight) + out_bias + matmul(active, down_weight) + down_bias

def reference(inputs, block_ids, norm_gain, norm_bias, query_weight, query_bias, key_weight, key_bias, value_weight, value_bias, out_weight, out_bias, up_weight, up_bias, down_weight, down_bias, grad_out):
    params = tuple((param_item.astype(jnp.float32) for param_item in (norm_gain, norm_bias, query_weight, query_bias, key_weight, key_bias, value_weight, value_bias, out_weight, out_bias, up_weight, up_bias, down_weight, down_bias)))
    sequences = inputs.astype(jnp.float32).reshape(SEQS, LENGTH, D)
    upstream = grad_out.astype(jnp.float32).reshape(SEQS, LENGTH, D)
    zero_sums = tuple((jnp.zeros_like(param_item) for param_item in params))

    def one_sequence(grad_sums, packed):
        seq_rows, block_row, seq_grad = packed

        def run_layer(rows_in, weights_in):
            return block_layer(rows_in, weights_in, block_row)
        result, pull_back = jax.vjp(run_layer, seq_rows, params)
        row_grad, weight_grads = pull_back(seq_grad)
        grad_sums = tuple((first_part + second_part for first_part, second_part in zip(grad_sums, weight_grads)))
        return (grad_sums, (result.astype(jnp.bfloat16), row_grad.astype(jnp.bfloat16)))
    grad_sums, (outputs, input_grads) = lax.scan(one_sequence, zero_sums, (sequences, block_ids, upstream))
    return (outputs.reshape(TOKENS, D), input_grads.reshape(TOKENS, D), grad_sums[0], grad_sums[1], grad_sums[2], grad_sums[3], grad_sums[4], grad_sums[5], grad_sums[6], grad_sums[7], grad_sums[8], grad_sums[9], grad_sums[10], grad_sums[11], grad_sums[12], grad_sums[13])
```

```python
import functools

import jax
import jax.numpy as jnp
from jax import lax
from jax.experimental import pallas as pl
from jax.experimental.pallas import tpu as pltpu
from jax.sharding import PartitionSpec as P

HEAD_DIM = 64
ROT = 32
SPAN = 256
EPS = 1e-05
F32 = jnp.float32
BF16 = jnp.bfloat16
VMEM_BYTES = 60 * 2**20


def nn(a, b):
    return jnp.dot(a, b, preferred_element_type=F32)


def nt(a, b):
    return lax.dot_general(a, b, (((1,), (1,)), ((), ())), preferred_element_type=F32)


def tn(a, b):
    return lax.dot_general(a, b, (((0,), (0,)), ((), ())), preferred_element_type=F32)


def params(semantics):
    return pltpu.CompilerParams(dimension_semantics=semantics, vmem_limit_bytes=VMEM_BYTES)


def cost(flops, bytes_accessed, transcendentals=0):
    return pl.CostEstimate(
        flops=int(flops), bytes_accessed=int(bytes_accessed), transcendentals=int(transcendentals)
    )


def once(shape, index_map):
    return pl.BlockSpec(shape, index_map, pipeline_mode=pl.Buffered(1))


def rotary_tables(length):
    halves = ROT // 2
    exponent = jnp.arange(halves, dtype=F32) * (2.0 / ROT)
    frequency = jnp.power(10000.0, -exponent)
    angles = jnp.arange(length, dtype=F32)[:, None] * frequency[None, :]
    cos, sin = jnp.cos(angles), jnp.sin(angles)
    zero = jnp.zeros((length, halves), F32)
    rest = HEAD_DIM - ROT
    head = lambda a, b, fill: jnp.concatenate([a, b, jnp.full((length, rest), fill, F32)], axis=1)
    return tuple(
        jnp.concatenate([t, t], axis=1)
        for t in (head(cos, cos, 1.0), head(-sin, zero, 0.0), head(zero, sin, 0.0))
    )


def rotated(values, cos, low, high):
    halves = ROT // 2
    pieces = []
    for start in range(0, values.shape[1], 128):
        u = values[:, start : start + 128]
        pieces.append(
            u * cos + pltpu.roll(u, 128 - halves, 1) * low + pltpu.roll(u, halves, 1) * high
        )
    return pieces[0] if len(pieces) == 1 else jnp.concatenate(pieces, axis=1)


GELU_A = 0.7978845608028654
GELU_B = 0.044715


def gelu(v):
    return 0.5 * v * (1.0 + jnp.tanh(GELU_A * (v + GELU_B * (v * v * v))))


def gelu_slope(v):
    square = v * v
    t = jnp.tanh(GELU_A * (v + GELU_B * (v * square)))
    return 0.5 * (1.0 + t) + 0.5 * v * (1.0 - t * t) * (GELU_A * (1.0 + 3.0 * GELU_B * square))


def project_kernel(width, x, w, bias, cos, low, high, q, k, v, active, hidden):
    rows = x[...]
    tables = (cos[...], low[...], high[...])
    q[...] = (
        rotated(nn(rows, w[:, :width]) + bias[:, :width], *tables).astype(BF16)
        * jnp.asarray(HEAD_DIM**-0.5, BF16)
    )
    k[...] = rotated(
        nn(rows, w[:, width : 2 * width]) + bias[:, width : 2 * width], *tables
    ).astype(BF16)
    v[...] = (nn(rows, w[:, 2 * width : 3 * width]) + bias[:, 2 * width : 3 * width]).astype(BF16)
    units = hidden.shape[1]
    step = min(256, units)
    for start in range(0, units, step):
        at = slice(3 * width + start, 3 * width + start + step)
        h = nn(rows, w[:, at]) + bias[:, at]
        hidden[:, start : start + step] = h
        active[:, start : start + step] = gelu(h).astype(BF16)


def project(x, w, bias, tables, width, units, length, tile=512):
    rows, depth = x.shape
    per = length // tile
    row = lambda n: pl.BlockSpec((tile, n), lambda i: (i, 0))
    table = pl.BlockSpec((tile, 128), lambda i: (i % per, 0))
    total = 3 * width + units
    return pl.pallas_call(
        functools.partial(project_kernel, width),
        grid=(rows // tile,),
        in_specs=[
            row(depth),
            once((depth, total), lambda i: (0, 0)),
            once((1, total), lambda i: (0, 0)),
            table,
            table,
            table,
        ],
        out_specs=[row(width), row(width), row(width), row(units), row(units)],
        out_shape=[
            jax.ShapeDtypeStruct((rows, width), BF16),
            jax.ShapeDtypeStruct((rows, width), BF16),
            jax.ShapeDtypeStruct((rows, width), BF16),
            jax.ShapeDtypeStruct((rows, units), BF16),
            jax.ShapeDtypeStruct((rows, units), F32),
        ],
        compiler_params=params(("arbitrary",)),
        cost_estimate=cost(2 * rows * depth * total, 2 * depth * (rows + total) + rows * units * 6),
        name="project",
    )(x, w, bias, *tables)


def mix_kernel(attended, active, w, out):
    parts, inner, columns = w.shape
    width = attended.shape[1]
    for d in range(parts):
        out[:, d * columns : (d + 1) * columns] = (
            nn(attended[...], w[d, :width, :]) + nn(active[...], w[d, width:, :])
        ).astype(out.dtype)


def mix(attended, active, w, tile=512):
    rows, width = attended.shape
    units = active.shape[1]
    parts, inner, columns = w.shape
    row = lambda n: pl.BlockSpec((tile, n), lambda i: (i, 0))
    return pl.pallas_call(
        mix_kernel,
        grid=(rows // tile,),
        in_specs=[row(width), row(units), once(w.shape, lambda i: (0, 0, 0))],
        out_specs=row(parts * columns),
        out_shape=jax.ShapeDtypeStruct((rows, parts * columns), BF16),
        compiler_params=params(("arbitrary",)),
        cost_estimate=cost(2 * rows * inner * parts * columns, 2 * inner * (rows + parts * columns)),
        name="mix",
    )(attended, active, w)


def unmix_kernel(g, w, hidden, attended_grad, hidden_grad, sums):
    parts, inner, columns = w.shape
    width = attended_grad.shape[1]
    units = hidden.shape[1]

    @pl.when(pl.program_id(0) == 0)
    def _():
        sums[...] = jnp.zeros_like(sums)

    def back(lo, hi):
        total = nt(g[:, :columns], w[0, lo:hi, :])
        for d in range(1, parts):
            total = total + nt(g[:, d * columns : (d + 1) * columns], w[d, lo:hi, :])
        return total

    attended_grad[...] = back(0, width).astype(BF16)
    step = min(256, units)
    for start in range(0, units, step):
        at = slice(start, start + step)
        low = (back(width + start, width + start + step) * gelu_slope(hidden[:, at])).astype(BF16)
        hidden_grad[:, at] = low
        sums[:, at] += jnp.sum(low.astype(F32), axis=0, keepdims=True)


def unmix(g, w, hidden, width, tile=512):
    rows, depth = g.shape
    units = hidden.shape[1]
    parts, inner, columns = w.shape
    row = lambda n: pl.BlockSpec((tile, n), lambda i: (i, 0))
    return pl.pallas_call(
        unmix_kernel,
        grid=(rows // tile,),
        in_specs=[row(depth), once(w.shape, lambda i: (0, 0, 0)), row(units)],
        out_specs=[row(width), row(units), pl.BlockSpec((1, units), lambda i: (0, 0))],
        out_shape=[
            jax.ShapeDtypeStruct((rows, width), BF16),
            jax.ShapeDtypeStruct((rows, units), BF16),
            jax.ShapeDtypeStruct((1, units), F32),
        ],
        compiler_params=params(("arbitrary",)),
        cost_estimate=cost(2 * rows * inner * depth, 2 * depth * (rows + inner) + rows * units * 6),
        name="unmix",
    )(g, w, hidden)


def unproject_kernel(qkv_grad, hidden_grad, w, out):
    three = qkv_grad.shape[1]
    depth = w.shape[0]
    step = min(512, depth)
    for start in range(0, depth, step):
        out[:, start : start + step] = (
            nt(qkv_grad[...], w[start : start + step, :three])
            + nt(hidden_grad[...], w[start : start + step, three:])
        ).astype(out.dtype)


def unproject(qkv_grad, hidden_grad, w, tile=512):
    rows, three = qkv_grad.shape
    units = hidden_grad.shape[1]
    depth, total = w.shape
    row = lambda n: pl.BlockSpec((tile, n), lambda i: (i, 0))
    return pl.pallas_call(
        unproject_kernel,
        grid=(rows // tile,),
        in_specs=[row(three), row(units), once(w.shape, lambda i: (0, 0))],
        out_specs=row(depth),
        out_shape=jax.ShapeDtypeStruct((rows, depth), BF16),
        compiler_params=params(("arbitrary",)),
        cost_estimate=cost(2 * rows * total * depth, 2 * depth * (rows + total)),
        name="unproject",
    )(qkv_grad, hidden_grad, w)


def outer_kernel(a, b, out):
    out[...] = tn(a[...], b[...]).astype(out.dtype)


def outer_rows(x, d, tile=512):
    rows, depth = x.shape
    n = d.shape[1]
    tile = min(tile, depth)
    return pl.pallas_call(
        outer_kernel,
        grid=(depth // tile,),
        in_specs=[pl.BlockSpec((rows, tile), lambda i: (0, i)), once((rows, n), lambda i: (0, 0))],
        out_specs=pl.BlockSpec((tile, n), lambda i: (i, 0)),
        out_shape=jax.ShapeDtypeStruct((depth, n), BF16),
        compiler_params=params(("arbitrary",)),
        cost_estimate=cost(2 * rows * depth * n, 2 * (rows * (depth + n) + depth * n)),
        name="outer_rows",
    )(x, d)


def outer_columns_kernel(a, b, g, out):
    width = a.shape[1]
    out[0, :width, :] = tn(a[...], g[...]).astype(out.dtype)
    out[0, width:, :] = tn(b[...], g[...]).astype(out.dtype)


def outer_columns(a, b, g, parts):
    rows, depth = g.shape
    width, units = a.shape[1], b.shape[1]
    tile = depth // parts
    return pl.pallas_call(
        outer_columns_kernel,
        grid=(parts,),
        in_specs=[
            once((rows, width), lambda i: (0, 0)),
            once((rows, units), lambda i: (0, 0)),
            pl.BlockSpec((rows, tile), lambda i: (0, i)),
        ],
        out_specs=pl.BlockSpec((1, width + units, tile), lambda i: (i, 0, 0)),
        out_shape=jax.ShapeDtypeStruct((parts, width + units, tile), BF16),
        compiler_params=params(("arbitrary",)),
        cost_estimate=cost(
            2 * rows * depth * (width + units), 2 * (rows * (depth + width + units) + depth * (width + units))
        ),
        name="outer_columns",
    )(a, b, g)


def head_lanes(width, head):
    return lax.broadcasted_iota(jnp.int32, (1, width), 1) // HEAD_DIM == head


def attend_kernel(q, k, v, column_ids, row_ids, out, log_sums):
    length, width = q.shape
    heads = width // HEAD_DIM
    tile = min(SPAN, length)
    lanes = lax.broadcasted_iota(jnp.int32, (1, 128), 1)
    for begin in range(0, length, tile):
        end = min(length, begin + tile + SPAN)
        q_ids = column_ids[begin : begin + tile, :]
        blocked = row_ids[:, begin:end] > q_ids
        rows = q[begin : begin + tile, :]

        def one_head(head, carry):
            total, sums = carry
            mine = head_lanes(width, head)
            scores = nt(jnp.where(mine, rows, jnp.zeros_like(rows)), k[:end, :])
            tail = jnp.where(blocked, -1e9, scores[:, begin:])
            scores = jnp.concatenate([scores[:, :begin], tail], axis=1) if begin else tail
            highest = jnp.max(scores, axis=1, keepdims=True)
            powers = jnp.exp(scores - highest)
            amount = jnp.sum(powers, axis=1, keepdims=True)
            low = (powers * (1.0 / amount)).astype(BF16)
            total = jnp.where(mine, nn(low, v[:end, :]), total)
            sums = jnp.where(lanes == head, highest + jnp.log(amount), sums)
            return total, sums

        total, sums = jnp.zeros((tile, width), F32), jnp.zeros((tile, 128), F32)
        for head in range(heads):
            total, sums = one_head(head, (total, sums))
        out[begin : begin + tile, :] = total.astype(BF16)
        log_sums[:, begin : begin + tile] = sums.T[:8, :]


def attend(q, k, v, column_ids, row_ids):
    rows, width = q.shape
    seqs, _, length = row_ids.shape
    heads = width // HEAD_DIM
    seq = pl.BlockSpec((length, width), lambda s: (s, 0))
    return pl.pallas_call(
        attend_kernel,
        grid=(seqs,),
        in_specs=[
            seq,
            seq,
            seq,
            pl.BlockSpec((length, 1), lambda s: (s, 0)),
            pl.BlockSpec((None, 1, length), lambda s: (s, 0, 0)),
        ],
        out_specs=[seq, pl.BlockSpec((8, length), lambda s: (0, s))],
        out_shape=[
            jax.ShapeDtypeStruct((rows, width), BF16),
            jax.ShapeDtypeStruct((8, rows), F32),
        ],
        compiler_params=params(("arbitrary",)),
        cost_estimate=cost(
            8 * seqs * heads * length * length * 256 * 0.8, 8 * rows * width, seqs * heads * length**2
        ),
        name="attend",
    )(q, k, v, column_ids, row_ids)


def unattend_kernel(
    q, k, v, g, log_sums, column_ids, row_ids, cos, low, high, out, sums, key_total, value_total
):
    length, width = q.shape
    heads = width // HEAD_DIM
    tile = min(SPAN, length)
    tables = (cos[...], -low[...], -high[...])

    @pl.when(pl.program_id(0) == 0)
    def _():
        sums[...] = jnp.zeros_like(sums)

    key_total[...] = jnp.zeros_like(key_total)
    value_total[...] = jnp.zeros_like(value_total)
    for begin in range(0, length, tile):
        end = min(length, begin + tile + SPAN)
        at = slice(begin, begin + tile)
        blocked = column_ids[begin:end, :] > row_ids[:, at]
        q_rows, g_rows = q[at, :], g[at, :]
        query_total = jnp.zeros((tile, width), F32)
        for head in range(heads):
            mine = head_lanes(width, head)
            q_head = jnp.where(mine, q_rows, jnp.zeros_like(q_rows))
            g_head = jnp.where(mine, g_rows, jnp.zeros_like(g_rows))
            scores = nt(k[:end, :], q_head)
            tail = jnp.where(blocked, -1e9, scores[begin:, :])
            scores = jnp.concatenate([scores[:begin, :], tail], axis=0) if begin else tail
            probs = jnp.exp(scores - log_sums[head : head + 1, at])
            value_total[:end, :] += nn(probs.astype(BF16), g_head)
            prob_grad = nt(v[:end, :], g_head)
            inner = jnp.sum(prob_grad * probs, axis=0, keepdims=True)
            score_grad = (probs * (prob_grad - inner)).astype(BF16)
            key_total[:end, :] += nn(score_grad, q_head)
            query_total = jnp.where(mine, tn(score_grad, k[:end, :]), query_total)
        turned = rotated(query_total * HEAD_DIM**-0.5, *(t[at, :] for t in tables)).astype(BF16)
        out[at, :width] = turned
        sums[:, :width] += jnp.sum(turned.astype(F32), axis=0, keepdims=True)
    turned = rotated(key_total[...], *tables).astype(BF16)
    out[:, width : 2 * width] = turned
    sums[:, width : 2 * width] += jnp.sum(turned.astype(F32), axis=0, keepdims=True)
    turned = value_total[...].astype(BF16)
    out[:, 2 * width :] = turned
    sums[:, 2 * width :] += jnp.sum(turned.astype(F32), axis=0, keepdims=True)


def unattend(q, k, v, g, log_sums, column_ids, row_ids, tables):
    rows, width = q.shape
    seqs, _, length = row_ids.shape
    heads = width // HEAD_DIM
    seq = pl.BlockSpec((length, width), lambda s: (s, 0))
    table = once((length, 128), lambda s: (0, 0))
    return pl.pallas_call(
        unattend_kernel,
        grid=(seqs,),
        in_specs=[
            seq,
            seq,
            seq,
            seq,
            pl.BlockSpec((8, length), lambda s: (0, s)),
            pl.BlockSpec((length, 1), lambda s: (s, 0)),
            pl.BlockSpec((None, 1, length), lambda s: (s, 0, 0)),
            table,
            table,
            table,
        ],
        out_specs=[
            pl.BlockSpec((length, 3 * width), lambda s: (s, 0)),
            pl.BlockSpec((1, 3 * width), lambda s: (0, 0)),
        ],
        out_shape=[
            jax.ShapeDtypeStruct((rows, 3 * width), BF16),
            jax.ShapeDtypeStruct((1, 3 * width), F32),
        ],
        scratch_shapes=[pltpu.VMEM((length, width), F32), pltpu.VMEM((length, width), F32)],
        compiler_params=params(("arbitrary",)),
        cost_estimate=cost(
            20 * seqs * heads * length * length * 256 * 0.8,
            14 * rows * width,
            seqs * heads * length**2,
        ),
        name="unattend",
    )(q, k, v, g, log_sums, column_ids, row_ids, *tables)


def per_device(
    inputs,
    block_ids,
    norm_gain,
    norm_bias,
    query_weight,
    query_bias,
    key_weight,
    key_bias,
    value_weight,
    value_bias,
    out_weight,
    out_bias,
    up_weight,
    up_bias,
    down_weight,
    down_bias,
    grad_out,
):
    seqs, length = block_ids.shape
    width = query_weight.shape[1]
    units = up_weight.shape[1]
    groups = lax.axis_size("dp")
    gain, shift = norm_gain.astype(F32), norm_bias.astype(F32)

    x = inputs.astype(F32)
    center = jnp.mean(x, axis=-1, keepdims=True)
    centered = x - center
    scale = lax.rsqrt(jnp.mean(centered * centered, axis=-1, keepdims=True) + EPS)
    normed = (centered * scale * gain + shift).astype(BF16)

    first = jnp.concatenate([query_weight, key_weight, value_weight, up_weight], axis=1)
    second = jnp.concatenate([out_weight, down_weight], axis=0)
    first_full = lax.all_gather(first, "dp", axis=0, tiled=True)
    rows = lax.all_gather(normed, "tensor", axis=0, tiled=True)
    second_full = lax.all_gather(second, "dp", axis=0)
    upstream = lax.all_gather(grad_out, "tensor", axis=0, tiled=True)
    bias = jnp.concatenate([query_bias, key_bias, value_bias, up_bias]).astype(F32)[None, :]
    tables = rotary_tables(length)
    column_ids = block_ids.reshape(seqs * length, 1)
    row_ids = block_ids.reshape(seqs, 1, length)

    q, k, v, active, hidden = project(rows, first_full, bias, tables, width, units, length)
    attended, log_sums = attend(q, k, v, column_ids, row_ids)
    partial = mix(attended, active, second_full)
    branch = lax.psum_scatter(partial, "tensor", scatter_dimension=0, tiled=True)
    output = (
        x + branch.astype(F32) + out_bias.astype(F32) + down_bias.astype(F32)
    ).astype(BF16)

    attended_grad, hidden_grad, up_sum = unmix(upstream, second_full, hidden, width)
    second_grad = outer_columns(attended, active, upstream, groups)
    qkv_grad, qkv_sum = unattend(
        q, k, v, attended_grad, log_sums, column_ids, row_ids, tables
    )
    normed_part = unproject(qkv_grad, hidden_grad, first_full)
    normed_grad = lax.psum_scatter(
        normed_part, "tensor", scatter_dimension=0, tiled=True
    ).astype(F32)
    up_grad = outer_rows(rows, hidden_grad)
    first_grad = outer_rows(rows, qkv_grad)

    second_grad = lax.psum_scatter(second_grad, "dp", scatter_dimension=0).astype(F32)
    up_grad = lax.psum_scatter(up_grad, "dp", scatter_dimension=0, tiled=True).astype(F32)
    first_grad = lax.psum_scatter(first_grad, "dp", scatter_dimension=0, tiled=True).astype(F32)

    hat = centered * scale
    e = normed_grad * gain
    input_grad = (
        grad_out.astype(F32)
        + (
            e
            - jnp.mean(e, axis=-1, keepdims=True)
            - hat * jnp.mean(e * hat, axis=-1, keepdims=True)
        )
        * scale
    ).astype(BF16)
    gain_grad, shift_grad, outer_bias_grad = lax.psum(
        (
            jnp.sum(normed_grad * hat, axis=0),
            jnp.sum(normed_grad, axis=0),
            jnp.sum(grad_out, axis=0, dtype=F32),
        ),
        ("dp", "tensor"),
    )
    qkv_sum, up_sum = lax.psum((qkv_sum[0], up_sum[0]), "dp")
    return (
        output,
        input_grad,
        gain_grad,
        shift_grad,
        first_grad[:, :width],
        qkv_sum[:width],
        first_grad[:, width : 2 * width],
        qkv_sum[width : 2 * width],
        first_grad[:, 2 * width :],
        qkv_sum[2 * width :],
        second_grad[:width],
        outer_bias_grad,
        up_grad,
        up_sum,
        second_grad[width:],
        outer_bias_grad,
    )


def solution(mesh):
    tokens = P(("dp", "tensor"), None)
    down = P("dp", "tensor")
    across = P("tensor", "dp")
    part = P("tensor")
    return jax.shard_map(
        per_device,
        mesh=mesh,
        in_specs=(
            tokens,
            P("dp", None),
            P(),
            P(),
            down,
            part,
            down,
            part,
            down,
            part,
            across,
            P(),
            down,
            part,
            across,
            P(),
            tokens,
        ),
        out_specs=(
            tokens,
            tokens,
            P(),
            P(),
            down,
            part,
            down,
            part,
            down,
            part,
            across,
            P(),
            down,
            part,
            across,
            P(),
        ),
        check_vma=False,
    )
```

```python
import functools

import jax
import jax.numpy as jnp
from jax import lax
from jax.experimental import pallas as pl
from jax.experimental.pallas import tpu as pltpu
from jax.sharding import PartitionSpec as P

HEAD_DIM = 64
ROT = 32
SPAN = 256
EPS = 1e-05
F32 = jnp.float32
BF16 = jnp.bfloat16
VMEM_BYTES = 60 * 2**20


def nn(a, b):
    return jnp.dot(a, b, preferred_element_type=F32)


def nt(a, b):
    return lax.dot_general(a, b, (((1,), (1,)), ((), ())), preferred_element_type=F32)


def tn(a, b):
    return lax.dot_general(a, b, (((0,), (0,)), ((), ())), preferred_element_type=F32)


def params(semantics):
    return pltpu.CompilerParams(dimension_semantics=semantics, vmem_limit_bytes=VMEM_BYTES)


def cost(flops, bytes_accessed, transcendentals=0):
    return pl.CostEstimate(
        flops=int(flops) // 10,
        bytes_accessed=int(bytes_accessed) // 10,
        transcendentals=int(transcendentals) // 10,
    )


def once(shape, index_map):
    return pl.BlockSpec(shape, index_map, pipeline_mode=pl.Buffered(1))


def rotary_tables(length):
    halves = ROT // 2
    exponent = jnp.arange(halves, dtype=F32) * (2.0 / ROT)
    frequency = jnp.power(10000.0, -exponent)
    angles = jnp.arange(length, dtype=F32)[:, None] * frequency[None, :]
    cos, sin = jnp.cos(angles), jnp.sin(angles)
    zero = jnp.zeros((length, halves), F32)
    rest = HEAD_DIM - ROT
    head = lambda a, b, fill: jnp.concatenate([a, b, jnp.full((length, rest), fill, F32)], axis=1)
    return tuple(
        jnp.concatenate([t, t], axis=1)
        for t in (head(cos, cos, 1.0), head(-sin, zero, 0.0), head(zero, sin, 0.0))
    )


def rotated(values, cos, low, high):
    halves = ROT // 2
    pieces = []
    for start in range(0, values.shape[1], 128):
        u = values[:, start : start + 128]
        pieces.append(
            u * cos + pltpu.roll(u, 128 - halves, 1) * low + pltpu.roll(u, halves, 1) * high
        )
    return pieces[0] if len(pieces) == 1 else jnp.concatenate(pieces, axis=1)


GELU_A = 0.7978845608028654
GELU_B = 0.044715


def gelu(v):
    return 0.5 * v * (1.0 + jnp.tanh(GELU_A * (v + GELU_B * (v * v * v))))


def gelu_slope(v):
    square = v * v
    t = jnp.tanh(GELU_A * (v + GELU_B * (v * square)))
    return 0.5 * (1.0 + t) + 0.5 * v * (1.0 - t * t) * (GELU_A * (1.0 + 3.0 * GELU_B * square))


def norm_kernel(x, gain, shift, out):
    values = x[...].astype(F32)
    centered = values - jnp.mean(values, axis=1, keepdims=True)
    scale = lax.rsqrt(jnp.mean(centered * centered, axis=1, keepdims=True) + EPS)
    out[...] = (centered * scale * gain[...] + shift[...]).astype(BF16)


def norm(x, gain, shift, tile=128):
    rows, depth = x.shape
    row = pl.BlockSpec((tile, depth), lambda i: (i, 0))
    one = once((1, depth), lambda i: (0, 0))
    return pl.pallas_call(
        norm_kernel,
        grid=(rows // tile,),
        in_specs=[row, one, one],
        out_specs=row,
        out_shape=jax.ShapeDtypeStruct((rows, depth), BF16),
        compiler_params=params(("arbitrary",)),
        cost_estimate=cost(10 * rows * depth, 4 * rows * depth),
        name="norm",
    )(x, gain, shift)


def unnorm_kernel(terms, x, g, gain, *refs):
    parts, (out, gain_sum, shift_sum) = refs[:terms], refs[terms:]

    @pl.when(pl.program_id(0) == 0)
    def _():
        gain_sum[...] = jnp.zeros_like(gain_sum)
        shift_sum[...] = jnp.zeros_like(shift_sum)

    values = x[...].astype(F32)
    centered = values - jnp.mean(values, axis=1, keepdims=True)
    scale = lax.rsqrt(jnp.mean(centered * centered, axis=1, keepdims=True) + EPS)
    hat = centered * scale
    back = parts[0][...].astype(F32)
    for part in parts[1:]:
        back = back + part[...].astype(F32)
    gain_sum[...] += jnp.sum(back * hat, axis=0, keepdims=True)
    shift_sum[...] += jnp.sum(back, axis=0, keepdims=True)
    e = back * gain[...]
    inner = (
        e - jnp.mean(e, axis=1, keepdims=True) - hat * jnp.mean(e * hat, axis=1, keepdims=True)
    )
    out[...] = (g[...].astype(F32) + inner * scale).astype(BF16)


def unnorm(x, g, gain, parts, tile=128):
    rows, depth = x.shape
    row = pl.BlockSpec((tile, depth), lambda i: (i, 0))
    one = once((1, depth), lambda i: (0, 0))
    late = [
        pl.BlockSpec((tile, depth), lambda i, o=o: (i + o // tile, 0)) for _, o in parts
    ]
    total = pl.BlockSpec((1, depth), lambda i: (0, 0))
    return pl.pallas_call(
        functools.partial(unnorm_kernel, len(parts)),
        grid=(rows // tile,),
        in_specs=[row, row, one] + late,
        out_specs=[row, total, total],
        out_shape=[
            jax.ShapeDtypeStruct((rows, depth), BF16),
            jax.ShapeDtypeStruct((1, depth), F32),
            jax.ShapeDtypeStruct((1, depth), F32),
        ],
        compiler_params=params(("arbitrary",)),
        cost_estimate=cost(30 * rows * depth, (6 + 2 * len(parts)) * rows * depth),
        name="unnorm",
    )(x, g, gain, *(p for p, _ in parts))


def project_kernel(width, order, x, w, bias, cos, low, high, q, k, v, active, hidden):
    rows = x[...]
    tables = (cos[...], low[...], high[...])
    q[...] = (
        rotated(nn(rows, w[:, :width]) + bias[:, :width], *tables).astype(BF16)
        * jnp.asarray(HEAD_DIM**-0.5, BF16)
    )
    k[...] = rotated(
        nn(rows, w[:, width : 2 * width]) + bias[:, width : 2 * width], *tables
    ).astype(BF16)
    v[...] = (nn(rows, w[:, 2 * width : 3 * width]) + bias[:, 2 * width : 3 * width]).astype(BF16)
    units = hidden.shape[1]
    step = min(256, units)
    for start in range(0, units, step):
        at = slice(3 * width + start, 3 * width + start + step)
        h = nn(rows, w[:, at]) + bias[:, at]
        hidden[:, start : start + step] = h
        active[:, start : start + step] = gelu(h).astype(BF16)


def project(order, x, w, bias, tables, width, units, length, tile=512):
    rows, depth = x.shape
    per = length // tile
    row = lambda n: pl.BlockSpec((tile, n), lambda i, o: (i, 0))
    table = pl.BlockSpec((tile, 128), lambda i, o: (i % per, 0))
    total = 3 * width + units
    return pl.pallas_call(
        functools.partial(project_kernel, width),
        grid_spec=pltpu.PrefetchScalarGridSpec(
            num_scalar_prefetch=1,
            grid=(rows // tile,),
            in_specs=[
                pl.BlockSpec((tile, depth), lambda i, o: (o[i // per] * per + i % per, 0)),
                once((depth, total), lambda i, o: (0, 0)),
                once((1, total), lambda i, o: (0, 0)),
                table,
                table,
                table,
            ],
            out_specs=[row(width), row(width), row(width), row(units), row(units)],
        ),
        out_shape=[
            jax.ShapeDtypeStruct((rows, width), BF16),
            jax.ShapeDtypeStruct((rows, width), BF16),
            jax.ShapeDtypeStruct((rows, width), BF16),
            jax.ShapeDtypeStruct((rows, units), BF16),
            jax.ShapeDtypeStruct((rows, units), F32),
        ],
        compiler_params=params(("arbitrary",)),
        cost_estimate=cost(2 * rows * depth * total, 2 * depth * (rows + total) + rows * units * 6),
        name="project",
    )(order, x, w, bias, *tables)


def each_tile_kernel(body, *refs):
    body(*refs)


def each_tile(body, arrays, w, depth, name, tile=512):
    rows = arrays[0].shape[0]
    return pl.pallas_call(
        functools.partial(each_tile_kernel, body),
        grid=(rows // tile,),
        in_specs=[pl.BlockSpec((tile, a.shape[1]), lambda i: (i, 0)) for a in arrays]
        + [once(w.shape, lambda i, n=len(w.shape): (0,) * n)],
        out_specs=pl.BlockSpec((tile, depth), lambda i: (i, 0)),
        out_shape=jax.ShapeDtypeStruct((rows, depth), BF16),
        compiler_params=params(("arbitrary",)),
        cost_estimate=cost(2 * w.size * rows, 2 * rows * depth),
        name=name,
    )(*arrays, w)


def core_sum_kernel(body, count, pieces, *refs):
    ins, outs, (w, sent, got, value, send_sem, got_sem) = (
        refs[: -count - 6],
        refs[-count - 5 : -5],
        (refs[-count - 6],) + refs[-5:],
    )
    slot = pl.program_id(0)
    me = lax.axis_index("tensor")
    core = lax.rem(me, 2)
    partner = me + 1 - 2 * core
    share = sent.shape[1]
    piece = share // pieces

    @pl.when(slot == 0)
    def _():
        barrier = pltpu.get_barrier_semaphore()
        pl.semaphore_signal(
            barrier, inc=1, device_id={"tensor": partner}, device_id_type=pl.DeviceIdType.MESH
        )
        pl.semaphore_wait(barrier, 1)

    def term(owner, i, to):
        rows = pl.ds(pl.multiple_of(owner * share + i * piece, piece), piece)
        body(*(r.at[rows, :] for r in ins), w, to)

    def copy(i):
        at = pl.ds(i * piece, piece)
        return pltpu.make_async_remote_copy(
            src_ref=sent.at[slot, at],
            dst_ref=got.at[slot, at],
            send_sem=send_sem.at[slot, i],
            recv_sem=got_sem.at[slot, i],
            device_id={"tensor": partner},
            device_id_type=pl.DeviceIdType.MESH,
        )

    for i in range(pieces):
        term(1 - core, i, sent.at[slot, pl.ds(i * piece, piece)])
        copy(i).start()
    for i in range(pieces):
        at = pl.ds(i * piece, piece)
        term(core, i, value)
        copy(i).wait_recv()
        for n, out in enumerate(outs):

            @pl.when(slot == n)
            def _(out=out):
                out[at, :] = (value[...] + got[slot, at].astype(F32)).astype(BF16)

    for i in range(pieces):
        copy(i).wait_send()


def core_sum(body, ident, count, length, arrays, w, depth, name, pieces=2):
    share = length // 2
    out = pl.BlockSpec((share, depth), lambda i: (0, 0), pipeline_mode=pl.Buffered(1))
    size = sum(a.shape[1] for a, _ in arrays)
    return pl.pallas_call(
        functools.partial(core_sum_kernel, body, count, pieces),
        grid=(count,),
        in_specs=[
            pl.BlockSpec((length, a.shape[1]), lambda i, f=f: (f + i, 0)) for a, f in arrays
        ]
        + [once(w.shape, lambda i, n=len(w.shape): (0,) * n)],
        out_specs=[out] * count,
        out_shape=[jax.ShapeDtypeStruct((share, depth), BF16)] * count,
        scratch_shapes=[
            pltpu.VMEM((count, share, depth), BF16),
            pltpu.VMEM((count, share, depth), BF16),
            pltpu.VMEM((share // pieces, depth), F32),
            pltpu.SemaphoreType.DMA((count, pieces)),
            pltpu.SemaphoreType.DMA((count, pieces)),
        ],
        compiler_params=pltpu.CompilerParams(
            dimension_semantics=("arbitrary",),
            vmem_limit_bytes=VMEM_BYTES,
            collective_id=ident,
            has_side_effects=True,
        ),
        cost_estimate=cost(
            2 * count * length * size * depth, 2 * count * length * (size + depth) + 2 * size * depth
        ),
        name=name,
    )(*(a for a, _ in arrays), w)


def mix_body(attended, active, w, out):
    parts, inner, columns = w.shape
    width = attended.shape[1]
    for d in range(parts):
        out[:, d * columns : (d + 1) * columns] = (
            nn(attended[...], w[d, :width, :]) + nn(active[...], w[d, width:, :])
        ).astype(out.dtype)


def unproject_body(qkv_grad, hidden_grad, w, out):
    three = qkv_grad.shape[1]
    depth = w.shape[0]
    step = min(512, depth)
    for start in range(0, depth, step):
        out[:, start : start + step] = (
            nt(qkv_grad[...], w[start : start + step, :three])
            + nt(hidden_grad[...], w[start : start + step, three:])
        ).astype(out.dtype)


def unmix_kernel(order, g, w, hidden, attended_grad, hidden_grad, sums):
    parts, inner, columns = w.shape
    width = attended_grad.shape[1]
    units = hidden.shape[1]

    @pl.when(pl.program_id(0) == 0)
    def _():
        sums[...] = jnp.zeros_like(sums)

    def back(lo, hi):
        total = nt(g[:, :columns], w[0, lo:hi, :])
        for d in range(1, parts):
            total = total + nt(g[:, d * columns : (d + 1) * columns], w[d, lo:hi, :])
        return total

    attended_grad[...] = back(0, width).astype(BF16)
    step = min(256, units)
    for start in range(0, units, step):
        at = slice(start, start + step)
        low = (back(width + start, width + start + step) * gelu_slope(hidden[:, at])).astype(BF16)
        hidden_grad[:, at] = low
        sums[:, at] += jnp.sum(low.astype(F32), axis=0, keepdims=True)


def unmix(order, g, w, hidden, width, length, tile=512):
    rows, depth = g.shape
    units = hidden.shape[1]
    parts, inner, columns = w.shape
    per = length // tile
    row = lambda n: pl.BlockSpec((tile, n), lambda i, o: (i, 0))
    return pl.pallas_call(
        unmix_kernel,
        grid_spec=pltpu.PrefetchScalarGridSpec(
            num_scalar_prefetch=1,
            grid=(rows // tile,),
            in_specs=[
                pl.BlockSpec((tile, depth), lambda i, o: (o[i // per] * per + i % per, 0)),
                once(w.shape, lambda i, o: (0, 0, 0)),
                row(units),
            ],
            out_specs=[row(width), row(units), pl.BlockSpec((1, units), lambda i, o: (0, 0))],
        ),
        out_shape=[
            jax.ShapeDtypeStruct((rows, width), BF16),
            jax.ShapeDtypeStruct((rows, units), BF16),
            jax.ShapeDtypeStruct((1, units), F32),
        ],
        compiler_params=params(("arbitrary",)),
        cost_estimate=cost(2 * rows * inner * depth, 2 * depth * (rows + inner) + rows * units * 6),
        name="unmix",
    )(order, g, w, hidden)


def outer_rows_kernel(length, order, x, *refs):
    parts, out = refs[:-1], refs[-1]
    total, slot = None, 0
    for part in parts:
        for at in range(0, part.shape[0], length):
            start = pl.multiple_of(order[slot] * length, length)
            term = tn(x[pl.ds(start, length), :], part[at : at + length, :])
            total = term if total is None else total + term
            slot += 1
    out[...] = total.astype(out.dtype)


def outer_rows(order, x, parts, length, tile=512):
    rows, depth = x.shape
    n = parts[0].shape[1]
    tile = min(tile, depth)
    return pl.pallas_call(
        functools.partial(outer_rows_kernel, length),
        grid_spec=pltpu.PrefetchScalarGridSpec(
            num_scalar_prefetch=1,
            grid=(depth // tile,),
            in_specs=[pl.BlockSpec((rows, tile), lambda i, o: (0, i))]
            + [once(p.shape, lambda i, o: (0, 0)) for p in parts],
            out_specs=pl.BlockSpec((tile, n), lambda i, o: (i, 0)),
        ),
        out_shape=jax.ShapeDtypeStruct((depth, n), BF16),
        compiler_params=params(("arbitrary",)),
        cost_estimate=cost(2 * rows * depth * n, 2 * (rows * (depth + n) + depth * n)),
        name="outer_rows",
    )(order, x, *parts)


def outer_columns_kernel(length, order, a, b, g, out):
    width = a.shape[1]
    for src, lo, hi in ((a, 0, width), (b, width, out.shape[1])):
        total = None
        for slot in range(a.shape[0] // length):
            start = pl.multiple_of(order[slot] * length, length)
            term = tn(src[slot * length : (slot + 1) * length, :], g[pl.ds(start, length), :])
            total = term if total is None else total + term
        out[0, lo:hi, :] = total.astype(out.dtype)


def outer_columns(order, a, b, g, parts, length):
    rows, depth = g.shape
    width, units = a.shape[1], b.shape[1]
    tile = depth // parts
    return pl.pallas_call(
        functools.partial(outer_columns_kernel, length),
        grid_spec=pltpu.PrefetchScalarGridSpec(
            num_scalar_prefetch=1,
            grid=(parts,),
            in_specs=[
                once((rows, width), lambda i, o: (0, 0)),
                once((rows, units), lambda i, o: (0, 0)),
                pl.BlockSpec((rows, tile), lambda i, o: (0, i)),
            ],
            out_specs=pl.BlockSpec((1, width + units, tile), lambda i, o: (i, 0, 0)),
        ),
        out_shape=jax.ShapeDtypeStruct((parts, width + units, tile), BF16),
        compiler_params=params(("arbitrary",)),
        cost_estimate=cost(
            2 * rows * depth * (width + units), 2 * (rows * (depth + width + units) + depth * (width + units))
        ),
        name="outer_columns",
    )(order, a, b, g)


def head_lanes(width, head):
    return lax.broadcasted_iota(jnp.int32, (1, width), 1) // HEAD_DIM == head


def attend_kernel(q, k, v, column_ids, row_ids, out, log_sums):
    length, width = q.shape
    heads = width // HEAD_DIM
    tile = min(SPAN, length)
    lanes = lax.broadcasted_iota(jnp.int32, (1, 128), 1)
    for begin in range(0, length, tile):
        end = min(length, begin + tile + SPAN)
        q_ids = column_ids[begin : begin + tile, :]
        blocked = row_ids[:, begin:end] > q_ids
        rows = q[begin : begin + tile, :]

        def one_head(head, carry):
            total, sums = carry
            mine = head_lanes(width, head)
            scores = nt(jnp.where(mine, rows, jnp.zeros_like(rows)), k[:end, :])
            tail = jnp.where(blocked, -1e9, scores[:, begin:])
            scores = jnp.concatenate([scores[:, :begin], tail], axis=1) if begin else tail
            highest = jnp.max(scores, axis=1, keepdims=True)
            powers = jnp.exp(scores - highest)
            amount = jnp.sum(powers, axis=1, keepdims=True)
            low = (powers * (1.0 / amount)).astype(BF16)
            total = jnp.where(mine, nn(low, v[:end, :]), total)
            sums = jnp.where(lanes == head, highest + jnp.log(amount), sums)
            return total, sums

        total, sums = jnp.zeros((tile, width), F32), jnp.zeros((tile, 128), F32)
        for head in range(heads):
            total, sums = one_head(head, (total, sums))
        out[begin : begin + tile, :] = total.astype(BF16)
        log_sums[:, begin : begin + tile] = sums.T[:8, :]


def attend(q, k, v, column_ids, row_ids):
    rows, width = q.shape
    seqs, _, length = row_ids.shape
    heads = width // HEAD_DIM
    seq = pl.BlockSpec((length, width), lambda s: (s, 0))
    return pl.pallas_call(
        attend_kernel,
        grid=(seqs,),
        in_specs=[
            seq,
            seq,
            seq,
            pl.BlockSpec((length, 1), lambda s: (s, 0)),
            pl.BlockSpec((None, 1, length), lambda s: (s, 0, 0)),
        ],
        out_specs=[seq, pl.BlockSpec((8, length), lambda s: (0, s))],
        out_shape=[
            jax.ShapeDtypeStruct((rows, width), BF16),
            jax.ShapeDtypeStruct((8, rows), F32),
        ],
        compiler_params=params(("arbitrary",)),
        cost_estimate=cost(
            8 * seqs * heads * length * length * 256 * 0.8, 8 * rows * width, seqs * heads * length**2
        ),
        name="attend",
    )(q, k, v, column_ids, row_ids)


def unattend_kernel(
    q, k, v, g, log_sums, column_ids, row_ids, cos, low, high, out, sums, key_total, value_total
):
    length, width = q.shape
    heads = width // HEAD_DIM
    tile = min(SPAN, length)
    tables = (cos[...], -low[...], -high[...])

    @pl.when(pl.program_id(0) == 0)
    def _():
        sums[...] = jnp.zeros_like(sums)

    key_total[...] = jnp.zeros_like(key_total)
    value_total[...] = jnp.zeros_like(value_total)
    for begin in range(0, length, tile):
        end = min(length, begin + tile + SPAN)
        at = slice(begin, begin + tile)
        blocked = column_ids[begin:end, :] > row_ids[:, at]
        q_rows, g_rows = q[at, :], g[at, :]
        query_total = jnp.zeros((tile, width), F32)
        for head in range(heads):
            mine = head_lanes(width, head)
            q_head = jnp.where(mine, q_rows, jnp.zeros_like(q_rows))
            g_head = jnp.where(mine, g_rows, jnp.zeros_like(g_rows))
            scores = nt(k[:end, :], q_head)
            tail = jnp.where(blocked, -1e9, scores[begin:, :])
            scores = jnp.concatenate([scores[:begin, :], tail], axis=0) if begin else tail
            probs = jnp.exp(scores - log_sums[head : head + 1, at])
            value_total[:end, :] += nn(probs.astype(BF16), g_head)
            prob_grad = nt(v[:end, :], g_head)
            inner = jnp.sum(prob_grad * probs, axis=0, keepdims=True)
            score_grad = (probs * (prob_grad - inner)).astype(BF16)
            key_total[:end, :] += nn(score_grad, q_head)
            query_total = jnp.where(mine, tn(score_grad, k[:end, :]), query_total)
        turned = rotated(query_total * HEAD_DIM**-0.5, *(t[at, :] for t in tables)).astype(BF16)
        out[at, :width] = turned
        sums[:, :width] += jnp.sum(turned.astype(F32), axis=0, keepdims=True)
    turned = rotated(key_total[...], *tables).astype(BF16)
    out[:, width : 2 * width] = turned
    sums[:, width : 2 * width] += jnp.sum(turned.astype(F32), axis=0, keepdims=True)
    turned = value_total[...].astype(BF16)
    out[:, 2 * width :] = turned
    sums[:, 2 * width :] += jnp.sum(turned.astype(F32), axis=0, keepdims=True)


def unattend(first, count, q, k, v, g, log_sums, column_ids, row_ids, tables):
    width = q.shape[1]
    length = row_ids.shape[2]
    rows, seqs = count * length, count
    heads = width // HEAD_DIM
    seq = pl.BlockSpec((length, width), lambda s: (first + s, 0))
    table = once((length, 128), lambda s: (0, 0))
    return pl.pallas_call(
        unattend_kernel,
        grid=(seqs,),
        in_specs=[
            seq,
            seq,
            seq,
            seq,
            pl.BlockSpec((8, length), lambda s: (0, first + s)),
            pl.BlockSpec((length, 1), lambda s: (first + s, 0)),
            pl.BlockSpec((None, 1, length), lambda s: (first + s, 0, 0)),
            table,
            table,
            table,
        ],
        out_specs=[
            pl.BlockSpec((length, 3 * width), lambda s: (s, 0)),
            pl.BlockSpec((1, 3 * width), lambda s: (0, 0)),
        ],
        out_shape=[
            jax.ShapeDtypeStruct((rows, 3 * width), BF16),
            jax.ShapeDtypeStruct((1, 3 * width), F32),
        ],
        scratch_shapes=[pltpu.VMEM((length, width), F32), pltpu.VMEM((length, width), F32)],
        compiler_params=params(("arbitrary",)),
        cost_estimate=cost(
            20 * seqs * heads * length * length * 256 * 0.8,
            14 * rows * width,
            seqs * heads * length**2,
        ),
        name="unattend",
    )(q, k, v, g, log_sums, column_ids, row_ids, *tables)


def gather_parts(part, groups):
    if groups != 4:
        return lax.all_gather(part, "dp", axis=0)
    mine = lax.axis_index("dp")
    full = jnp.zeros((groups,) + part.shape, part.dtype)
    pieces = [part] + [
        lax.ppermute(part, "dp", [(i, i ^ step) for i in range(groups)]) for step in (1, 2, 3)
    ]
    for step, piece in enumerate(pieces):
        full = lax.dynamic_update_slice(full, piece[None], (mine ^ step,) + (0,) * part.ndim)
    return full


def along_chips(values, hops):
    return lax.ppermute(
        values, "tensor", [(2 * a + core, 2 * b + core) for a, b in hops for core in range(2)]
    )


INWARD = ((0, 1), (3, 2))
MIDDLE = ((1, 2), (2, 1))
SIDES = ((0, 1), (1, 0), (2, 3), (3, 2))


def add_up(*parts):
    total = parts[0].astype(F32)
    for part in parts[1:]:
        total = total + part.astype(F32)
    return total.astype(BF16)


def after(values, *others):
    return lax.optimization_barrier((values,) + others)[0]


def sum_everywhere_kernel(groups, members, gain, shift, bias, qkv, up, wide, narrow, buf, in_dp, in_tensor, send_dp, got_dp, send_tensor, got_tensor):
    dp, tensor = lax.axis_index("dp"), lax.axis_index("tensor")
    mesh = pl.DeviceIdType.MESH
    barrier = pltpu.get_barrier_semaphore()
    for step in range(1, groups):
        pl.semaphore_signal(barrier, inc=1, device_id={"dp": lax.rem(dp + step, groups)}, device_id_type=mesh)
    for step in range(1, members):
        pl.semaphore_signal(barrier, inc=1, device_id={"tensor": lax.rem(tensor + step, members)}, device_id_type=mesh)
    pl.semaphore_wait(barrier, groups + members - 2)
    lanes = buf.shape[2] // 4
    for k, ref in enumerate((gain, shift, bias)):
        for r in range(8):
            buf[0, r : r + 1, k * lanes : (k + 1) * lanes] = ref[:, r * lanes : (r + 1) * lanes]
    row = 0
    buf[0, :, 3 * lanes :] = jnp.zeros((8, lanes), F32)
    for ref in (qkv, up):
        for start in range(0, ref.shape[1], lanes):
            buf[0, row : row + 1, 3 * lanes :] = ref[:, start : start + lanes]
            row += 1

    def exchange(axis, me, size, source, into, send, got):
        copies = []
        for step in range(1, size):
            copies.append(
                pltpu.make_async_remote_copy(
                    src_ref=source,
                    dst_ref=into.at[step - 1],
                    send_sem=send.at[step - 1],
                    recv_sem=got.at[step - 1],
                    device_id={axis: lax.rem(me + step, size)},
                    device_id_type=mesh,
                )
            )
        for copy in copies:
            copy.start()
        for copy in copies:
            copy.wait()

    exchange("dp", dp, groups, buf.at[0], in_dp, send_dp, got_dp)
    total = buf[0]
    for step in range(groups - 1):
        total = total + in_dp[step]
    row = 0
    for start in range(0, narrow.shape[1], lanes):
        narrow[:, start : start + lanes] = total[row : row + 1, 3 * lanes :]
        row += 1
    buf[1] = total
    exchange("tensor", tensor, members, buf.at[1], in_tensor, send_tensor, got_tensor)
    total = buf[1]
    for step in range(members - 1):
        total = total + in_tensor[step]
    for k in range(3):
        for r in range(8):
            wide[k : k + 1, r * lanes : (r + 1) * lanes] = total[r : r + 1, k * lanes : (k + 1) * lanes]


def sum_everywhere(ident, groups, members, gain, shift, bias, qkv, up):
    depth = gain.shape[1]
    whole = pl.BlockSpec(memory_space=pltpu.VMEM)
    return pl.pallas_call(
        functools.partial(sum_everywhere_kernel, groups, members),
        in_specs=[whole] * 5,
        out_specs=[whole] * 2,
        out_shape=[
            jax.ShapeDtypeStruct((8, depth), F32),
            jax.ShapeDtypeStruct((1, qkv.shape[1] + up.shape[1]), F32),
        ],
        scratch_shapes=[
            pltpu.VMEM((2, 8, depth // 2), F32),
            pltpu.VMEM((groups - 1, 8, depth // 2), F32),
            pltpu.VMEM((members - 1, 8, depth // 2), F32),
            pltpu.SemaphoreType.DMA((groups - 1,)),
            pltpu.SemaphoreType.DMA((groups - 1,)),
            pltpu.SemaphoreType.DMA((members - 1,)),
            pltpu.SemaphoreType.DMA((members - 1,)),
        ],
        compiler_params=pltpu.CompilerParams(collective_id=ident, has_side_effects=True),
        name="sum_everywhere",
    )(gain, shift, bias, qkv, up)


def per_device(
    inputs,
    block_ids,
    norm_gain,
    norm_bias,
    query_weight,
    query_bias,
    key_weight,
    key_bias,
    value_weight,
    value_bias,
    out_weight,
    out_bias,
    up_weight,
    up_bias,
    down_weight,
    down_bias,
    grad_out,
):
    seqs, length = block_ids.shape
    share, depth = inputs.shape
    width = query_weight.shape[1]
    units = up_weight.shape[1]
    groups, members = lax.axis_size("dp"), lax.axis_size("tensor")
    gain, shift = norm_gain.astype(F32)[None, :], norm_bias.astype(F32)[None, :]
    paired = members == 8 and seqs == 4 and 2 * share == length
    me = lax.axis_index("tensor")
    if paired:
        order = jnp.arange(3, -1, -1, dtype=jnp.int32) ^ (me // 2)
    else:
        order = jnp.arange(seqs, dtype=jnp.int32)

    normed = norm(inputs, gain, shift)
    rows = lax.all_gather(normed, "tensor", axis=0, tiled=True)
    upstream = lax.all_gather(grad_out, "tensor", axis=0, tiled=True)
    first = jnp.concatenate([query_weight, key_weight, value_weight, up_weight], axis=1)
    second = jnp.concatenate([out_weight, down_weight], axis=0)
    first_full = gather_parts(first, groups).reshape(depth, 3 * width + units)
    second_full = gather_parts(second, groups)
    bias = jnp.concatenate([query_bias, key_bias, value_bias, up_bias]).astype(F32)[None, :]
    tables = rotary_tables(length)
    ids = block_ids[order]
    column_ids = ids.reshape(seqs * length, 1)
    row_ids = ids.reshape(seqs, 1, length)

    q, k, v, active, hidden = project(order, rows, first_full, bias, tables, width, units, length)
    attended, log_sums = attend(q, k, v, column_ids, row_ids)
    pair = seqs // 2

    if paired:
        far = core_sum(
            mix_body, 1, pair, length, [(attended, 0), (active, 0)], second_full, depth, "mix"
        )
        from_end, from_end_2 = along_chips(far[0], INWARD), along_chips(far[1], INWARD)
        near = core_sum(
            mix_body,
            2,
            pair,
            length,
            [(attended, pair), (active, pair)],
            after(second_full, far[0]),
            depth,
            "mix",
        )
        crossing = add_up(far[1], from_end)
        crossed = along_chips(crossing, MIDDLE)
        upstream = after(upstream, near[0], crossing)
    else:
        whole = each_tile(mix_body, [attended, active], second_full, depth, "mix")
        terms = [lax.psum_scatter(whole, "tensor", scatter_dimension=0, tiled=True)]

    attended_grad, hidden_grad, up_sum = unmix(order, upstream, second_full, hidden, width, length)
    if paired:
        to_side = add_up(near[0], crossed)
        to_middle = add_up(far[0], from_end_2)
        terms = [near[1], along_chips(to_side, SIDES), along_chips(to_middle, MIDDLE)]
        attended_grad = after(attended_grad, to_side, to_middle)
    total = inputs.astype(F32) + out_bias.astype(F32) + down_bias.astype(F32)
    for values in terms:
        total = total + values.astype(F32)
    output = total.astype(BF16)

    def back(at, count, g):
        return unattend(at, count, q, k, v, g, log_sums, column_ids, row_ids, tables)

    if paired:
        far_grad, far_sum = back(0, pair, attended_grad)
        far = core_sum(
            unproject_body, 3, pair, length, [(far_grad, 0), (hidden_grad, 0)], first_full, depth, "unproject"
        )
        from_end, from_end_2 = along_chips(far[0], INWARD), along_chips(far[1], INWARD)
        second_grad = outer_columns(
            order, after(attended, far[0]), active, upstream, groups, length
        )
        near_grad, near_sum = back(pair, pair, after(attended_grad, second_grad, output))
        crossing = add_up(far[1], from_end)
        crossed = along_chips(crossing, MIDDLE)
        near = core_sum(
            unproject_body,
            4,
            pair,
            length,
            [(near_grad, 0), (hidden_grad, pair)],
            after(first_full, crossing, near_grad),
            depth,
            "unproject",
        )
        qkv_sum = far_sum + near_sum
        first_grad = outer_rows(order, after(rows, near[0]), [far_grad, near_grad], length)
        to_side = add_up(near[0], crossed)
        to_middle = add_up(far[0], from_end_2)
        terms = [near[1], along_chips(to_side, SIDES), along_chips(to_middle, MIDDLE)]
        up_grad = outer_rows(
            order, rows, [after(hidden_grad, first_grad, to_side, to_middle)], length
        )
    else:
        qkv_grad, qkv_sum = back(0, seqs, attended_grad)
        whole = each_tile(unproject_body, [qkv_grad, hidden_grad], first_full, depth, "unproject")
        terms = [lax.psum_scatter(whole, "tensor", scatter_dimension=0, tiled=True)]
        second_grad = outer_columns(order, attended, active, upstream, groups, length)
        first_grad = outer_rows(order, rows, [qkv_grad], length)
        up_grad = outer_rows(order, rows, [hidden_grad], length)

    second_grad = lax.psum_scatter(second_grad, "dp", scatter_dimension=0).astype(F32)
    first_grad = lax.psum_scatter(first_grad, "dp", scatter_dimension=0, tiled=True).astype(F32)
    up_grad = lax.psum_scatter(up_grad, "dp", scatter_dimension=0, tiled=True).astype(F32)

    input_grad, gain_part, shift_part = unnorm(inputs, grad_out, gain, [(t, 0) for t in terms])
    bias_part = jnp.sum(grad_out, axis=0, dtype=F32)[None, :]
    if paired and groups == 4:
        wide, narrow = sum_everywhere(
            5, groups, members, gain_part, shift_part, bias_part, qkv_sum, up_sum
        )
        gain_grad, shift_grad, outer_bias_grad = wide[0], wide[1], wide[2]
        qkv_sum, up_sum = narrow[0, : 3 * width], narrow[0, 3 * width :]
    else:
        gain_grad, shift_grad, outer_bias_grad = lax.psum(
            (gain_part[0], shift_part[0], bias_part[0]), ("dp", "tensor")
        )
        qkv_sum, up_sum = lax.psum((qkv_sum[0], up_sum[0]), "dp")
    return (
        output,
        input_grad,
        gain_grad,
        shift_grad,
        first_grad[:, :width],
        qkv_sum[:width],
        first_grad[:, width : 2 * width],
        qkv_sum[width : 2 * width],
        first_grad[:, 2 * width :],
        qkv_sum[2 * width :],
        second_grad[:width],
        outer_bias_grad,
        up_grad,
        up_sum,
        second_grad[width:],
        outer_bias_grad,
    )


def solution(mesh):
    tokens = P(("dp", "tensor"), None)
    down = P("dp", "tensor")
    across = P("tensor", "dp")
    part = P("tensor")
    return jax.shard_map(
        per_device,
        mesh=mesh,
        in_specs=(
            tokens,
            P("dp", None),
            P(),
            P(),
            down,
            part,
            down,
            part,
            down,
            part,
            across,
            P(),
            down,
            part,
            across,
            P(),
            tokens,
        ),
        out_specs=(
            tokens,
            tokens,
            P(),
            P(),
            down,
            part,
            down,
            part,
            down,
            part,
            across,
            P(),
            down,
            part,
            across,
            P(),
        ),
        check_vma=False,
    )
```

```python
import functools

import jax
import jax.numpy as jnp
from jax import lax
from jax.experimental import pallas as pl
from jax.experimental.pallas import tpu as pltpu
from jax.sharding import PartitionSpec as P

HEAD_DIM = 64
ROT = 32
SPAN = 256
EPS = 1e-05
F32 = jnp.float32
BF16 = jnp.bfloat16
VMEM_BYTES = 60 * 2**20


def nn(a, b):
    return jnp.dot(a, b, preferred_element_type=F32)


def nt(a, b):
    return lax.dot_general(a, b, (((1,), (1,)), ((), ())), preferred_element_type=F32)


def tn(a, b):
    return lax.dot_general(a, b, (((0,), (0,)), ((), ())), preferred_element_type=F32)


def params(semantics):
    return pltpu.CompilerParams(dimension_semantics=semantics, vmem_limit_bytes=VMEM_BYTES)


def cost(flops, bytes_accessed, transcendentals=0):
    return pl.CostEstimate(
        flops=int(flops) // 10,
        bytes_accessed=int(bytes_accessed) // 10,
        transcendentals=int(transcendentals) // 10,
    )


def once(shape, index_map):
    return pl.BlockSpec(shape, index_map, pipeline_mode=pl.Buffered(1))


def rotary_tables(length):
    halves = ROT // 2
    exponent = jnp.arange(halves, dtype=F32) * (2.0 / ROT)
    frequency = jnp.power(10000.0, -exponent)
    angles = jnp.arange(length, dtype=F32)[:, None] * frequency[None, :]
    cos, sin = jnp.cos(angles), jnp.sin(angles)
    zero = jnp.zeros((length, halves), F32)
    rest = HEAD_DIM - ROT
    head = lambda a, b, fill: jnp.concatenate([a, b, jnp.full((length, rest), fill, F32)], axis=1)
    return tuple(
        jnp.concatenate([t, t], axis=1)
        for t in (head(cos, cos, 1.0), head(-sin, zero, 0.0), head(zero, sin, 0.0))
    )


def rotated(values, cos, low, high):
    halves = ROT // 2
    pieces = []
    for start in range(0, values.shape[1], 128):
        u = values[:, start : start + 128]
        pieces.append(
            u * cos + pltpu.roll(u, 128 - halves, 1) * low + pltpu.roll(u, halves, 1) * high
        )
    return pieces[0] if len(pieces) == 1 else jnp.concatenate(pieces, axis=1)


GELU_A = 0.7978845608028654
GELU_B = 0.044715


def gelu(v):
    return 0.5 * v * (1.0 + jnp.tanh(GELU_A * (v + GELU_B * (v * v * v))))


def gelu_slope(v):
    square = v * v
    t = jnp.tanh(GELU_A * (v + GELU_B * (v * square)))
    return 0.5 * (1.0 + t) + 0.5 * v * (1.0 - t * t) * (GELU_A * (1.0 + 3.0 * GELU_B * square))


def norm_kernel(x, gain, shift, out):
    values = x[...].astype(F32)
    centered = values - jnp.mean(values, axis=1, keepdims=True)
    scale = lax.rsqrt(jnp.mean(centered * centered, axis=1, keepdims=True) + EPS)
    out[...] = (centered * scale * gain[...] + shift[...]).astype(BF16)


def norm(x, gain, shift, tile=128):
    rows, depth = x.shape
    row = pl.BlockSpec((tile, depth), lambda i: (i, 0))
    one = once((1, depth), lambda i: (0, 0))
    return pl.pallas_call(
        norm_kernel,
        grid=(rows // tile,),
        in_specs=[row, one, one],
        out_specs=row,
        out_shape=jax.ShapeDtypeStruct((rows, depth), BF16),
        compiler_params=params(("arbitrary",)),
        cost_estimate=cost(10 * rows * depth, 4 * rows * depth),
        name="norm",
    )(x, gain, shift)


def unnorm_kernel(terms, skipped, flag, x, g, gain, *refs):
    parts, (out, gain_sum, shift_sum) = refs[:terms], refs[terms + skipped :]

    @pl.when(pl.program_id(0) == 0)
    def _():
        gain_sum[...] = jnp.zeros_like(gain_sum)
        shift_sum[...] = jnp.zeros_like(shift_sum)

    values = x[...].astype(F32)
    centered = values - jnp.mean(values, axis=1, keepdims=True)
    scale = lax.rsqrt(jnp.mean(centered * centered, axis=1, keepdims=True) + EPS)
    hat = centered * scale
    back = parts[0][...].astype(F32)
    for part in parts[1:]:
        term = part[...].astype(F32)
        if part is parts[-1]:
            term = jnp.where(flag[0] == 1, term, 0.0)
        back = back + term
    gain_sum[...] += jnp.sum(back * hat, axis=0, keepdims=True)
    shift_sum[...] += jnp.sum(back, axis=0, keepdims=True)
    e = back * gain[...]
    inner = (
        e - jnp.mean(e, axis=1, keepdims=True) - hat * jnp.mean(e * hat, axis=1, keepdims=True)
    )
    out[...] = (g[...].astype(F32) + inner * scale).astype(BF16)


def unnorm(flag, x, g, gain, parts, wait_for=(), tile=128):
    rows, depth = x.shape
    row = pl.BlockSpec((tile, depth), lambda i, f: (i, 0))
    one = once((1, depth), lambda i, f: (0, 0))
    total = pl.BlockSpec((1, depth), lambda i, f: (0, 0))
    return pl.pallas_call(
        functools.partial(unnorm_kernel, len(parts), len(wait_for)),
        grid_spec=pltpu.PrefetchScalarGridSpec(
            num_scalar_prefetch=1,
            grid=(rows // tile,),
            in_specs=[row, row, one] + [row] * len(parts) + [ANYWHERE] * len(wait_for),
            out_specs=[row, total, total],
        ),
        out_shape=[
            jax.ShapeDtypeStruct((rows, depth), BF16),
            jax.ShapeDtypeStruct((1, depth), F32),
            jax.ShapeDtypeStruct((1, depth), F32),
        ],
        compiler_params=params(("arbitrary",)),
        cost_estimate=cost(30 * rows * depth, 14 * rows * depth),
        name="unnorm",
    )(flag, x, g, gain, *parts, *wait_for)


MESH = pl.DeviceIdType.MESH
ANYWHERE = pl.BlockSpec(memory_space=pl.ANY)


def places():
    me = lax.axis_index("tensor")
    core, chip = lax.rem(me, 2), lax.div(me, 2)
    beside = chip + 1 - 2 * lax.rem(chip, 2)
    inner = jnp.logical_or(chip == 1, chip == 2)
    return dict(
        core=core,
        partner=me + 1 - 2 * core,
        beside=2 * beside + core,
        opposite=2 * (3 - chip) + core,
        inner=inner,
        outer=jnp.logical_not(inner),
        all=None,
    )


def greet(at, others=()):
    barrier = pltpu.get_barrier_semaphore()
    ids = [{"tensor": at[name]} for name in ("partner", "beside", "opposite")] + list(others)
    for device in ids:
        pl.semaphore_signal(barrier, inc=1, device_id=device, device_id_type=MESH)
    pl.semaphore_wait(barrier, len(ids))


def to_device(src, dst, sent, got, device):
    return pltpu.make_async_remote_copy(
        src_ref=src,
        dst_ref=dst,
        send_sem=sent,
        recv_sem=got,
        device_id=device,
        device_id_type=MESH,
    )


def under(condition, act):
    if condition is None:
        act()
    else:
        pl.when(condition)(act)


def start_all(at, copies):
    for sender, _, copy in copies:
        under(at[sender], copy.start)


def finish_all(at, copies):
    for sender, receiver, copy in copies:
        under(at[receiver], copy.wait_recv)
        under(at[sender], copy.wait_send)


class Gather:
    MOVES = {
        1: (("all", "all", 3, 2, "beside"), ("inner", "inner", 3, 0, "opposite")),
        2: (("inner", "inner", 2, 1, "opposite"), ("inner", "outer", 0, 1, "beside")),
        3: (("inner", "outer", 1, 0, "beside"),),
        "own": (("all", "all", 3, 3, "partner"),),
        "first": (("all", "all", 2, 2, "partner"), ("inner", "inner", 0, 0, "partner")),
        "second": (("all", "all", 1, 1, "partner"),),
        "third": (("outer", "outer", 0, 0, "partner"),),
    }

    def __init__(self, *moves):
        self.moves = [(m, lo, hi) for name, lo, hi in moves for m in self.MOVES[name]]
        self.count = len(self.moves)

    def copies(self, at, full, sent, got):
        found = []
        for i, ((sender, receiver, src, dst, target), lo, hi) in enumerate(self.moves):
            rows = pl.ds(lo, hi - lo)
            found.append(
                (
                    sender,
                    receiver,
                    to_device(
                        full.at[src, at["core"], rows],
                        full.at[dst, at["core"], rows],
                        sent.at[i],
                        got.at[i],
                        {"tensor": at[target]},
                    ),
                )
            )
        return found


class Riding:
    def __init__(self, ins, outs, aliased, count, copies):
        self.ins, self.outs, self.aliased, self.count, self.copies = ins, outs, aliased, count, copies


def like(array):
    return jax.ShapeDtypeStruct(array.shape, array.dtype)


def gathering(full, *moves):
    plan = Gather(*moves)

    def copies(at, ins, outs, sent, got):
        return plan.copies(at, outs[0], sent, got)

    return Riding([full], [like(full)], True, plan.count, copies)


SENDS = {
    "in": ("outer", "inner", "beside"),
    "middle": ("inner", "inner", "opposite"),
    "side": ("all", "all", "beside"),
}


def sending(values, kind, lo, hi, into=None):
    sender, receiver, target = SENDS[kind]

    def copies(at, ins, outs, sent, got):
        rows = pl.ds(lo, hi - lo)
        copy = to_device(
            ins[0].at[rows], outs[0].at[rows], sent.at[0], got.at[0], {"tensor": at[target]}
        )
        return [(sender, receiver, copy)]

    return Riding([values] + ([] if into is None else [into]), [like(values)], into is not None, 1, copies)


def launch(body, args, ins, outs, shapes, grid, name, estimate, scratch=(), riding=(), ident=None, place=False, wait_for=()):
    if ident is None:
        return pl.pallas_call(
            body,
            grid=(grid,),
            in_specs=ins,
            out_specs=outs,
            out_shape=shapes,
            scratch_shapes=list(scratch),
            compiler_params=params(("arbitrary",)),
            cost_estimate=estimate,
            name=name,
        )(*args)
    riding = list(riding) + [Riding([a], [], False, 1, lambda *_: []) for a in wait_for]
    extra_in = [a for r in riding for a in r.ins]
    extra_out = [o for r in riding for o in r.outs]
    aliases, n_in, n_out = {}, len(args), len(shapes)
    for r in riding:
        if r.aliased:
            aliases[n_in + len(r.ins) - 1] = n_out
        n_in, n_out = n_in + len(r.ins), n_out + len(r.outs)

    def kernel(*refs):
        take = iter(refs)
        some = lambda n: [next(take) for _ in range(n)]
        own_ins, ride_ins = some(len(args)), [some(len(r.ins)) for r in riding]
        own_outs, ride_outs = some(len(shapes)), [some(len(r.outs)) for r in riding]
        own_scratch = some(len(scratch))
        at = places()
        copies = []
        for r, i, o in zip(riding, ride_ins, ride_outs):
            copies += r.copies(at, i, o, *some(2))

        @pl.when(pl.program_id(0) == 0)
        def _():
            greet(at)
            start_all(at, copies)

        body(*([at] if place else []), *own_ins, *own_outs, *own_scratch)

        @pl.when(pl.program_id(0) == grid - 1)
        def _():
            finish_all(at, copies)

    return pl.pallas_call(
        kernel,
        grid=(grid,),
        in_specs=ins + [ANYWHERE] * len(extra_in),
        out_specs=outs + [ANYWHERE] * len(extra_out),
        out_shape=shapes + extra_out,
        input_output_aliases=aliases,
        scratch_shapes=list(scratch)
        + [pltpu.SemaphoreType.DMA((r.count,)) for r in riding for _ in range(2)],
        compiler_params=pltpu.CompilerParams(
            dimension_semantics=("arbitrary",),
            vmem_limit_bytes=VMEM_BYTES,
            collective_id=ident,
            has_side_effects=True,
        ),
        cost_estimate=estimate,
        name=name,
    )(*args, *extra_in)


def gather_kernel(tile, groups, x, gain, shift, g, first, second, rows_full, g_full, first_full, second_full, own, kept, first_kept, second_kept, local, w_sent, w_got, *sems):
    at = places()
    dp = lax.axis_index("dp")
    peers = [{"dp": jnp.bitwise_xor(dp, step)} for step in range(1, groups)]
    greet(at, peers)
    loads = [
        pltpu.make_async_copy(src, dst, local.at[i])
        for i, (src, dst) in enumerate(((first, first_kept), (second, second_kept), (g, kept)))
    ]
    stores = [
        pltpu.make_async_copy(src, dst, local.at[i])
        for i, (src, dst) in enumerate(
            (
                (first_kept, first_full.at[dp]),
                (second_kept, second_full.at[dp]),
                (kept, g_full.at[3, at["core"]]),
                (own, rows_full.at[3, at["core"]]),
            )
        )
    ]
    weights = [
        [to_device(src, dst.at[dp], w_sent.at[k, i], w_got.at[k, i], peer) for i, peer in enumerate(peers)]
        for k, (src, dst) in enumerate(((first, first_full), (second, second_full)))
    ]
    for copy in loads + weights[0]:
        copy.start()
    share = own.shape[0]

    @pl.loop(0, share // tile)
    def _(i):
        rows = pl.ds(pl.multiple_of(i * tile, tile), tile)
        values = x[rows, :].astype(F32)
        centered = values - jnp.mean(values, axis=1, keepdims=True)
        scale = lax.rsqrt(jnp.mean(centered * centered, axis=1, keepdims=True) + EPS)
        own[rows, :] = (centered * scale * gain[...] + shift[...]).astype(BF16)

    stores[3].start()
    for load, store in zip(loads, stores):
        load.wait()
        store.start()
    stores[3].wait()
    half = share // 2
    lows, highs = (0, half), (half, share)
    plans = [
        Gather((1, *lows)),
        Gather((1, *highs), ("own", 0, share)),
        Gather((2, *lows), ("first", *lows)),
        Gather((2, *highs), ("first", *highs)),
        Gather((3, *lows), ("second", *lows)),
        Gather((3, *highs), ("second", *highs)),
        Gather(("third", *lows)),
        Gather(("third", *highs)),
    ]
    moves = [p.copies(at, rows_full, sems[2 * i], sems[2 * i + 1]) for i, p in enumerate(plans)]
    mine = Gather(("own", 0, share)).copies(at, g_full, sems[16], sems[17])
    start_all(at, moves[0])
    start_all(at, moves[1])
    for store in stores[:3]:
        store.wait()
    start_all(at, mine)
    for copy in weights[1]:
        copy.start()
    for i in range(6):
        finish_all(at, moves[i])
        start_all(at, moves[i + 2])
    finish_all(at, moves[6])
    finish_all(at, moves[7])
    finish_all(at, mine)
    for copy in weights[0] + weights[1]:
        copy.wait()


def gather(ident, x, gain, shift, g, first, second, groups, tile=64):
    rows, depth = x.shape
    whole = pl.BlockSpec(memory_space=pltpu.VMEM)
    full = jax.ShapeDtypeStruct((4, 2, rows, depth), BF16)
    sizes = [2, 3, 4, 4, 2, 2, 1, 1, 1]
    return pl.pallas_call(
        functools.partial(gather_kernel, tile, groups),
        in_specs=[whole] * 3 + [ANYWHERE] * 3,
        out_specs=[ANYWHERE] * 4,
        out_shape=[
            full,
            full,
            jax.ShapeDtypeStruct((groups,) + first.shape, BF16),
            jax.ShapeDtypeStruct((groups,) + second.shape, BF16),
        ],
        scratch_shapes=[
            pltpu.VMEM((rows, depth), BF16),
            pltpu.VMEM((rows, depth), BF16),
            pltpu.VMEM(first.shape, BF16),
            pltpu.VMEM(second.shape, BF16),
            pltpu.SemaphoreType.DMA((4,)),
            pltpu.SemaphoreType.DMA((2, groups - 1)),
            pltpu.SemaphoreType.DMA((2, groups - 1)),
        ]
        + [pltpu.SemaphoreType.DMA((n,)) for n in sizes for _ in range(2)],
        compiler_params=pltpu.CompilerParams(
            vmem_limit_bytes=VMEM_BYTES, collective_id=ident, has_side_effects=True
        ),
        cost_estimate=cost(10 * rows * depth, 60 * rows * depth),
        name="gather",
    )(x, gain, shift, g, first, second)


def project_tile(width, x, w, bias, cos, low, high, q, k, v, active, hidden):
    rows = x[...]
    tables = (cos[...], low[...], high[...])
    q[...] = (
        rotated(nn(rows, w[:, :width]) + bias[:, :width], *tables).astype(BF16)
        * jnp.asarray(HEAD_DIM**-0.5, BF16)
    )
    k[...] = rotated(
        nn(rows, w[:, width : 2 * width]) + bias[:, width : 2 * width], *tables
    ).astype(BF16)
    v[...] = (nn(rows, w[:, 2 * width : 3 * width]) + bias[:, 2 * width : 3 * width]).astype(BF16)
    units = hidden.shape[1]
    step = min(256, units)
    for start in range(0, units, step):
        at = slice(3 * width + start, 3 * width + start + step)
        h = nn(rows, w[:, at]) + bias[:, at]
        hidden[:, start : start + step] = h
        active[:, start : start + step] = gelu(h).astype(BF16)


def project(x, w, bias, tables, width, units, length, riding=(), ident=None, tile=512):
    rows, depth = x.shape
    per = length // tile
    row = lambda n: pl.BlockSpec((tile, n), lambda i: (i, 0))
    table = pl.BlockSpec((tile, 128), lambda i: (i % per, 0))
    total = 3 * width + units
    return launch(
        functools.partial(project_tile, width),
        [x, w, bias, *tables],
        [
            row(depth),
            once((depth, total), lambda i: (0, 0)),
            once((1, total), lambda i: (0, 0)),
            table,
            table,
            table,
        ],
        [row(width), row(width), row(width), row(units), row(units)],
        [jax.ShapeDtypeStruct((rows, width), BF16)] * 3
        + [jax.ShapeDtypeStruct((rows, units), BF16), jax.ShapeDtypeStruct((rows, units), F32)],
        rows // tile,
        "project",
        cost(2 * rows * depth * total, 2 * depth * (rows + total) + rows * units * 6),
        riding=riding,
        ident=ident,
    )


def each_tile_kernel(body, *refs):
    body(*refs)


def each_tile(body, arrays, w, depth, name, tile=512):
    rows = arrays[0].shape[0]
    return pl.pallas_call(
        functools.partial(each_tile_kernel, body),
        grid=(rows // tile,),
        in_specs=[pl.BlockSpec((tile, a.shape[1]), lambda i: (i, 0)) for a in arrays]
        + [once(w.shape, lambda i, n=len(w.shape): (0,) * n)],
        out_specs=pl.BlockSpec((tile, depth), lambda i: (i, 0)),
        out_shape=jax.ShapeDtypeStruct((rows, depth), BF16),
        compiler_params=params(("arbitrary",)),
        cost_estimate=cost(2 * w.size * rows, 2 * rows * depth),
        name=name,
    )(*arrays, w)


def core_sum_body(body, count, pieces, n_in, at, *refs):
    ins, w, outs = refs[:n_in], refs[n_in], refs[n_in + 1 : n_in + 1 + count]
    sent, got, value, send_sem, got_sem = refs[n_in + 1 + count :]
    slot = pl.program_id(0)
    core = at["core"]
    share = sent.shape[1]
    piece = share // pieces

    def term(owner, i, to):
        rows = pl.ds(pl.multiple_of(owner * share + i * piece, piece), piece)
        body(*(r.at[rows, :] for r in ins), w, to)

    def copy(i):
        rows = pl.ds(i * piece, piece)
        return to_device(
            sent.at[slot, rows],
            got.at[slot, rows],
            send_sem.at[slot, i],
            got_sem.at[slot, i],
            {"tensor": at["partner"]},
        )

    for i in range(pieces):
        term(1 - core, i, sent.at[slot, pl.ds(i * piece, piece)])
        copy(i).start()
    for i in range(pieces):
        rows = pl.ds(i * piece, piece)
        term(core, i, value)
        copy(i).wait_recv()
        for n, out in enumerate(outs):

            @pl.when(slot == n)
            def _(out=out):
                out[rows, :] = (value[...] + got[slot, rows].astype(F32)).astype(BF16)

    for i in range(pieces):
        copy(i).wait_send()


def core_sum(body, ident, count, length, arrays, w, depth, name, pieces=2, riding=()):
    share = length // 2
    out = pl.BlockSpec((share, depth), lambda i: (0, 0), pipeline_mode=pl.Buffered(1))
    size = sum(a.shape[1] for a, _ in arrays)
    return launch(
        functools.partial(core_sum_body, body, count, pieces, len(arrays)),
        [a for a, _ in arrays] + [w],
        [pl.BlockSpec((length, a.shape[1]), lambda i, f=f: (f + i, 0)) for a, f in arrays]
        + [once(w.shape, lambda i, n=len(w.shape): (0,) * n)],
        [out] * count,
        [jax.ShapeDtypeStruct((share, depth), BF16)] * count,
        count,
        name,
        cost(2 * count * length * size * depth, 2 * count * length * (size + depth) + 2 * size * depth),
        scratch=[
            pltpu.VMEM((count, share, depth), BF16),
            pltpu.VMEM((count, share, depth), BF16),
            pltpu.VMEM((share // pieces, depth), F32),
            pltpu.SemaphoreType.DMA((count, pieces)),
            pltpu.SemaphoreType.DMA((count, pieces)),
        ],
        riding=riding,
        ident=ident,
        place=True,
    )


def mix_body(attended, active, w, out):
    parts, inner, columns = w.shape
    width = attended.shape[1]
    for d in range(parts):
        out[:, d * columns : (d + 1) * columns] = (
            nn(attended[...], w[d, :width, :]) + nn(active[...], w[d, width:, :])
        ).astype(out.dtype)


def unproject_body(qkv_grad, hidden_grad, w, out):
    three = qkv_grad.shape[1]
    depth = w.shape[0]
    step = min(512, depth)
    for start in range(0, depth, step):
        out[:, start : start + step] = (
            nt(qkv_grad[...], w[start : start + step, :three])
            + nt(hidden_grad[...], w[start : start + step, three:])
        ).astype(out.dtype)


def unmix_tile(g, w, hidden, attended_grad, hidden_grad, sums):
    parts, inner, columns = w.shape
    width = attended_grad.shape[1]
    units = hidden.shape[1]

    @pl.when(pl.program_id(0) == 0)
    def _():
        sums[...] = jnp.zeros_like(sums)

    def back(lo, hi):
        total = nt(g[:, :columns], w[0, lo:hi, :])
        for d in range(1, parts):
            total = total + nt(g[:, d * columns : (d + 1) * columns], w[d, lo:hi, :])
        return total

    attended_grad[...] = back(0, width).astype(BF16)
    step = min(256, units)
    for start in range(0, units, step):
        at = slice(start, start + step)
        low = (back(width + start, width + start + step) * gelu_slope(hidden[:, at])).astype(BF16)
        hidden_grad[:, at] = low
        sums[:, at] += jnp.sum(low.astype(F32), axis=0, keepdims=True)


def unmix(g, w, hidden, width, first, count, length, riding=(), ident=None, tile=512):
    rows = count * length
    units = hidden.shape[1]
    parts, inner, columns = w.shape
    depth = parts * columns
    per = length // tile
    row = lambda n: pl.BlockSpec((tile, n), lambda i: (i, 0))
    late = lambda n: pl.BlockSpec((tile, n), lambda i: (first * per + i, 0))
    return launch(
        unmix_tile,
        [g, w, hidden],
        [late(depth), once(w.shape, lambda i: (0, 0, 0)), late(units)],
        [row(width), row(units), pl.BlockSpec((1, units), lambda i: (0, 0))],
        [
            jax.ShapeDtypeStruct((rows, width), BF16),
            jax.ShapeDtypeStruct((rows, units), BF16),
            jax.ShapeDtypeStruct((1, units), F32),
        ],
        rows // tile,
        "unmix",
        cost(2 * rows * inner * depth, 2 * depth * (rows + inner) + rows * units * 6),
        riding=riding,
        ident=ident,
    )


def unmix_gather_body(first, tile, moves, last_moves, at, w, hidden, whole_in, attended_grad, hidden_grad, sums, full, g, local, *sems):
    step, last = pl.program_id(0), pl.num_programs(0) - 1
    share = full.shape[2]
    per = share // tile
    early = Gather(*moves).copies(at, full, *sems[:2])
    late = Gather(*last_moves).copies(at, full, *sems[2:])

    def load(i):
        n = first * 2 * per + i
        rows = pl.ds(pl.multiple_of(lax.rem(n, per) * tile, tile), tile)
        return pltpu.make_async_copy(
            full.at[lax.div(n, 2 * per), lax.rem(lax.div(n, per), 2), rows],
            g.at[lax.rem(i, 2)],
            local.at[lax.rem(i, 2)],
        )

    @pl.when(step == 0)
    def _():
        start_all(at, early)
        load(step).start()

    @pl.when(step < last)
    def _():
        load(step + 1).start()

    load(step).wait()
    unmix_tile(g.at[lax.rem(step, 2)], w, hidden, attended_grad, hidden_grad, sums)

    @pl.when(step == last)
    def _():
        finish_all(at, early)
        start_all(at, late)
        finish_all(at, late)


def unmix_gather(full, w, hidden, width, first, count, length, moves, last_moves, ident, riding=(), tile=512):
    rows = count * length
    units = hidden.shape[1]
    parts, inner, columns = w.shape
    depth = parts * columns
    per = length // tile
    row = lambda n: pl.BlockSpec((tile, n), lambda i: (i, 0))
    counts = [Gather(*moves).count, Gather(*last_moves).count]

    body = functools.partial(unmix_gather_body, first, tile, moves, last_moves)
    extra = list(riding)
    args = [w, hidden, full] + [a for r in extra for a in r.ins]
    shapes = [
        jax.ShapeDtypeStruct((rows, width), BF16),
        jax.ShapeDtypeStruct((rows, units), BF16),
        jax.ShapeDtypeStruct((1, units), F32),
        like(full),
    ]
    aliases, n_in, n_out = {2: 3}, 3, 4
    for r in extra:
        if r.aliased:
            aliases[n_in + len(r.ins) - 1] = n_out
        n_in, n_out = n_in + len(r.ins), n_out + len(r.outs)

    def kernel(*refs):
        take = iter(refs)
        some = lambda n: [next(take) for _ in range(n)]
        own_ins, ride_ins = some(3), [some(len(r.ins)) for r in extra]
        own_outs, ride_outs = some(4), [some(len(r.outs)) for r in extra]
        own_scratch = some(6)
        at = places()
        copies = []
        for r, i, o in zip(extra, ride_ins, ride_outs):
            copies += r.copies(at, i, o, *some(2))

        @pl.when(pl.program_id(0) == 0)
        def _():
            greet(at)
            start_all(at, copies)

        body(at, *own_ins, *own_outs, *own_scratch)

        @pl.when(pl.program_id(0) == rows // tile - 1)
        def _():
            finish_all(at, copies)

    return pl.pallas_call(
        kernel,
        grid=(rows // tile,),
        in_specs=[
            once(w.shape, lambda i: (0, 0, 0)),
            pl.BlockSpec((tile, units), lambda i: (first * per + i, 0)),
        ]
        + [ANYWHERE] * (len(args) - 2),
        out_specs=[row(width), row(units), pl.BlockSpec((1, units), lambda i: (0, 0)), ANYWHERE]
        + [ANYWHERE for r in extra for _ in r.outs],
        out_shape=shapes + [o for r in extra for o in r.outs],
        input_output_aliases=aliases,
        scratch_shapes=[pltpu.VMEM((2, tile, depth), BF16), pltpu.SemaphoreType.DMA((2,))]
        + [pltpu.SemaphoreType.DMA((n,)) for n in counts for _ in range(2)]
        + [pltpu.SemaphoreType.DMA((r.count,)) for r in extra for _ in range(2)],
        compiler_params=pltpu.CompilerParams(
            dimension_semantics=("arbitrary",),
            vmem_limit_bytes=VMEM_BYTES,
            collective_id=ident,
            has_side_effects=True,
        ),
        cost_estimate=cost(2 * rows * inner * depth, 2 * depth * (rows + inner) + rows * units * 6),
        name="unmix",
    )(*args)


def outer_rows_kernel(x, *refs):
    parts, out = refs[:-1], refs[-1]
    total, start = None, 0
    for part in parts:
        term = tn(x[start : start + part.shape[0], :], part[...])
        total = term if total is None else total + term
        start += part.shape[0]
    out[...] = total.astype(out.dtype)


def outer_rows(x, parts, riding=(), ident=None, tile=512, wait_for=()):
    rows, depth = x.shape
    n = parts[0].shape[1]
    tile = min(tile, depth)
    return launch(
        outer_rows_kernel,
        [x, *parts],
        [pl.BlockSpec((rows, tile), lambda i: (0, i))]
        + [once(p.shape, lambda i: (0, 0)) for p in parts],
        [pl.BlockSpec((tile, n), lambda i: (i, 0))],
        [jax.ShapeDtypeStruct((depth, n), BF16)],
        depth // tile,
        "outer_rows",
        cost(2 * rows * depth * n, 2 * (rows * (depth + n) + depth * n)),
        riding=riding,
        ident=ident,
        wait_for=wait_for,
    )


def outer_columns_kernel(a, b, g, out):
    width = a.shape[1]
    out[0, :width, :] = tn(a[...], g[...]).astype(out.dtype)
    out[0, width:, :] = tn(b[...], g[...]).astype(out.dtype)


def outer_columns(a, b, g, parts, riding=(), ident=None):
    rows, depth = g.shape
    width, units = a.shape[1], b.shape[1]
    tile = depth // parts
    return launch(
        outer_columns_kernel,
        [a, b, g],
        [
            once((rows, width), lambda i: (0, 0)),
            once((rows, units), lambda i: (0, 0)),
            pl.BlockSpec((rows, tile), lambda i: (0, i)),
        ],
        [pl.BlockSpec((1, width + units, tile), lambda i: (i, 0, 0))],
        [jax.ShapeDtypeStruct((parts, width + units, tile), BF16)],
        parts,
        "outer_columns",
        cost(2 * rows * depth * (width + units), 2 * (rows * (depth + width + units) + depth * (width + units))),
        riding=riding,
        ident=ident,
    )


def head_lanes(width, head):
    return lax.broadcasted_iota(jnp.int32, (1, width), 1) // HEAD_DIM == head


def attend_kernel(q, k, v, column_ids, row_ids, out, log_sums):
    length, width = q.shape
    heads = width // HEAD_DIM
    tile = min(SPAN, length)
    lanes = lax.broadcasted_iota(jnp.int32, (1, 128), 1)
    for begin in range(0, length, tile):
        end = min(length, begin + tile + SPAN)
        q_ids = column_ids[begin : begin + tile, :]
        blocked = row_ids[:, begin:end] > q_ids
        rows = q[begin : begin + tile, :]

        def one_head(head, carry):
            total, sums = carry
            mine = head_lanes(width, head)
            scores = nt(jnp.where(mine, rows, jnp.zeros_like(rows)), k[:end, :])
            tail = jnp.where(blocked, -1e9, scores[:, begin:])
            scores = jnp.concatenate([scores[:, :begin], tail], axis=1) if begin else tail
            highest = jnp.max(scores, axis=1, keepdims=True)
            powers = jnp.exp(scores - highest)
            amount = jnp.sum(powers, axis=1, keepdims=True)
            low = (powers * (1.0 / amount)).astype(BF16)
            total = jnp.where(mine, nn(low, v[:end, :]), total)
            sums = jnp.where(lanes == head, highest + jnp.log(amount), sums)
            return total, sums

        total, sums = jnp.zeros((tile, width), F32), jnp.zeros((tile, 128), F32)
        for head in range(heads):
            total, sums = one_head(head, (total, sums))
        out[begin : begin + tile, :] = total.astype(BF16)
        log_sums[:, begin : begin + tile] = sums.T[:8, :]


def attend(q, k, v, column_ids, row_ids, riding=(), ident=None):
    rows, width = q.shape
    seqs, _, length = row_ids.shape
    heads = width // HEAD_DIM
    seq = pl.BlockSpec((length, width), lambda s: (s, 0))
    return launch(
        attend_kernel,
        [q, k, v, column_ids, row_ids],
        [
            seq,
            seq,
            seq,
            pl.BlockSpec((length, 1), lambda s: (s, 0)),
            pl.BlockSpec((None, 1, length), lambda s: (s, 0, 0)),
        ],
        [seq, pl.BlockSpec((8, length), lambda s: (0, s))],
        [jax.ShapeDtypeStruct((rows, width), BF16), jax.ShapeDtypeStruct((8, rows), F32)],
        seqs,
        "attend",
        cost(8 * seqs * heads * length * length * 256 * 0.8, 8 * rows * width, seqs * heads * length**2),
        riding=riding,
        ident=ident,
    )


def unattend_kernel(
    q, k, v, g, log_sums, column_ids, row_ids, cos, low, high, out, sums, key_total, value_total
):
    length, width = q.shape
    heads = width // HEAD_DIM
    tile = min(SPAN, length)
    tables = (cos[...], -low[...], -high[...])

    @pl.when(pl.program_id(0) == 0)
    def _():
        sums[...] = jnp.zeros_like(sums)

    key_total[...] = jnp.zeros_like(key_total)
    value_total[...] = jnp.zeros_like(value_total)
    for begin in range(0, length, tile):
        end = min(length, begin + tile + SPAN)
        at = slice(begin, begin + tile)
        blocked = column_ids[begin:end, :] > row_ids[:, at]
        q_rows, g_rows = q[at, :], g[at, :]
        query_total = jnp.zeros((tile, width), F32)
        for head in range(heads):
            mine = head_lanes(width, head)
            q_head = jnp.where(mine, q_rows, jnp.zeros_like(q_rows))
            g_head = jnp.where(mine, g_rows, jnp.zeros_like(g_rows))
            scores = nt(k[:end, :], q_head)
            tail = jnp.where(blocked, -1e9, scores[begin:, :])
            scores = jnp.concatenate([scores[:begin, :], tail], axis=0) if begin else tail
            probs = jnp.exp(scores - log_sums[head : head + 1, at])
            value_total[:end, :] += nn(probs.astype(BF16), g_head)
            prob_grad = nt(v[:end, :], g_head)
            inner = jnp.sum(prob_grad * probs, axis=0, keepdims=True)
            score_grad = (probs * (prob_grad - inner)).astype(BF16)
            key_total[:end, :] += nn(score_grad, q_head)
            query_total = jnp.where(mine, tn(score_grad, k[:end, :]), query_total)
        turned = rotated(query_total * HEAD_DIM**-0.5, *(t[at, :] for t in tables)).astype(BF16)
        out[at, :width] = turned
        sums[:, :width] += jnp.sum(turned.astype(F32), axis=0, keepdims=True)
    turned = rotated(key_total[...], *tables).astype(BF16)
    out[:, width : 2 * width] = turned
    sums[:, width : 2 * width] += jnp.sum(turned.astype(F32), axis=0, keepdims=True)
    turned = value_total[...].astype(BF16)
    out[:, 2 * width :] = turned
    sums[:, 2 * width :] += jnp.sum(turned.astype(F32), axis=0, keepdims=True)


def unattend(first, count, q, k, v, g, g_first, log_sums, column_ids, row_ids, tables, riding=(), ident=None, wait_for=()):
    width = q.shape[1]
    length = row_ids.shape[2]
    rows, seqs = count * length, count
    heads = width // HEAD_DIM
    seq = pl.BlockSpec((length, width), lambda s: (first + s, 0))
    table = once((length, 128), lambda s: (0, 0))
    return launch(
        unattend_kernel,
        [q, k, v, g, log_sums, column_ids, row_ids, *tables],
        [
            seq,
            seq,
            seq,
            pl.BlockSpec((length, width), lambda s: (g_first + s, 0)),
            pl.BlockSpec((8, length), lambda s: (0, first + s)),
            pl.BlockSpec((length, 1), lambda s: (first + s, 0)),
            pl.BlockSpec((None, 1, length), lambda s: (first + s, 0, 0)),
            table,
            table,
            table,
        ],
        [
            pl.BlockSpec((length, 3 * width), lambda s: (s, 0)),
            pl.BlockSpec((1, 3 * width), lambda s: (0, 0)),
        ],
        [jax.ShapeDtypeStruct((rows, 3 * width), BF16), jax.ShapeDtypeStruct((1, 3 * width), F32)],
        count,
        "unattend",
        cost(20 * seqs * heads * length * length * 256 * 0.8, 14 * rows * width, seqs * heads * length**2),
        scratch=[pltpu.VMEM((length, width), F32), pltpu.VMEM((length, width), F32)],
        riding=riding,
        ident=ident,
        wait_for=wait_for,
    )


def add_up(*parts):
    total = parts[0].astype(F32)
    for part in parts[1:]:
        total = total + part.astype(F32)
    return total.astype(BF16)


def after(values, *others):
    return lax.optimization_barrier((values,) + others)[0]


def sum_everywhere_kernel(groups, members, gain, shift, bias, qkv, up, wide, narrow, buf, in_dp, in_tensor, send_dp, got_dp, send_tensor, got_tensor):
    dp, tensor = lax.axis_index("dp"), lax.axis_index("tensor")
    mesh = pl.DeviceIdType.MESH
    barrier = pltpu.get_barrier_semaphore()
    for step in range(1, groups):
        pl.semaphore_signal(barrier, inc=1, device_id={"dp": lax.rem(dp + step, groups)}, device_id_type=mesh)
    for step in range(1, members):
        pl.semaphore_signal(barrier, inc=1, device_id={"tensor": lax.rem(tensor + step, members)}, device_id_type=mesh)
    pl.semaphore_wait(barrier, groups + members - 2)
    lanes = buf.shape[2] // 4
    for k, ref in enumerate((gain, shift, bias)):
        for r in range(8):
            buf[0, r : r + 1, k * lanes : (k + 1) * lanes] = ref[:, r * lanes : (r + 1) * lanes]
    row = 0
    buf[0, :, 3 * lanes :] = jnp.zeros((8, lanes), F32)
    for ref in (qkv, up):
        for start in range(0, ref.shape[1], lanes):
            buf[0, row : row + 1, 3 * lanes :] = ref[:, start : start + lanes]
            row += 1

    def exchange(axis, me, size, source, into, send, got):
        copies = []
        for step in range(1, size):
            copies.append(
                pltpu.make_async_remote_copy(
                    src_ref=source,
                    dst_ref=into.at[step - 1],
                    send_sem=send.at[step - 1],
                    recv_sem=got.at[step - 1],
                    device_id={axis: lax.rem(me + step, size)},
                    device_id_type=mesh,
                )
            )
        for copy in copies:
            copy.start()
        for copy in copies:
            copy.wait()

    exchange("dp", dp, groups, buf.at[0], in_dp, send_dp, got_dp)
    total = buf[0]
    for step in range(groups - 1):
        total = total + in_dp[step]
    row = 0
    for start in range(0, narrow.shape[1], lanes):
        narrow[:, start : start + lanes] = total[row : row + 1, 3 * lanes :]
        row += 1
    buf[1] = total
    exchange("tensor", tensor, members, buf.at[1], in_tensor, send_tensor, got_tensor)
    total = buf[1]
    for step in range(members - 1):
        total = total + in_tensor[step]
    for k in range(3):
        for r in range(8):
            wide[k : k + 1, r * lanes : (r + 1) * lanes] = total[r : r + 1, k * lanes : (k + 1) * lanes]


def sum_everywhere(ident, groups, members, gain, shift, bias, qkv, up):
    depth = gain.shape[1]
    whole = pl.BlockSpec(memory_space=pltpu.VMEM)
    return pl.pallas_call(
        functools.partial(sum_everywhere_kernel, groups, members),
        in_specs=[whole] * 5,
        out_specs=[whole] * 2,
        out_shape=[
            jax.ShapeDtypeStruct((8, depth), F32),
            jax.ShapeDtypeStruct((1, qkv.shape[1] + up.shape[1]), F32),
        ],
        scratch_shapes=[
            pltpu.VMEM((2, 8, depth // 2), F32),
            pltpu.VMEM((groups - 1, 8, depth // 2), F32),
            pltpu.VMEM((members - 1, 8, depth // 2), F32),
            pltpu.SemaphoreType.DMA((groups - 1,)),
            pltpu.SemaphoreType.DMA((groups - 1,)),
            pltpu.SemaphoreType.DMA((members - 1,)),
            pltpu.SemaphoreType.DMA((members - 1,)),
        ],
        compiler_params=pltpu.CompilerParams(collective_id=ident, has_side_effects=True),
        name="sum_everywhere",
    )(gain, shift, bias, qkv, up)


def per_device(
    inputs,
    block_ids,
    norm_gain,
    norm_bias,
    query_weight,
    query_bias,
    key_weight,
    key_bias,
    value_weight,
    value_bias,
    out_weight,
    out_bias,
    up_weight,
    up_bias,
    down_weight,
    down_bias,
    grad_out,
):
    seqs, length = block_ids.shape
    share, depth = inputs.shape
    width = query_weight.shape[1]
    units = up_weight.shape[1]
    groups, members = lax.axis_size("dp"), lax.axis_size("tensor")
    gain, shift = norm_gain.astype(F32)[None, :], norm_bias.astype(F32)[None, :]
    paired = groups == 4 and members == 8 and seqs == 4 and 2 * share == length
    me = lax.axis_index("tensor")
    if paired:
        chip = me // 2
        order = jnp.arange(3, -1, -1, dtype=jnp.int32) ^ chip
        inner = ((chip == 1) | (chip == 2)).astype(jnp.int32)
    else:
        order = jnp.arange(seqs, dtype=jnp.int32)

    first = jnp.concatenate([query_weight, key_weight, value_weight, up_weight], axis=1)
    second = jnp.concatenate([out_weight, down_weight], axis=0)
    bias = jnp.concatenate([query_bias, key_bias, value_bias, up_bias]).astype(F32)[None, :]
    tables = rotary_tables(length)
    ids = block_ids[order]
    column_ids = ids.reshape(seqs * length, 1)
    row_ids = ids.reshape(seqs, 1, length)
    pair = seqs // 2
    everything = seqs * length

    idents = iter(range(1, 100))

    if paired:
        kept = lambda values: jnp.where(inner == 1, values, jnp.zeros_like(values))
        rows, full, first_full, second_full = gather(
            next(idents), inputs, gain, shift, grad_out, first, second, groups
        )
        rows = rows.reshape(everything, depth)
        first_full = first_full.reshape(depth, 3 * width + units)
        q, k, v, active, hidden, full = project(
            rows,
            first_full,
            bias,
            tables,
            width,
            units,
            length,
            riding=[gathering(full, (1, 0, share))],
            ident=next(idents),
        )
        half, more = share // 2, share * 9 // 16
        attended, log_sums, full = attend(
            q,
            k,
            v,
            column_ids,
            row_ids,
            riding=[gathering(full, (2, 0, more), ("first", 0, share))],
            ident=next(idents),
        )
        *far, full = core_sum(
            mix_body,
            next(idents),
            pair,
            length,
            [(attended, 0), (active, 0)],
            second_full,
            depth,
            "mix",
            riding=[gathering(full, (2, more, share))],
        )
        *near, full, end = core_sum(
            mix_body,
            next(idents),
            pair,
            length,
            [(attended, pair), (active, pair)],
            second_full,
            depth,
            "mix",
            riding=[
                gathering(full, (3, 0, half), ("second", 0, share)),
                sending(far[0], "in", 0, half),
            ],
        )
        near_attended_grad, near_hidden_grad, near_up_sum, full, end = unmix_gather(
            full,
            second_full,
            hidden,
            width,
            pair,
            pair,
            length,
            [(3, half, share), ("third", 0, half)],
            [("third", half, share)],
            next(idents),
            riding=[sending(far[0], "in", half, share, end)],
        )
        upstream = full.reshape(everything, depth)
        cut = share * 3 // 8
        crossing = add_up(far[1], end)
        far_attended_grad, far_hidden_grad, far_up_sum, end, middle = unmix(
            upstream,
            second_full,
            hidden,
            width,
            0,
            pair,
            length,
            riding=[sending(far[1], "in", 0, cut), sending(crossing, "middle", 0, cut)],
            ident=next(idents),
        )
        up_sum = near_up_sum + far_up_sum
        far_grad, far_sum, end, middle = unattend(
            0,
            pair,
            q,
            k,
            v,
            far_attended_grad,
            0,
            log_sums,
            column_ids,
            row_ids,
            tables,
            riding=[
                sending(far[1], "in", cut, share, end),
                sending(crossing, "middle", cut, share, middle),
            ],
            ident=next(idents),
        )
        to_side = add_up(near[0], kept(middle))
        to_middle = add_up(far[0], end)
        mine = near[1]
        *far, side, middle = core_sum(
            unproject_body,
            next(idents),
            pair,
            length,
            [(far_grad, 0), (far_hidden_grad, 0)],
            first_full,
            depth,
            "unproject",
            riding=[sending(to_side, "side", 0, half), sending(to_middle, "middle", 0, half)],
        )
        second_part, side, middle, end = outer_columns(
            attended,
            active,
            upstream,
            groups,
            riding=[
                sending(to_side, "side", half, share, side),
                sending(to_middle, "middle", half, share, middle),
                sending(far[0], "in", 0, half),
            ],
            ident=next(idents),
        )
        terms = [mine, side, kept(middle)]
        second_grad = lax.psum_scatter(second_part, "dp", scatter_dimension=0)
        up_part, end = outer_rows(
            rows,
            [far_hidden_grad, near_hidden_grad],
            riding=[sending(far[0], "in", half, share, end)],
            ident=next(idents),
            wait_for=[second_part],
        )
        up_grad = lax.psum_scatter(up_part, "dp", scatter_dimension=0, tiled=True)
    else:
        first_full = lax.all_gather(first, "dp", axis=0, tiled=True)
        second_full = lax.all_gather(second, "dp", axis=0)
        rows = lax.all_gather(norm(inputs, gain, shift), "tensor", axis=0, tiled=True)
        upstream = lax.all_gather(grad_out, "tensor", axis=0, tiled=True)
        q, k, v, active, hidden = project(rows, first_full, bias, tables, width, units, length)
        attended, log_sums = attend(q, k, v, column_ids, row_ids)
        whole = each_tile(mix_body, [attended, active], second_full, depth, "mix")
        terms = [lax.psum_scatter(whole, "tensor", scatter_dimension=0, tiled=True)]
        attended_grad, hidden_grad, up_sum = unmix(
            upstream, second_full, hidden, width, 0, seqs, length
        )
    total = inputs.astype(F32) + out_bias.astype(F32) + down_bias.astype(F32)
    for values in terms:
        total = total + values.astype(F32)
    output = total.astype(BF16)

    if paired:
        crossing = add_up(far[1], end)
        near_grad, near_sum, end, middle = unattend(
            pair,
            pair,
            q,
            k,
            v,
            near_attended_grad,
            0,
            log_sums,
            column_ids,
            row_ids,
            tables,
            riding=[sending(far[1], "in", 0, more), sending(crossing, "middle", 0, more)],
            ident=next(idents),
            wait_for=[output],
        )
        *near, end, middle = core_sum(
            unproject_body,
            next(idents),
            pair,
            length,
            [(near_grad, 0), (near_hidden_grad, 0)],
            first_full,
            depth,
            "unproject",
            riding=[
                sending(far[1], "in", more, share, end),
                sending(crossing, "middle", more, share, middle),
            ],
        )
        qkv_sum = far_sum + near_sum
        to_side = add_up(near[0], kept(middle))
        to_middle = add_up(far[0], end)
        first_part, side, middle = outer_rows(
            rows,
            [far_grad, near_grad],
            riding=[sending(to_side, "side", 0, share), sending(to_middle, "middle", 0, share)],
            ident=next(idents),
            wait_for=[second_grad],
        )
        first_grad = lax.psum_scatter(first_part, "dp", scatter_dimension=0, tiled=True)
        terms = [near[1], side, middle]
    else:
        inner = jnp.ones((), jnp.int32)
        qkv_grad, qkv_sum = unattend(
            0, seqs, q, k, v, attended_grad, 0, log_sums, column_ids, row_ids, tables
        )
        whole = each_tile(unproject_body, [qkv_grad, hidden_grad], first_full, depth, "unproject")
        terms = [lax.psum_scatter(whole, "tensor", scatter_dimension=0, tiled=True)]
        (second_part,) = outer_columns(attended, active, upstream, groups)
        (first_part,) = outer_rows(rows, [qkv_grad])
        (up_part,) = outer_rows(rows, [hidden_grad])
        second_grad = lax.psum_scatter(second_part, "dp", scatter_dimension=0)
        first_grad = lax.psum_scatter(first_part, "dp", scatter_dimension=0, tiled=True)
        up_grad = lax.psum_scatter(up_part, "dp", scatter_dimension=0, tiled=True)

    second_grad, first_grad, up_grad = (t.astype(F32) for t in (second_grad, first_grad, up_grad))
    input_grad, gain_part, shift_part = unnorm(
        inner[None], inputs, grad_out, gain, terms, [up_grad] if paired else []
    )
    bias_part = jnp.sum(grad_out, axis=0, dtype=F32)[None, :]
    if paired and groups == 4:
        wide, narrow = sum_everywhere(
            next(idents), groups, members, gain_part, shift_part, bias_part, qkv_sum, up_sum
        )
        gain_grad, shift_grad, outer_bias_grad = wide[0], wide[1], wide[2]
        qkv_sum, up_sum = narrow[0, : 3 * width], narrow[0, 3 * width :]
    else:
        gain_grad, shift_grad, outer_bias_grad = lax.psum(
            (gain_part[0], shift_part[0], bias_part[0]), ("dp", "tensor")
        )
        qkv_sum, up_sum = lax.psum((qkv_sum[0], up_sum[0]), "dp")
    return (
        output,
        input_grad,
        gain_grad,
        shift_grad,
        first_grad[:, :width],
        qkv_sum[:width],
        first_grad[:, width : 2 * width],
        qkv_sum[width : 2 * width],
        first_grad[:, 2 * width :],
        qkv_sum[2 * width :],
        second_grad[:width],
        outer_bias_grad,
        up_grad,
        up_sum,
        second_grad[width:],
        outer_bias_grad,
    )


def solution(mesh):
    tokens = P(("dp", "tensor"), None)
    down = P("dp", "tensor")
    across = P("tensor", "dp")
    part = P("tensor")
    return jax.shard_map(
        per_device,
        mesh=mesh,
        in_specs=(
            tokens,
            P("dp", None),
            P(),
            P(),
            down,
            part,
            down,
            part,
            down,
            part,
            across,
            P(),
            down,
            part,
            across,
            P(),
            tokens,
        ),
        out_specs=(
            tokens,
            tokens,
            P(),
            P(),
            down,
            part,
            down,
            part,
            down,
            part,
            across,
            P(),
            down,
            part,
            across,
            P(),
        ),
        check_vma=False,
    )
```

```python
import functools

import jax
import jax.numpy as jnp
import numpy as np
from jax import lax
from jax.experimental import pallas as pl
from jax.experimental.pallas import tpu as pltpu
from jax.sharding import PartitionSpec as P

HEAD_DIM = 64
ROT = 32
SPAN = 256
EPS = 1e-05
F32 = jnp.float32
BF16 = jnp.bfloat16
VMEM_BYTES = 60 * 2**20


def nn(a, b):
    return jnp.dot(a, b, preferred_element_type=F32)


def nt(a, b):
    return lax.dot_general(a, b, (((1,), (1,)), ((), ())), preferred_element_type=F32)


def tn(a, b):
    return lax.dot_general(a, b, (((0,), (0,)), ((), ())), preferred_element_type=F32)


def params(semantics):
    return pltpu.CompilerParams(dimension_semantics=semantics, vmem_limit_bytes=VMEM_BYTES)


def cost(flops, bytes_accessed, transcendentals=0):
    return pl.CostEstimate(
        flops=int(flops) // 10,
        bytes_accessed=int(bytes_accessed) // 10,
        transcendentals=int(transcendentals) // 10,
    )


def once(shape, index_map):
    return pl.BlockSpec(shape, index_map, pipeline_mode=pl.Buffered(1))


def rotary_tables(length):
    halves = ROT // 2
    exponent = jnp.arange(halves, dtype=F32) * (2.0 / ROT)
    frequency = jnp.power(10000.0, -exponent)
    angles = jnp.arange(length, dtype=F32)[:, None] * frequency[None, :]
    cos, sin = jnp.cos(angles), jnp.sin(angles)
    zero = jnp.zeros((length, halves), F32)
    rest = HEAD_DIM - ROT
    head = lambda a, b, fill: jnp.concatenate([a, b, jnp.full((length, rest), fill, F32)], axis=1)
    return tuple(
        jnp.concatenate([t, t], axis=1)
        for t in (head(cos, cos, 1.0), head(-sin, zero, 0.0), head(zero, sin, 0.0))
    )


def rotated(values, cos, low, high):
    halves = ROT // 2
    pieces = []
    for start in range(0, values.shape[1], 128):
        u = values[:, start : start + 128]
        pieces.append(
            u * cos + pltpu.roll(u, 128 - halves, 1) * low + pltpu.roll(u, halves, 1) * high
        )
    return pieces[0] if len(pieces) == 1 else jnp.concatenate(pieces, axis=1)


GELU_A = 0.7978845608028654
GELU_B = 0.044715


def gelu(v):
    return 0.5 * v * (1.0 + jnp.tanh(GELU_A * (v + GELU_B * (v * v * v))))


def gelu_slope(v):
    square = v * v
    t = jnp.tanh(GELU_A * (v + GELU_B * (v * square)))
    return 0.5 * (1.0 + t) + 0.5 * v * (1.0 - t * t) * (GELU_A * (1.0 + 3.0 * GELU_B * square))


def norm_kernel(x, gain, shift, out):
    values = x[...].astype(F32)
    centered = values - jnp.mean(values, axis=1, keepdims=True)
    scale = lax.rsqrt(jnp.mean(centered * centered, axis=1, keepdims=True) + EPS)
    out[...] = (centered * scale * gain[...] + shift[...]).astype(BF16)


def norm(x, gain, shift, tile=128):
    rows, depth = x.shape
    row = pl.BlockSpec((tile, depth), lambda i: (i, 0))
    one = once((1, depth), lambda i: (0, 0))
    return pl.pallas_call(
        norm_kernel,
        grid=(rows // tile,),
        in_specs=[row, one, one],
        out_specs=row,
        out_shape=jax.ShapeDtypeStruct((rows, depth), BF16),
        compiler_params=params(("arbitrary",)),
        cost_estimate=cost(10 * rows * depth, 4 * rows * depth),
        name="norm",
    )(x, gain, shift)


def unnorm_kernel(terms, skipped, flag, x, g, gain, *refs):
    parts, (out, gain_sum, shift_sum) = refs[:terms], refs[terms + skipped :]

    @pl.when(pl.program_id(0) == 0)
    def _():
        gain_sum[...] = jnp.zeros_like(gain_sum)
        shift_sum[...] = jnp.zeros_like(shift_sum)

    values = x[...].astype(F32)
    centered = values - jnp.mean(values, axis=1, keepdims=True)
    scale = lax.rsqrt(jnp.mean(centered * centered, axis=1, keepdims=True) + EPS)
    hat = centered * scale
    back = parts[0][...].astype(F32)
    for part in parts[1:]:
        term = part[...].astype(F32)
        if part is parts[-1]:
            term = jnp.where(flag[0] == 1, term, 0.0)
        back = back + term
    gain_sum[...] += jnp.sum(back * hat, axis=0, keepdims=True)
    shift_sum[...] += jnp.sum(back, axis=0, keepdims=True)
    e = back * gain[...]
    inner = (
        e - jnp.mean(e, axis=1, keepdims=True) - hat * jnp.mean(e * hat, axis=1, keepdims=True)
    )
    out[...] = (g[...].astype(F32) + inner * scale).astype(BF16)


def unnorm(flag, x, g, gain, parts, wait_for=(), tile=128):
    rows, depth = x.shape
    row = pl.BlockSpec((tile, depth), lambda i, f: (i, 0))
    one = once((1, depth), lambda i, f: (0, 0))
    total = pl.BlockSpec((1, depth), lambda i, f: (0, 0))
    return pl.pallas_call(
        functools.partial(unnorm_kernel, len(parts), len(wait_for)),
        grid_spec=pltpu.PrefetchScalarGridSpec(
            num_scalar_prefetch=1,
            grid=(rows // tile,),
            in_specs=[row, row, one] + [row] * len(parts) + [ANYWHERE] * len(wait_for),
            out_specs=[row, total, total],
        ),
        out_shape=[
            jax.ShapeDtypeStruct((rows, depth), BF16),
            jax.ShapeDtypeStruct((1, depth), F32),
            jax.ShapeDtypeStruct((1, depth), F32),
        ],
        compiler_params=params(("arbitrary",)),
        cost_estimate=cost(30 * rows * depth, 14 * rows * depth),
        name="unnorm",
    )(flag, x, g, gain, *parts, *wait_for)


MESH = pl.DeviceIdType.MESH
ANYWHERE = pl.BlockSpec(memory_space=pl.ANY)


def places():
    me = lax.axis_index("tensor")
    core, chip = lax.rem(me, 2), lax.div(me, 2)
    beside = chip + 1 - 2 * lax.rem(chip, 2)
    inner = jnp.logical_or(chip == 1, chip == 2)
    return dict(
        core=core,
        partner=me + 1 - 2 * core,
        beside=2 * beside + core,
        opposite=2 * (3 - chip) + core,
        inner=inner,
        outer=jnp.logical_not(inner),
        all=None,
    )


def greet(at, others=()):
    barrier = pltpu.get_barrier_semaphore()
    ids = [{"tensor": at[name]} for name in ("partner", "beside", "opposite")] + list(others)
    for device in ids:
        pl.semaphore_signal(barrier, inc=1, device_id=device, device_id_type=MESH)
    pl.semaphore_wait(barrier, len(ids))


def to_device(src, dst, sent, got, device):
    return pltpu.make_async_remote_copy(
        src_ref=src,
        dst_ref=dst,
        send_sem=sent,
        recv_sem=got,
        device_id=device,
        device_id_type=MESH,
    )


def under(condition, act):
    if condition is None:
        act()
    else:
        pl.when(condition)(act)


def start_all(at, copies):
    for sender, _, copy in copies:
        under(at[sender], copy.start)


def finish_all(at, copies):
    for sender, receiver, copy in copies:
        under(at[receiver], copy.wait_recv)
        under(at[sender], copy.wait_send)


class Gather:
    MOVES = {
        1: (("all", "all", 3, 2, "beside"), ("inner", "inner", 3, 0, "opposite")),
        2: (("inner", "inner", 2, 1, "opposite"), ("inner", "outer", 0, 1, "beside")),
        3: (("inner", "outer", 1, 0, "beside"),),
        "own": (("all", "all", 3, 3, "partner"),),
        "first": (("all", "all", 2, 2, "partner"), ("inner", "inner", 0, 0, "partner")),
        "second": (("all", "all", 1, 1, "partner"),),
        "third": (("outer", "outer", 0, 0, "partner"),),
    }

    def __init__(self, *moves):
        self.moves = [(m, lo, hi) for name, lo, hi in moves for m in self.MOVES[name]]
        self.count = len(self.moves)

    def copies(self, at, full, sent, got):
        found = []
        for i, ((sender, receiver, src, dst, target), lo, hi) in enumerate(self.moves):
            rows = pl.ds(lo, hi - lo)
            found.append(
                (
                    sender,
                    receiver,
                    to_device(
                        full.at[src, at["core"], rows],
                        full.at[dst, at["core"], rows],
                        sent.at[i],
                        got.at[i],
                        {"tensor": at[target]},
                    ),
                )
            )
        return found


class Riding:
    def __init__(self, ins, outs, aliased, count, copies, late=0):
        self.ins, self.outs, self.aliased, self.count, self.copies = ins, outs, aliased, count, copies
        self.late = late


def like(array):
    return jax.ShapeDtypeStruct(array.shape, array.dtype)


def gathering(full, *moves, late=()):
    plan = Gather(*moves, *late)

    def copies(at, ins, outs, sent, got):
        return plan.copies(at, outs[0], sent, got)

    return Riding([full], [like(full)], True, plan.count, copies, Gather(*late).count)


SENDS = {
    "in": ("outer", "inner", "beside"),
    "middle": ("inner", "inner", "opposite"),
    "side": ("all", "all", "beside"),
}


def sending(values, kind, lo, hi, into=None):
    sender, receiver, target = SENDS[kind]

    def copies(at, ins, outs, sent, got):
        rows = pl.ds(lo, hi - lo)
        copy = to_device(
            ins[0].at[rows], outs[0].at[rows], sent.at[0], got.at[0], {"tensor": at[target]}
        )
        return [(sender, receiver, copy)]

    return Riding([values] + ([] if into is None else [into]), [like(values)], into is not None, 1, copies)


def launch(body, args, ins, outs, shapes, grid, name, estimate, scratch=(), riding=(), ident=None, place=False, wait_for=()):
    if ident is None:
        return pl.pallas_call(
            body,
            grid=(grid,),
            in_specs=ins,
            out_specs=outs,
            out_shape=shapes,
            scratch_shapes=list(scratch),
            compiler_params=params(("arbitrary",)),
            cost_estimate=estimate,
            name=name,
        )(*args)
    riding = list(riding) + [Riding([a], [], False, 1, lambda *_: []) for a in wait_for]
    extra_in = [a for r in riding for a in r.ins]
    extra_out = [o for r in riding for o in r.outs]
    aliases, n_in, n_out = {}, len(args), len(shapes)
    for r in riding:
        if r.aliased:
            aliases[n_in + len(r.ins) - 1] = n_out
        n_in, n_out = n_in + len(r.ins), n_out + len(r.outs)

    def kernel(*refs):
        take = iter(refs)
        some = lambda n: [next(take) for _ in range(n)]
        own_ins, ride_ins = some(len(args)), [some(len(r.ins)) for r in riding]
        own_outs, ride_outs = some(len(shapes)), [some(len(r.outs)) for r in riding]
        own_scratch = some(len(scratch))
        at = places()
        copies, late = [], []
        for r, i, o in zip(riding, ride_ins, ride_outs):
            found = r.copies(at, i, o, *some(2))
            copies += found[: len(found) - r.late]
            late += found[len(found) - r.late :]

        @pl.when(pl.program_id(0) == 0)
        def _():
            greet(at)
            start_all(at, copies)

        body(*([at] if place else []), *own_ins, *own_outs, *own_scratch)

        @pl.when(pl.program_id(0) == grid - 1)
        def _():
            finish_all(at, copies)
            start_all(at, late)
            finish_all(at, late)

    return pl.pallas_call(
        kernel,
        grid=(grid,),
        in_specs=ins + [ANYWHERE] * len(extra_in),
        out_specs=outs + [ANYWHERE] * len(extra_out),
        out_shape=shapes + extra_out,
        input_output_aliases=aliases,
        scratch_shapes=list(scratch)
        + [pltpu.SemaphoreType.DMA((r.count,)) for r in riding for _ in range(2)],
        compiler_params=pltpu.CompilerParams(
            dimension_semantics=("arbitrary",),
            vmem_limit_bytes=VMEM_BYTES,
            collective_id=ident,
            has_side_effects=True,
        ),
        cost_estimate=estimate,
        name=name,
    )(*args, *extra_in)


def opening_kernel(tile, groups, width, cut, *refs):
    x, gain, shift, g, *weights = refs[:10]
    biases, frequency, refs = refs[10:14], refs[14], refs[15:]
    rows_full, g_full, first_full, second_full, q, k, v, active, hidden, cos, low, high = refs[:12]
    own, kept, first_kept, second_kept, w, bias, x_tile = refs[12:19]
    staged, (local, x_sem, out_sem, w_sent, w_got), sems = refs[19:24], refs[24:29], refs[29:]
    at = places()
    core, dp = at["core"], lax.axis_index("dp")
    peers = [{"dp": jnp.bitwise_xor(dp, step)} for step in range(1, groups)]
    share, depth = own.shape
    half = share // 2
    units = hidden.shape[1]
    lows, highs = (0, half), (half, share)
    greet(at, peers)

    columns = [(0, width), (width, width), (2 * width, width), (3 * width, units)]
    loads = [
        pltpu.make_async_copy(src, first_kept.at[:, pl.ds(start, size)], local.at[i])
        for i, (src, (start, size)) in enumerate(zip(weights[:4], columns))
    ] + [
        pltpu.make_async_copy(weights[4], second_kept.at[pl.ds(0, width)], local.at[4]),
        pltpu.make_async_copy(weights[5], second_kept.at[pl.ds(width, units)], local.at[5]),
        pltpu.make_async_copy(g, kept, local.at[6]),
    ]
    stores = [
        pltpu.make_async_copy(first_kept, first_full.at[dp], local.at[0]),
        pltpu.make_async_copy(second_kept, second_full.at[dp], local.at[1]),
        pltpu.make_async_copy(kept, g_full.at[3, core], local.at[2]),
        pltpu.make_async_copy(own, rows_full.at[3, core], local.at[7]),
    ]
    spread = [
        [to_device(src, dst.at[dp], w_sent.at[n, i], w_got.at[n, i], peer) for i, peer in enumerate(peers)]
        for n, (src, dst) in enumerate(((first_kept, first_full), (second_kept, second_full)))
    ]
    plans = dict(
        n1_low=[(1, *lows)],
        n1_high=[(1, *highs), ("own", 0, share)],
        n2_low=[(2, *lows)],
        n2_high=[(2, *highs)],
        e2_low=[("first", *lows)],
        e2_high=[("first", *highs)],
        n3_low=[(3, *lows)],
        n3_high=[(3, *highs)],
        e1_low=[("second", *lows)],
        e1_high=[("second", *highs)],
        e0_low=[("third", *lows)],
        e0_high=[("third", *highs)],
        g_own=[("own", 0, share)],
        g1=[(1, 0, cut)],
    )
    moves = {
        name: Gather(*plan).copies(
            at, g_full if name[0] == "g" else rows_full, sems[2 * i], sems[2 * i + 1]
        )
        for i, (name, plan) in enumerate(plans.items())
    }

    def start(*names):
        for name in names:
            start_all(at, moves[name])

    def finish(*names):
        for name in names:
            finish_all(at, moves[name])

    for copy in loads:
        copy.start()

    @pl.loop(0, share // tile)
    def _(i):
        rows = pl.ds(pl.multiple_of(i * tile, tile), tile)
        values = x[rows, :].astype(F32)
        centered = values - jnp.mean(values, axis=1, keepdims=True)
        scale = lax.rsqrt(jnp.mean(centered * centered, axis=1, keepdims=True) + EPS)
        own[rows, :] = (
            centered * scale * gain[...].astype(F32) + shift[...].astype(F32)
        ).astype(BF16)

    stores[3].start()
    for copy in loads:
        copy.wait()
    for copy in spread[0]:
        copy.start()
    for copy in stores[:3]:
        copy.start()
    stores[3].wait()
    start("n1_low", "n1_high")

    lane = lax.broadcasted_iota(jnp.int32, (1, 128), 1) % HEAD_DIM
    position = lax.broadcasted_iota(jnp.int32, cos.shape, 0).astype(F32)
    angle = position * frequency[...]
    sine = jnp.sin(angle)
    cos[...] = jnp.where(lane < ROT, jnp.cos(angle), 1.0)
    low[...] = jnp.where(lane < ROT // 2, -sine, 0.0)
    high[...] = jnp.where(jnp.logical_and(lane >= ROT // 2, lane < ROT), sine, 0.0)
    for ref, (begin, size) in zip(biases, columns):
        bias[:, begin : begin + size] = ref[...].astype(F32)

    for copy in stores[:3]:
        copy.wait()
    start("g_own")
    for copy in spread[1]:
        copy.start()
    finish("n1_low")
    start("n2_low", "e2_low")
    finish("n1_high")
    start("n2_high", "e2_high")
    finish("n2_low")
    start("n3_low", "e1_low")
    for copy in spread[0]:
        copy.wait()
    fetch = [
        pltpu.make_async_copy(
            first_full.at[d], w.at[pl.ds(d * first_full.shape[1], first_full.shape[1])], local.at[d]
        )
        for d in range(groups)
    ]
    for copy in fetch:
        copy.start()
    for copy in fetch:
        copy.wait()

    outs = (q, k, v, active, hidden)

    def results(i):
        part = jnp.where(lax.rem(i, 2) == 0, core, 1 - core)
        slot = 3 - lax.div(i, 2)
        rows = pl.ds(pl.multiple_of((2 * slot + part) * share, share), share)
        return [
            pltpu.make_async_copy(src.at[lax.rem(i, 2)], dst.at[rows], out_sem.at[lax.rem(i, 2), n])
            for n, (src, dst) in enumerate(zip(staged, outs))
        ]

    @pl.loop(0, 8)
    def _(i):
        @pl.when(i == 2)
        def _():
            finish("n2_high")
            start("n3_high", "e1_high")
            finish("e2_low", "e2_high")

        @pl.when(i == 4)
        def _():
            finish("e1_low", "e1_high")

        @pl.when(i == 6)
        def _():
            finish("n3_low")
            start("e0_low")
            finish("n3_high")
            start("e0_high")
            finish("g_own")
            start("g1")

        @pl.when(i == 7)
        def _():
            finish("e0_low", "e0_high")

        part = jnp.where(lax.rem(i, 2) == 0, core, 1 - core)
        load = pltpu.make_async_copy(rows_full.at[3 - lax.div(i, 2), part], x_tile, x_sem)
        load.start()

        @pl.when(i >= 2)
        def _():
            for copy in results(i - 2):
                copy.wait()

        load.wait()
        here = pl.ds(pl.multiple_of(part * share, share), share)
        project_tile(
            width,
            x_tile,
            w,
            bias,
            cos.at[here],
            low.at[here],
            high.at[here],
            *(r.at[lax.rem(i, 2)] for r in staged),
        )
        for copy in results(i):
            copy.start()

    for i in (6, 7):
        for copy in results(i):
            copy.wait()
    finish("g1")
    for copy in spread[1]:
        copy.wait()


OPENING_PLANS = (2, 3, 2, 2, 2, 2, 1, 1, 1, 1, 1, 1, 1, 2)


def opening(ident, x, gain, shift, g, weights, biases, groups, length, cut, tile=64):
    rows, depth = x.shape
    width, units = weights[0].shape[1], weights[3].shape[1]
    total = 3 * width + units
    inner = width + units
    columns = weights[4].shape[1]
    everything = 8 * rows
    whole = pl.BlockSpec(memory_space=pltpu.VMEM)
    full = jax.ShapeDtypeStruct((4, 2, rows, depth), BF16)
    exponent = np.arange(ROT // 2, dtype=np.float32) * np.float32(2.0 / ROT)
    frequency = np.tile(np.power(np.float32(10000.0), -exponent), 8)[None, :]
    table = jax.ShapeDtypeStruct((length, 128), F32)
    narrow = jax.ShapeDtypeStruct((everything, width), BF16)
    return pl.pallas_call(
        functools.partial(opening_kernel, tile, groups, width, cut),
        in_specs=[whole] * 3 + [ANYWHERE] * 7 + [whole] * 5,
        out_specs=[ANYWHERE] * 9 + [whole] * 3,
        out_shape=[
            full,
            full,
            jax.ShapeDtypeStruct((groups, depth // groups, total), BF16),
            jax.ShapeDtypeStruct((groups, inner, columns), BF16),
            narrow,
            narrow,
            narrow,
            jax.ShapeDtypeStruct((everything, units), BF16),
            jax.ShapeDtypeStruct((everything, units), F32),
            table,
            table,
            table,
        ],
        scratch_shapes=[
            pltpu.VMEM((rows, depth), BF16),
            pltpu.VMEM((rows, depth), BF16),
            pltpu.VMEM((depth // groups, total), BF16),
            pltpu.VMEM((inner, columns), BF16),
            pltpu.VMEM((depth, total), BF16),
            pltpu.VMEM((1, total), F32),
            pltpu.VMEM((rows, depth), BF16),
            pltpu.VMEM((2, rows, width), BF16),
            pltpu.VMEM((2, rows, width), BF16),
            pltpu.VMEM((2, rows, width), BF16),
            pltpu.VMEM((2, rows, units), BF16),
            pltpu.VMEM((2, rows, units), F32),
            pltpu.SemaphoreType.DMA((8,)),
            pltpu.SemaphoreType.DMA,
            pltpu.SemaphoreType.DMA((2, 5)),
            pltpu.SemaphoreType.DMA((2, groups - 1)),
            pltpu.SemaphoreType.DMA((2, groups - 1)),
        ]
        + [pltpu.SemaphoreType.DMA((n,)) for n in OPENING_PLANS for _ in range(2)],
        compiler_params=pltpu.CompilerParams(
            vmem_limit_bytes=VMEM_BYTES, collective_id=ident, has_side_effects=True
        ),
        cost_estimate=cost(2 * everything * depth * total, 60 * rows * depth),
        name="opening",
    )(x, gain, shift, g, *weights, *biases, jnp.asarray(frequency))


def project_tile(width, x, w, bias, cos, low, high, q, k, v, active, hidden):
    rows = x[...]
    tables = (cos[...], low[...], high[...])
    q[...] = (
        rotated(nn(rows, w[:, :width]) + bias[:, :width], *tables).astype(BF16)
        * jnp.asarray(HEAD_DIM**-0.5, BF16)
    )
    k[...] = rotated(
        nn(rows, w[:, width : 2 * width]) + bias[:, width : 2 * width], *tables
    ).astype(BF16)
    v[...] = (nn(rows, w[:, 2 * width : 3 * width]) + bias[:, 2 * width : 3 * width]).astype(BF16)
    units = hidden.shape[1]
    step = min(256, units)
    for start in range(0, units, step):
        at = slice(3 * width + start, 3 * width + start + step)
        h = nn(rows, w[:, at]) + bias[:, at]
        hidden[:, start : start + step] = h
        active[:, start : start + step] = gelu(h).astype(BF16)


def project(x, w, bias, tables, width, units, length, riding=(), ident=None, tile=512):
    rows, depth = x.shape
    per = length // tile
    row = lambda n: pl.BlockSpec((tile, n), lambda i: (i, 0))
    table = pl.BlockSpec((tile, 128), lambda i: (i % per, 0))
    total = 3 * width + units
    return launch(
        functools.partial(project_tile, width),
        [x, w, bias, *tables],
        [
            row(depth),
            once((depth, total), lambda i: (0, 0)),
            once((1, total), lambda i: (0, 0)),
            table,
            table,
            table,
        ],
        [row(width), row(width), row(width), row(units), row(units)],
        [jax.ShapeDtypeStruct((rows, width), BF16)] * 3
        + [jax.ShapeDtypeStruct((rows, units), BF16), jax.ShapeDtypeStruct((rows, units), F32)],
        rows // tile,
        "project",
        cost(2 * rows * depth * total, 2 * depth * (rows + total) + rows * units * 6),
        riding=riding,
        ident=ident,
    )


def each_tile_kernel(body, *refs):
    body(*refs)


def each_tile(body, arrays, w, depth, name, tile=512):
    rows = arrays[0].shape[0]
    return pl.pallas_call(
        functools.partial(each_tile_kernel, body),
        grid=(rows // tile,),
        in_specs=[pl.BlockSpec((tile, a.shape[1]), lambda i: (i, 0)) for a in arrays]
        + [once(w.shape, lambda i, n=len(w.shape): (0,) * n)],
        out_specs=pl.BlockSpec((tile, depth), lambda i: (i, 0)),
        out_shape=jax.ShapeDtypeStruct((rows, depth), BF16),
        compiler_params=params(("arbitrary",)),
        cost_estimate=cost(2 * w.size * rows, 2 * rows * depth),
        name=name,
    )(*arrays, w)


def core_sum_body(body, count, pieces, n_in, at, *refs):
    ins, w, outs = refs[:n_in], refs[n_in], refs[n_in + 1 : n_in + 1 + count]
    sent, got, value, send_sem, got_sem = refs[n_in + 1 + count :]
    slot = pl.program_id(0)
    core = at["core"]
    share = sent.shape[1]
    piece = share // pieces

    def term(owner, i, to):
        rows = pl.ds(pl.multiple_of(owner * share + i * piece, piece), piece)
        body(*(r.at[rows, :] for r in ins), w, to)

    def copy(i):
        rows = pl.ds(i * piece, piece)
        return to_device(
            sent.at[slot, rows],
            got.at[slot, rows],
            send_sem.at[slot, i],
            got_sem.at[slot, i],
            {"tensor": at["partner"]},
        )

    for i in range(pieces):
        term(1 - core, i, sent.at[slot, pl.ds(i * piece, piece)])
        copy(i).start()
    for i in range(pieces):
        rows = pl.ds(i * piece, piece)
        term(core, i, value)
        copy(i).wait_recv()
        for n, out in enumerate(outs):

            @pl.when(slot == n)
            def _(out=out):
                out[rows, :] = (value[...] + got[slot, rows].astype(F32)).astype(BF16)

    for i in range(pieces):
        copy(i).wait_send()


def core_sum(body, ident, count, length, arrays, w, depth, name, pieces=2, riding=()):
    share = length // 2
    out = pl.BlockSpec((share, depth), lambda i: (0, 0), pipeline_mode=pl.Buffered(1))
    size = sum(a.shape[1] for a, _ in arrays)
    return launch(
        functools.partial(core_sum_body, body, count, pieces, len(arrays)),
        [a for a, _ in arrays] + [w],
        [pl.BlockSpec((length, a.shape[1]), lambda i, f=f: (f + i, 0)) for a, f in arrays]
        + [once(w.shape, lambda i, n=len(w.shape): (0,) * n)],
        [out] * count,
        [jax.ShapeDtypeStruct((share, depth), BF16)] * count,
        count,
        name,
        cost(2 * count * length * size * depth, 2 * count * length * (size + depth) + 2 * size * depth),
        scratch=[
            pltpu.VMEM((count, share, depth), BF16),
            pltpu.VMEM((count, share, depth), BF16),
            pltpu.VMEM((share // pieces, depth), F32),
            pltpu.SemaphoreType.DMA((count, pieces)),
            pltpu.SemaphoreType.DMA((count, pieces)),
        ],
        riding=riding,
        ident=ident,
        place=True,
    )


def mix_body(attended, active, w, out):
    parts, inner, columns = w.shape
    width = attended.shape[1]
    for d in range(parts):
        out[:, d * columns : (d + 1) * columns] = (
            nn(attended[...], w[d, :width, :]) + nn(active[...], w[d, width:, :])
        ).astype(out.dtype)


def unproject_body(qkv_grad, hidden_grad, w, out):
    three = qkv_grad.shape[1]
    depth = w.shape[0]
    step = min(512, depth)
    for start in range(0, depth, step):
        out[:, start : start + step] = (
            nt(qkv_grad[...], w[start : start + step, :three])
            + nt(hidden_grad[...], w[start : start + step, three:])
        ).astype(out.dtype)


def unmix_tile(g, w, hidden, attended_grad, hidden_grad, sums):
    parts, inner, columns = w.shape
    width = attended_grad.shape[1]
    units = hidden.shape[1]

    @pl.when(pl.program_id(0) == 0)
    def _():
        sums[...] = jnp.zeros_like(sums)

    def back(lo, hi):
        total = nt(g[:, :columns], w[0, lo:hi, :])
        for d in range(1, parts):
            total = total + nt(g[:, d * columns : (d + 1) * columns], w[d, lo:hi, :])
        return total

    attended_grad[...] = back(0, width).astype(BF16)
    step = min(256, units)
    for start in range(0, units, step):
        at = slice(start, start + step)
        low = (back(width + start, width + start + step) * gelu_slope(hidden[:, at])).astype(BF16)
        hidden_grad[:, at] = low
        sums[:, at] += jnp.sum(low.astype(F32), axis=0, keepdims=True)


def unmix(g, w, hidden, width, first, count, length, riding=(), ident=None, tile=512):
    rows = count * length
    units = hidden.shape[1]
    parts, inner, columns = w.shape
    depth = parts * columns
    per = length // tile
    row = lambda n: pl.BlockSpec((tile, n), lambda i: (i, 0))
    late = lambda n: pl.BlockSpec((tile, n), lambda i: (first * per + i, 0))
    return launch(
        unmix_tile,
        [g, w, hidden],
        [late(depth), once(w.shape, lambda i: (0, 0, 0)), late(units)],
        [row(width), row(units), pl.BlockSpec((1, units), lambda i: (0, 0))],
        [
            jax.ShapeDtypeStruct((rows, width), BF16),
            jax.ShapeDtypeStruct((rows, units), BF16),
            jax.ShapeDtypeStruct((1, units), F32),
        ],
        rows // tile,
        "unmix",
        cost(2 * rows * inner * depth, 2 * depth * (rows + inner) + rows * units * 6),
        riding=riding,
        ident=ident,
    )


def unmix_gather_body(first, tile, moves, last_moves, at, w, hidden, whole_in, attended_grad, hidden_grad, sums, full, g, local, *sems):
    step, last = pl.program_id(0), pl.num_programs(0) - 1
    share = full.shape[2]
    per = share // tile
    early = Gather(*moves).copies(at, full, *sems[:2])
    late = Gather(*last_moves).copies(at, full, *sems[2:])

    def load(i):
        n = first * 2 * per + i
        rows = pl.ds(pl.multiple_of(lax.rem(n, per) * tile, tile), tile)
        return pltpu.make_async_copy(
            full.at[lax.div(n, 2 * per), lax.rem(lax.div(n, per), 2), rows],
            g.at[lax.rem(i, 2)],
            local.at[lax.rem(i, 2)],
        )

    @pl.when(step == 0)
    def _():
        start_all(at, early)
        load(step).start()

    @pl.when(step < last)
    def _():
        load(step + 1).start()

    load(step).wait()
    unmix_tile(g.at[lax.rem(step, 2)], w, hidden, attended_grad, hidden_grad, sums)

    @pl.when(step == last)
    def _():
        finish_all(at, early)
        start_all(at, late)
        finish_all(at, late)


def unmix_gather(full, w, hidden, width, first, count, length, moves, last_moves, ident, riding=(), tile=512):
    rows = count * length
    units = hidden.shape[1]
    parts, inner, columns = w.shape
    depth = parts * columns
    per = length // tile
    row = lambda n: pl.BlockSpec((tile, n), lambda i: (i, 0))
    counts = [Gather(*moves).count, Gather(*last_moves).count]

    body = functools.partial(unmix_gather_body, first, tile, moves, last_moves)
    extra = list(riding)
    args = [w, hidden, full] + [a for r in extra for a in r.ins]
    shapes = [
        jax.ShapeDtypeStruct((rows, width), BF16),
        jax.ShapeDtypeStruct((rows, units), BF16),
        jax.ShapeDtypeStruct((1, units), F32),
        like(full),
    ]
    aliases, n_in, n_out = {2: 3}, 3, 4
    for r in extra:
        if r.aliased:
            aliases[n_in + len(r.ins) - 1] = n_out
        n_in, n_out = n_in + len(r.ins), n_out + len(r.outs)

    def kernel(*refs):
        take = iter(refs)
        some = lambda n: [next(take) for _ in range(n)]
        own_ins, ride_ins = some(3), [some(len(r.ins)) for r in extra]
        own_outs, ride_outs = some(4), [some(len(r.outs)) for r in extra]
        own_scratch = some(6)
        at = places()
        copies = []
        for r, i, o in zip(extra, ride_ins, ride_outs):
            copies += r.copies(at, i, o, *some(2))

        @pl.when(pl.program_id(0) == 0)
        def _():
            greet(at)
            start_all(at, copies)

        body(at, *own_ins, *own_outs, *own_scratch)

        @pl.when(pl.program_id(0) == rows // tile - 1)
        def _():
            finish_all(at, copies)

    return pl.pallas_call(
        kernel,
        grid=(rows // tile,),
        in_specs=[
            once(w.shape, lambda i: (0, 0, 0)),
            pl.BlockSpec((tile, units), lambda i: (first * per + i, 0)),
        ]
        + [ANYWHERE] * (len(args) - 2),
        out_specs=[row(width), row(units), pl.BlockSpec((1, units), lambda i: (0, 0)), ANYWHERE]
        + [ANYWHERE for r in extra for _ in r.outs],
        out_shape=shapes + [o for r in extra for o in r.outs],
        input_output_aliases=aliases,
        scratch_shapes=[pltpu.VMEM((2, tile, depth), BF16), pltpu.SemaphoreType.DMA((2,))]
        + [pltpu.SemaphoreType.DMA((max(n, 1),)) for n in counts for _ in range(2)]
        + [pltpu.SemaphoreType.DMA((r.count,)) for r in extra for _ in range(2)],
        compiler_params=pltpu.CompilerParams(
            dimension_semantics=("arbitrary",),
            vmem_limit_bytes=VMEM_BYTES,
            collective_id=ident,
            has_side_effects=True,
        ),
        cost_estimate=cost(2 * rows * inner * depth, 2 * depth * (rows + inner) + rows * units * 6),
        name="unmix",
    )(*args)


def outer_rows_kernel(x, *refs):
    parts, out = refs[:-1], refs[-1]
    total, start = None, 0
    for part in parts:
        term = tn(x[start : start + part.shape[0], :], part[...])
        total = term if total is None else total + term
        start += part.shape[0]
    out[...] = total.astype(out.dtype)


def outer_rows(x, parts, riding=(), ident=None, tile=512, wait_for=()):
    rows, depth = x.shape
    n = parts[0].shape[1]
    tile = min(tile, depth)
    return launch(
        outer_rows_kernel,
        [x, *parts],
        [pl.BlockSpec((rows, tile), lambda i: (0, i))]
        + [once(p.shape, lambda i: (0, 0)) for p in parts],
        [pl.BlockSpec((tile, n), lambda i: (i, 0))],
        [jax.ShapeDtypeStruct((depth, n), BF16)],
        depth // tile,
        "outer_rows",
        cost(2 * rows * depth * n, 2 * (rows * (depth + n) + depth * n)),
        riding=riding,
        ident=ident,
        wait_for=wait_for,
    )


def outer_columns_kernel(parts, b, g, *refs):
    many, out = refs[:parts], refs[-1]
    width = many[0].shape[1]
    total, start = None, 0
    for a in many:
        term = tn(a[...], g[start : start + a.shape[0], :])
        total = term if total is None else total + term
        start += a.shape[0]
    out[0, :width, :] = total.astype(out.dtype)
    out[0, width:, :] = tn(b[...], g[...]).astype(out.dtype)


def outer_columns(many, b, g, parts, riding=(), ident=None):
    rows, depth = g.shape
    width, units = many[0].shape[1], b.shape[1]
    tile = depth // parts
    return launch(
        functools.partial(outer_columns_kernel, len(many)),
        [b, g, *many],
        [once((rows, units), lambda i: (0, 0)), pl.BlockSpec((rows, tile), lambda i: (0, i))]
        + [once(a.shape, lambda i: (0, 0)) for a in many],
        [pl.BlockSpec((1, width + units, tile), lambda i: (i, 0, 0))],
        [jax.ShapeDtypeStruct((parts, width + units, tile), BF16)],
        parts,
        "outer_columns",
        cost(2 * rows * depth * (width + units), 2 * (rows * (depth + width + units) + depth * (width + units))),
        riding=riding,
        ident=ident,
    )


def head_lanes(width, head):
    return lax.broadcasted_iota(jnp.int32, (1, width), 1) // HEAD_DIM == head


def attend_kernel(q, k, v, column_ids, row_ids, out, log_sums):
    length, width = q.shape
    heads = width // HEAD_DIM
    tile = min(SPAN, length)
    lanes = lax.broadcasted_iota(jnp.int32, (1, 128), 1)
    for begin in range(0, length, tile):
        end = min(length, begin + tile + SPAN)
        q_ids = column_ids[begin : begin + tile, :]
        blocked = row_ids[:, begin:end] > q_ids
        rows = q[begin : begin + tile, :]

        def one_head(head, carry):
            total, sums = carry
            mine = head_lanes(width, head)
            scores = nt(jnp.where(mine, rows, jnp.zeros_like(rows)), k[:end, :])
            tail = jnp.where(blocked, -1e9, scores[:, begin:])
            scores = jnp.concatenate([scores[:, :begin], tail], axis=1) if begin else tail
            highest = jnp.max(scores, axis=1, keepdims=True)
            powers = jnp.exp(scores - highest)
            amount = jnp.sum(powers, axis=1, keepdims=True)
            low = (powers * (1.0 / amount)).astype(BF16)
            total = jnp.where(mine, nn(low, v[:end, :]), total)
            sums = jnp.where(lanes == head, highest + jnp.log(amount), sums)
            return total, sums

        total, sums = jnp.zeros((tile, width), F32), jnp.zeros((tile, 128), F32)
        for head in range(heads):
            total, sums = one_head(head, (total, sums))
        out[begin : begin + tile, :] = total.astype(BF16)
        log_sums[:, begin : begin + tile] = sums.T[:8, :]


def attend(first, count, q, k, v, column_ids, row_ids, riding=(), ident=None):
    width = q.shape[1]
    length = row_ids.shape[2]
    rows, seqs = count * length, count
    heads = width // HEAD_DIM
    seq = pl.BlockSpec((length, width), lambda s: (first + s, 0))
    out = pl.BlockSpec((length, width), lambda s: (s, 0))
    return launch(
        attend_kernel,
        [q, k, v, column_ids, row_ids],
        [
            seq,
            seq,
            seq,
            pl.BlockSpec((length, 1), lambda s: (first + s, 0)),
            pl.BlockSpec((None, 1, length), lambda s: (first + s, 0, 0)),
        ],
        [out, pl.BlockSpec((8, length), lambda s: (0, s))],
        [jax.ShapeDtypeStruct((rows, width), BF16), jax.ShapeDtypeStruct((8, rows), F32)],
        seqs,
        "attend",
        cost(8 * seqs * heads * length * length * 256 * 0.8, 8 * rows * width, seqs * heads * length**2),
        riding=riding,
        ident=ident,
    )


def unattend_kernel(
    q, k, v, g, log_sums, column_ids, row_ids, cos, low, high, out, sums, key_total, value_total
):
    length, width = q.shape
    heads = width // HEAD_DIM
    tile = min(SPAN, length)
    tables = (cos[...], -low[...], -high[...])

    @pl.when(pl.program_id(0) == 0)
    def _():
        sums[...] = jnp.zeros_like(sums)

    key_total[...] = jnp.zeros_like(key_total)
    value_total[...] = jnp.zeros_like(value_total)
    for begin in range(0, length, tile):
        end = min(length, begin + tile + SPAN)
        at = slice(begin, begin + tile)
        blocked = column_ids[begin:end, :] > row_ids[:, at]
        q_rows, g_rows = q[at, :], g[at, :]
        query_total = jnp.zeros((tile, width), F32)
        for head in range(heads):
            mine = head_lanes(width, head)
            q_head = jnp.where(mine, q_rows, jnp.zeros_like(q_rows))
            g_head = jnp.where(mine, g_rows, jnp.zeros_like(g_rows))
            scores = nt(k[:end, :], q_head)
            tail = jnp.where(blocked, -1e9, scores[begin:, :])
            scores = jnp.concatenate([scores[:begin, :], tail], axis=0) if begin else tail
            probs = jnp.exp(scores - log_sums[head : head + 1, at])
            value_total[:end, :] += nn(probs.astype(BF16), g_head)
            prob_grad = nt(v[:end, :], g_head)
            inner = jnp.sum(prob_grad * probs, axis=0, keepdims=True)
            score_grad = (probs * (prob_grad - inner)).astype(BF16)
            key_total[:end, :] += nn(score_grad, q_head)
            query_total = jnp.where(mine, tn(score_grad, k[:end, :]), query_total)
        turned = rotated(query_total * HEAD_DIM**-0.5, *(t[at, :] for t in tables)).astype(BF16)
        out[at, :width] = turned
        sums[:, :width] += jnp.sum(turned.astype(F32), axis=0, keepdims=True)
    turned = rotated(key_total[...], *tables).astype(BF16)
    out[:, width : 2 * width] = turned
    sums[:, width : 2 * width] += jnp.sum(turned.astype(F32), axis=0, keepdims=True)
    turned = value_total[...].astype(BF16)
    out[:, 2 * width :] = turned
    sums[:, 2 * width :] += jnp.sum(turned.astype(F32), axis=0, keepdims=True)


def unattend(first, count, q, k, v, g, g_first, log_sums, sums_first, column_ids, row_ids, tables, riding=(), ident=None, wait_for=()):
    width = q.shape[1]
    length = row_ids.shape[2]
    rows, seqs = count * length, count
    heads = width // HEAD_DIM
    seq = pl.BlockSpec((length, width), lambda s: (first + s, 0))
    table = once((length, 128), lambda s: (0, 0))
    return launch(
        unattend_kernel,
        [q, k, v, g, log_sums, column_ids, row_ids, *tables],
        [
            seq,
            seq,
            seq,
            pl.BlockSpec((length, width), lambda s: (g_first + s, 0)),
            pl.BlockSpec((8, length), lambda s: (0, sums_first + s)),
            pl.BlockSpec((length, 1), lambda s: (first + s, 0)),
            pl.BlockSpec((None, 1, length), lambda s: (first + s, 0, 0)),
            table,
            table,
            table,
        ],
        [
            pl.BlockSpec((length, 3 * width), lambda s: (s, 0)),
            pl.BlockSpec((1, 3 * width), lambda s: (0, 0)),
        ],
        [jax.ShapeDtypeStruct((rows, 3 * width), BF16), jax.ShapeDtypeStruct((1, 3 * width), F32)],
        count,
        "unattend",
        cost(20 * seqs * heads * length * length * 256 * 0.8, 14 * rows * width, seqs * heads * length**2),
        scratch=[pltpu.VMEM((length, width), F32), pltpu.VMEM((length, width), F32)],
        riding=riding,
        ident=ident,
        wait_for=wait_for,
    )


def add_up(*parts):
    total = parts[0].astype(F32)
    for part in parts[1:]:
        total = total + part.astype(F32)
    return total.astype(BF16)


def after(values, *others):
    return lax.optimization_barrier((values,) + others)[0]


def sum_everywhere_kernel(groups, members, gain, shift, bias, qkv, up, wide, narrow, buf, in_dp, in_tensor, send_dp, got_dp, send_tensor, got_tensor):
    dp, tensor = lax.axis_index("dp"), lax.axis_index("tensor")
    mesh = pl.DeviceIdType.MESH
    barrier = pltpu.get_barrier_semaphore()
    for step in range(1, groups):
        pl.semaphore_signal(barrier, inc=1, device_id={"dp": lax.rem(dp + step, groups)}, device_id_type=mesh)
    for step in range(1, members):
        pl.semaphore_signal(barrier, inc=1, device_id={"tensor": lax.rem(tensor + step, members)}, device_id_type=mesh)
    pl.semaphore_wait(barrier, groups + members - 2)
    lanes = buf.shape[2] // 4
    for k, ref in enumerate((gain, shift, bias)):
        for r in range(8):
            buf[0, r : r + 1, k * lanes : (k + 1) * lanes] = ref[:, r * lanes : (r + 1) * lanes]
    row = 0
    buf[0, :, 3 * lanes :] = jnp.zeros((8, lanes), F32)
    for ref in (qkv, up):
        for start in range(0, ref.shape[1], lanes):
            buf[0, row : row + 1, 3 * lanes :] = ref[:, start : start + lanes]
            row += 1

    def exchange(axis, me, size, source, into, send, got):
        copies = []
        for step in range(1, size):
            copies.append(
                pltpu.make_async_remote_copy(
                    src_ref=source,
                    dst_ref=into.at[step - 1],
                    send_sem=send.at[step - 1],
                    recv_sem=got.at[step - 1],
                    device_id={axis: lax.rem(me + step, size)},
                    device_id_type=mesh,
                )
            )
        for copy in copies:
            copy.start()
        for copy in copies:
            copy.wait()

    exchange("dp", dp, groups, buf.at[0], in_dp, send_dp, got_dp)
    total = buf[0]
    for step in range(groups - 1):
        total = total + in_dp[step]
    row = 0
    for start in range(0, narrow.shape[1], lanes):
        narrow[:, start : start + lanes] = total[row : row + 1, 3 * lanes :]
        row += 1
    buf[1] = total
    exchange("tensor", tensor, members, buf.at[1], in_tensor, send_tensor, got_tensor)
    total = buf[1]
    for step in range(members - 1):
        total = total + in_tensor[step]
    for k in range(3):
        for r in range(8):
            wide[k : k + 1, r * lanes : (r + 1) * lanes] = total[r : r + 1, k * lanes : (k + 1) * lanes]


def sum_everywhere(ident, groups, members, gain, shift, bias, qkv, up):
    depth = gain.shape[1]
    whole = pl.BlockSpec(memory_space=pltpu.VMEM)
    return pl.pallas_call(
        functools.partial(sum_everywhere_kernel, groups, members),
        in_specs=[whole] * 5,
        out_specs=[whole] * 2,
        out_shape=[
            jax.ShapeDtypeStruct((8, depth), F32),
            jax.ShapeDtypeStruct((1, qkv.shape[1] + up.shape[1]), F32),
        ],
        scratch_shapes=[
            pltpu.VMEM((2, 8, depth // 2), F32),
            pltpu.VMEM((groups - 1, 8, depth // 2), F32),
            pltpu.VMEM((members - 1, 8, depth // 2), F32),
            pltpu.SemaphoreType.DMA((groups - 1,)),
            pltpu.SemaphoreType.DMA((groups - 1,)),
            pltpu.SemaphoreType.DMA((members - 1,)),
            pltpu.SemaphoreType.DMA((members - 1,)),
        ],
        compiler_params=pltpu.CompilerParams(collective_id=ident, has_side_effects=True),
        name="sum_everywhere",
    )(gain, shift, bias, qkv, up)


def per_device(
    inputs,
    block_ids,
    norm_gain,
    norm_bias,
    query_weight,
    query_bias,
    key_weight,
    key_bias,
    value_weight,
    value_bias,
    out_weight,
    out_bias,
    up_weight,
    up_bias,
    down_weight,
    down_bias,
    grad_out,
):
    seqs, length = block_ids.shape
    share, depth = inputs.shape
    width = query_weight.shape[1]
    units = up_weight.shape[1]
    groups, members = lax.axis_size("dp"), lax.axis_size("tensor")
    gain, shift = norm_gain.astype(F32)[None, :], norm_bias.astype(F32)[None, :]
    paired = groups == 4 and members == 8 and seqs == 4 and 2 * share == length
    me = lax.axis_index("tensor")
    if paired:
        chip = me // 2
        order = jnp.arange(3, -1, -1, dtype=jnp.int32) ^ chip
        inner = ((chip == 1) | (chip == 2)).astype(jnp.int32)
    else:
        order = jnp.arange(seqs, dtype=jnp.int32)

    ids = block_ids[order]
    column_ids = ids.reshape(seqs * length, 1)
    row_ids = ids.reshape(seqs, 1, length)
    pair = seqs // 2
    everything = seqs * length
    idents = iter(range(1, 100))

    if paired:
        kept = lambda values: jnp.where(inner == 1, values, jnp.zeros_like(values))
        cuts = lambda fraction: int(share * fraction) // 32 * 32
        g1, g1_more = cuts(0.25), cuts(0.56)
        rows, full, first_full, second_full, q, k, v, active, hidden, *tables = opening(
            next(idents),
            inputs,
            norm_gain[None, :],
            norm_bias[None, :],
            grad_out,
            [query_weight, key_weight, value_weight, up_weight, out_weight, down_weight],
            [b[None, :] for b in (query_bias, key_bias, value_bias, up_bias)],
            groups,
            length,
            g1,
        )
        rows = rows.reshape(everything, depth)
        first_full = first_full.reshape(depth, 3 * width + units)

        def heads(at, riding):
            return attend(at, pair, q, k, v, column_ids, row_ids, riding=riding, ident=next(idents))

        def mixed(values, at, riding):
            return core_sum(
                mix_body,
                next(idents),
                pair,
                length,
                [(values, 0), (active, at)],
                second_full,
                depth,
                "mix",
                riding=riding,
            )

        def unheads(at, count, g, g_at, sums, sums_at, riding, wait_for=()):
            return unattend(
                at,
                count,
                q,
                k,
                v,
                g,
                g_at,
                sums,
                sums_at,
                column_ids,
                row_ids,
                tables,
                riding=riding,
                ident=next(idents),
                wait_for=wait_for,
            )

        def unprojected(count, grads, riding):
            return core_sum(
                unproject_body,
                next(idents),
                count,
                length,
                grads,
                first_full,
                depth,
                "unproject",
                riding=riding,
            )

        far_attended, far_sums, full = heads(0, [gathering(full, (1, g1, g1_more))])
        *far, full = mixed(far_attended, 0, [gathering(full, (1, g1_more, share))])

        part = cuts(0.44)
        near_attended, near_sums, full, end = heads(
            pair,
            [
                gathering(full, (2, 0, part), ("first", 0, share)),
                sending(far[0], "in", 0, part),
            ],
        )
        *near, full, end = mixed(
            near_attended,
            pair,
            [gathering(full, (2, part, share)), sending(far[0], "in", part, share, end)],
        )

        crossing = add_up(far[1], end)
        part = cuts(0.4)
        near_attended_grad, near_hidden_grad, near_up_sum, full, end, middle = unmix_gather(
            full,
            second_full,
            hidden,
            width,
            pair,
            pair,
            length,
            [(3, 0, part), ("second", 0, share)],
            [],
            next(idents),
            riding=[sending(far[1], "in", 0, part), sending(crossing, "middle", 0, part)],
        )
        near_grad, near_sum, full, end, middle = unheads(
            pair,
            pair,
            near_attended_grad,
            0,
            near_sums,
            0,
            [
                gathering(
                    full, (3, part, share), ("third", 0, part), late=[("third", part, share)]
                ),
                sending(far[1], "in", part, share, end),
                sending(crossing, "middle", part, share, middle),
            ],
        )
        upstream = full.reshape(everything, depth)

        to_side = add_up(near[0], kept(middle))
        to_middle = add_up(far[0], end)
        mine = near[1]
        part, more = cuts(0.4), cuts(0.75)

        def outward(lo, hi, side=None, middle=None):
            return [sending(to_side, "side", lo, hi, side), sending(to_middle, "middle", lo, hi, middle)]

        far_attended_grad, far_hidden_grad, far_up_sum, side, middle = unmix(
            upstream,
            second_full,
            hidden,
            width,
            0,
            pair,
            length,
            riding=outward(0, part),
            ident=next(idents),
        )
        up_sum = near_up_sum + far_up_sum
        grads_0, sum_0, side, middle = unheads(
            0, 1, far_attended_grad, 0, far_sums, 0, outward(part, more, side, middle)
        )
        far_0, side, middle = unprojected(
            1, [(grads_0, 0), (far_hidden_grad, 0)], outward(more, share, side, middle)
        )
        terms = [mine, side, kept(middle)]

        part, more = cuts(0.5), cuts(0.8)
        second_part, end = outer_columns(
            [far_attended, near_attended],
            active,
            upstream,
            groups,
            riding=[sending(far_0, "in", 0, part)],
            ident=next(idents),
        )
        second_grad = lax.psum_scatter(second_part, "dp", scatter_dimension=0)
        grads_1, sum_1, end = unheads(
            1,
            1,
            far_attended_grad,
            1,
            far_sums,
            1,
            [sending(far_0, "in", part, more, end)],
            wait_for=[second_part],
        )
        far_1, end = unprojected(
            1, [(grads_1, 0), (far_hidden_grad, 1)], [sending(far_0, "in", more, share, end)]
        )
    else:
        tables = rotary_tables(length)
        first = jnp.concatenate([query_weight, key_weight, value_weight, up_weight], axis=1)
        second = jnp.concatenate([out_weight, down_weight], axis=0)
        bias = jnp.concatenate([query_bias, key_bias, value_bias, up_bias]).astype(F32)[None, :]
        first_full = lax.all_gather(first, "dp", axis=0, tiled=True)
        second_full = lax.all_gather(second, "dp", axis=0)
        rows = lax.all_gather(norm(inputs, gain, shift), "tensor", axis=0, tiled=True)
        upstream = lax.all_gather(grad_out, "tensor", axis=0, tiled=True)
        q, k, v, active, hidden = project(rows, first_full, bias, tables, width, units, length)
        attended, log_sums = attend(0, seqs, q, k, v, column_ids, row_ids)
        whole = each_tile(mix_body, [attended, active], second_full, depth, "mix")
        terms = [lax.psum_scatter(whole, "tensor", scatter_dimension=0, tiled=True)]
        attended_grad, hidden_grad, up_sum = unmix(
            upstream, second_full, hidden, width, 0, seqs, length
        )
    total = inputs.astype(F32) + out_bias.astype(F32) + down_bias.astype(F32)
    for values in terms:
        total = total + values.astype(F32)
    output = total.astype(BF16)

    if paired:
        crossing = add_up(far_1, end)
        part = cuts(0.5)
        up_part, end, middle = outer_rows(
            rows,
            [far_hidden_grad, near_hidden_grad],
            riding=[sending(far_1, "in", 0, part), sending(crossing, "middle", 0, part)],
            ident=next(idents),
            wait_for=[output],
        )
        up_grad = lax.psum_scatter(up_part, "dp", scatter_dimension=0, tiled=True)
        *near, end, middle = unprojected(
            pair,
            [(near_grad, 0), (near_hidden_grad, 0)],
            [
                sending(far_1, "in", part, share, end),
                sending(crossing, "middle", part, share, middle),
            ],
        )
        qkv_sum = sum_0 + sum_1 + near_sum
        to_side = add_up(near[0], kept(middle))
        to_middle = add_up(far_0, end)
        first_part, side, middle = outer_rows(
            rows,
            [grads_0, grads_1, near_grad],
            riding=[sending(to_side, "side", 0, share), sending(to_middle, "middle", 0, share)],
            ident=next(idents),
            wait_for=[second_grad],
        )
        first_grad = lax.psum_scatter(first_part, "dp", scatter_dimension=0, tiled=True)
        terms = [near[1], side, middle]
    else:
        inner = jnp.ones((), jnp.int32)
        qkv_grad, qkv_sum = unattend(
            0, seqs, q, k, v, attended_grad, 0, log_sums, 0, column_ids, row_ids, tables
        )
        whole = each_tile(unproject_body, [qkv_grad, hidden_grad], first_full, depth, "unproject")
        terms = [lax.psum_scatter(whole, "tensor", scatter_dimension=0, tiled=True)]
        (second_part,) = outer_columns([attended], active, upstream, groups)
        (first_part,) = outer_rows(rows, [qkv_grad])
        (up_part,) = outer_rows(rows, [hidden_grad])
        second_grad = lax.psum_scatter(second_part, "dp", scatter_dimension=0)
        first_grad = lax.psum_scatter(first_part, "dp", scatter_dimension=0, tiled=True)
        up_grad = lax.psum_scatter(up_part, "dp", scatter_dimension=0, tiled=True)

    second_grad, first_grad, up_grad = (t.astype(F32) for t in (second_grad, first_grad, up_grad))
    input_grad, gain_part, shift_part = unnorm(
        inner[None], inputs, grad_out, gain, terms, [up_grad] if paired else []
    )
    bias_part = jnp.sum(grad_out, axis=0, dtype=F32)[None, :]
    if paired and groups == 4:
        wide, narrow = sum_everywhere(
            next(idents), groups, members, gain_part, shift_part, bias_part, qkv_sum, up_sum
        )
        gain_grad, shift_grad, outer_bias_grad = wide[0], wide[1], wide[2]
        qkv_sum, up_sum = narrow[0, : 3 * width], narrow[0, 3 * width :]
    else:
        gain_grad, shift_grad, outer_bias_grad = lax.psum(
            (gain_part[0], shift_part[0], bias_part[0]), ("dp", "tensor")
        )
        qkv_sum, up_sum = lax.psum((qkv_sum[0], up_sum[0]), "dp")
    return (
        output,
        input_grad,
        gain_grad,
        shift_grad,
        first_grad[:, :width],
        qkv_sum[:width],
        first_grad[:, width : 2 * width],
        qkv_sum[width : 2 * width],
        first_grad[:, 2 * width :],
        qkv_sum[2 * width :],
        second_grad[:width],
        outer_bias_grad,
        up_grad,
        up_sum,
        second_grad[width:],
        outer_bias_grad,
    )


def solution(mesh):
    tokens = P(("dp", "tensor"), None)
    down = P("dp", "tensor")
    across = P("tensor", "dp")
    part = P("tensor")
    return jax.shard_map(
        per_device,
        mesh=mesh,
        in_specs=(
            tokens,
            P("dp", None),
            P(),
            P(),
            down,
            part,
            down,
            part,
            down,
            part,
            across,
            P(),
            down,
            part,
            across,
            P(),
            tokens,
        ),
        out_specs=(
            tokens,
            tokens,
            P(),
            P(),
            down,
            part,
            down,
            part,
            down,
            part,
            across,
            P(),
            down,
            part,
            across,
            P(),
        ),
        check_vma=False,
    )
```

```python
import functools

import jax
import jax.numpy as jnp
import numpy as np
from jax import lax
from jax.experimental import pallas as pl
from jax.experimental.pallas import tpu as pltpu
from jax.sharding import PartitionSpec as P

HEAD_DIM = 64
ROT = 32
SPAN = 256
EPS = 1e-05
F32 = jnp.float32
BF16 = jnp.bfloat16
VMEM_BYTES = 60 * 2**20


def nn(a, b):
    return jnp.dot(a, b, preferred_element_type=F32)


def nt(a, b):
    return lax.dot_general(a, b, (((1,), (1,)), ((), ())), preferred_element_type=F32)


def tn(a, b):
    return lax.dot_general(a, b, (((0,), (0,)), ((), ())), preferred_element_type=F32)


def params(semantics):
    return pltpu.CompilerParams(dimension_semantics=semantics, vmem_limit_bytes=VMEM_BYTES)


def cost(flops, bytes_accessed, transcendentals=0):
    return pl.CostEstimate(
        flops=int(flops) // 10,
        bytes_accessed=int(bytes_accessed) // 10,
        transcendentals=int(transcendentals) // 10,
    )


def once(shape, index_map):
    return pl.BlockSpec(shape, index_map, pipeline_mode=pl.Buffered(1))


def rotary_tables(length):
    halves = ROT // 2
    exponent = jnp.arange(halves, dtype=F32) * (2.0 / ROT)
    frequency = jnp.power(10000.0, -exponent)
    angles = jnp.arange(length, dtype=F32)[:, None] * frequency[None, :]
    cos, sin = jnp.cos(angles), jnp.sin(angles)
    zero = jnp.zeros((length, halves), F32)
    rest = HEAD_DIM - ROT
    head = lambda a, b, fill: jnp.concatenate([a, b, jnp.full((length, rest), fill, F32)], axis=1)
    return tuple(
        jnp.concatenate([t, t], axis=1)
        for t in (head(cos, cos, 1.0), head(-sin, zero, 0.0), head(zero, sin, 0.0))
    )


def rotated(values, cos, low, high):
    halves = ROT // 2
    pieces = []
    for start in range(0, values.shape[1], 128):
        u = values[:, start : start + 128]
        pieces.append(
            u * cos + pltpu.roll(u, 128 - halves, 1) * low + pltpu.roll(u, halves, 1) * high
        )
    return pieces[0] if len(pieces) == 1 else jnp.concatenate(pieces, axis=1)


GELU_A = 0.7978845608028654
GELU_B = 0.044715


def gelu(v):
    return 0.5 * v * (1.0 + jnp.tanh(GELU_A * (v + GELU_B * (v * v * v))))


def gelu_slope(v):
    square = v * v
    half = 0.5 + 0.5 * jnp.tanh(v * (GELU_A + GELU_A * GELU_B * square))
    return half + (half - half * half) * (v * (2.0 * GELU_A + 6.0 * GELU_A * GELU_B * square))


def norm_kernel(x, gain, shift, out):
    values = x[...].astype(F32)
    centered = values - jnp.mean(values, axis=1, keepdims=True)
    scale = lax.rsqrt(jnp.mean(centered * centered, axis=1, keepdims=True) + EPS)
    out[...] = (centered * scale * gain[...] + shift[...]).astype(BF16)


def norm(x, gain, shift, tile=128):
    rows, depth = x.shape
    row = pl.BlockSpec((tile, depth), lambda i: (i, 0))
    one = once((1, depth), lambda i: (0, 0))
    return pl.pallas_call(
        norm_kernel,
        grid=(rows // tile,),
        in_specs=[row, one, one],
        out_specs=row,
        out_shape=jax.ShapeDtypeStruct((rows, depth), BF16),
        compiler_params=params(("arbitrary",)),
        cost_estimate=cost(10 * rows * depth, 4 * rows * depth),
        name="norm",
    )(x, gain, shift)


def closing_kernel(terms, flag, x, g, gain, bias, other_bias, second, up, *refs):
    parts, more, refs = refs[:terms], refs[terms : 2 * terms], refs[2 * terms :]
    input_grad, output, gain_sum, shift_sum, out_grad, down_grad, up_grad = refs

    @pl.when(pl.program_id(0) == 0)
    def _():
        gain_sum[...] = jnp.zeros_like(gain_sum)
        shift_sum[...] = jnp.zeros_like(shift_sum)
        width = out_grad.shape[0]
        out_grad[...] = second[:width, :].astype(F32)
        down_grad[...] = second[width:, :].astype(F32)

    def total(many):
        result = many[0][...].astype(F32)
        for part in many[1:]:
            term = part[...].astype(F32)
            if part is many[-1]:
                term = jnp.where(flag[0] == 1, term, 0.0)
            result = result + term
        return result

    up_grad[...] = up[...].astype(F32)
    values = x[...].astype(F32)
    output[...] = (
        values + total(more) + bias[...].astype(F32) + other_bias[...].astype(F32)
    ).astype(BF16)
    centered = values - jnp.mean(values, axis=1, keepdims=True)
    scale = lax.rsqrt(jnp.mean(centered * centered, axis=1, keepdims=True) + EPS)
    hat = centered * scale
    back = total(parts)
    gain_sum[...] += jnp.sum(back * hat, axis=0, keepdims=True)
    shift_sum[...] += jnp.sum(back, axis=0, keepdims=True)
    e = back * gain[...]
    inner = (
        e - jnp.mean(e, axis=1, keepdims=True) - hat * jnp.mean(e * hat, axis=1, keepdims=True)
    )
    input_grad[...] = (g[...].astype(F32) + inner * scale).astype(BF16)


def closing(flag, x, g, gain, bias, other_bias, second, up, width, parts, more, tile=128):
    rows, depth = x.shape
    row = pl.BlockSpec((tile, depth), lambda i, f: (i, 0))
    one = once((1, depth), lambda i, f: (0, 0))
    total = pl.BlockSpec((1, depth), lambda i, f: (0, 0))
    still = lambda shape: once(shape, lambda i, f: (0, 0))
    step = up.shape[0] // (rows // tile)
    ups = pl.BlockSpec((step, up.shape[1]), lambda i, f: (i, 0))
    inner, columns = second.shape
    return pl.pallas_call(
        functools.partial(closing_kernel, len(parts)),
        grid_spec=pltpu.PrefetchScalarGridSpec(
            num_scalar_prefetch=1,
            grid=(rows // tile,),
            in_specs=[row, row, one, one, one, still(second.shape), ups] + [row] * (2 * len(parts)),
            out_specs=[
                row,
                row,
                total,
                total,
                still((width, columns)),
                still((inner - width, columns)),
                ups,
            ],
        ),
        out_shape=[
            jax.ShapeDtypeStruct((rows, depth), BF16),
            jax.ShapeDtypeStruct((rows, depth), BF16),
            jax.ShapeDtypeStruct((1, depth), F32),
            jax.ShapeDtypeStruct((1, depth), F32),
            jax.ShapeDtypeStruct((width, columns), F32),
            jax.ShapeDtypeStruct((inner - width, columns), F32),
            jax.ShapeDtypeStruct(up.shape, F32),
        ],
        compiler_params=params(("arbitrary",)),
        cost_estimate=cost(30 * rows * depth, 14 * rows * depth),
        name="closing",
    )(flag, x, g, gain, bias, other_bias, second, up, *parts, *more)


MESH = pl.DeviceIdType.MESH
ANYWHERE = pl.BlockSpec(memory_space=pl.ANY)


def places():
    me = lax.axis_index("tensor")
    core, chip = lax.rem(me, 2), lax.div(me, 2)
    beside = chip + 1 - 2 * lax.rem(chip, 2)
    inner = jnp.logical_or(chip == 1, chip == 2)
    return dict(
        core=core,
        partner=me + 1 - 2 * core,
        beside=2 * beside + core,
        opposite=2 * (3 - chip) + core,
        inner=inner,
        outer=jnp.logical_not(inner),
        all=None,
    )


def greet(at, others=()):
    barrier = pltpu.get_barrier_semaphore()
    ids = [{"tensor": at[name]} for name in ("partner", "beside", "opposite")] + list(others)
    for device in ids:
        pl.semaphore_signal(barrier, inc=1, device_id=device, device_id_type=MESH)
    pl.semaphore_wait(barrier, len(ids))


def to_device(src, dst, sent, got, device):
    return pltpu.make_async_remote_copy(
        src_ref=src,
        dst_ref=dst,
        send_sem=sent,
        recv_sem=got,
        device_id=device,
        device_id_type=MESH,
    )


def under(condition, act):
    if condition is None:
        act()
    else:
        pl.when(condition)(act)


def start_all(at, copies):
    for sender, _, copy in copies:
        under(at[sender], copy.start)


def finish_all(at, copies):
    for sender, receiver, copy in copies:
        under(at[receiver], copy.wait_recv)
        under(at[sender], copy.wait_send)


class Gather:
    MOVES = {
        1: (("all", "all", 3, 2, "beside"), ("inner", "inner", 3, 0, "opposite")),
        2: (("inner", "inner", 2, 1, "opposite"), ("inner", "outer", 0, 1, "beside")),
        3: (("inner", "outer", 1, 0, "beside"),),
        "own": (("all", "all", 3, 3, "partner"),),
        "first": (("all", "all", 2, 2, "partner"), ("inner", "inner", 0, 0, "partner")),
        "second": (("all", "all", 1, 1, "partner"),),
        "third": (("outer", "outer", 0, 0, "partner"),),
    }

    def __init__(self, *moves):
        self.moves = [(m, lo, hi) for name, lo, hi in moves for m in self.MOVES[name]]
        self.count = len(self.moves)

    def copies(self, at, full, sent, got):
        found = []
        for i, ((sender, receiver, src, dst, target), lo, hi) in enumerate(self.moves):
            rows = pl.ds(lo, hi - lo)
            found.append(
                (
                    sender,
                    receiver,
                    to_device(
                        full.at[src, at["core"], rows],
                        full.at[dst, at["core"], rows],
                        sent.at[i],
                        got.at[i],
                        {"tensor": at[target]},
                    ),
                )
            )
        return found


class Riding:
    def __init__(self, ins, outs, aliased, count, copies, late=0):
        self.ins, self.outs, self.aliased, self.count, self.copies = ins, outs, aliased, count, copies
        self.late = late


def like(array):
    return jax.ShapeDtypeStruct(array.shape, array.dtype)


def gathering(full, *moves, late=()):
    plan = Gather(*moves, *late)

    def copies(at, ins, outs, sent, got):
        return plan.copies(at, outs[0], sent, got)

    return Riding([full], [like(full)], True, plan.count, copies, Gather(*late).count)


SENDS = {
    "in": ("outer", "inner", "beside"),
    "middle": ("inner", "inner", "opposite"),
    "side": ("all", "all", "beside"),
}


def sending(values, kind, lo, hi, into=None):
    sender, receiver, target = SENDS[kind]

    def copies(at, ins, outs, sent, got):
        rows = pl.ds(lo, hi - lo)
        copy = to_device(
            ins[0].at[rows], outs[0].at[rows], sent.at[0], got.at[0], {"tensor": at[target]}
        )
        return [(sender, receiver, copy)]

    return Riding([values] + ([] if into is None else [into]), [like(values)], into is not None, 1, copies)


def launch(body, args, ins, outs, shapes, grid, name, estimate, scratch=(), riding=(), ident=None, place=False, wait_for=(), lazy=(), seen=(), in_turn=False):
    if ident is None:
        return pl.pallas_call(
            functools.partial(body, lambda *which: None) if in_turn else body,
            grid=(grid,),
            in_specs=ins + [once(a.shape, lambda i, n=len(a.shape): (0,) * n) for a in lazy],
            out_specs=outs,
            out_shape=shapes,
            scratch_shapes=list(scratch),
            compiler_params=params(("arbitrary",)),
            cost_estimate=estimate,
            name=name,
        )(*args, *lazy)
    args, n_own = list(args) + list(lazy), len(args)
    riding = list(riding) + [Riding([a], [], False, 1, lambda *_: []) for a in wait_for]
    extra_in = [a for r in riding for a in r.ins]
    extra_out = [o for r in riding for o in r.outs]
    aliases, n_in, n_out = {}, len(args), len(shapes)
    for r in riding:
        if r.aliased:
            aliases[n_in + len(r.ins) - 1] = n_out
        n_in, n_out = n_in + len(r.ins), n_out + len(r.outs)

    def kernel(*refs):
        take = iter(refs)
        some = lambda n: [next(take) for _ in range(n)]
        own_ins, ride_ins = some(len(args)), [some(len(r.ins)) for r in riding]
        own_outs, ride_outs = some(len(shapes)), [some(len(r.outs)) for r in riding]
        own_scratch = some(len(scratch))
        loaded = some(len(lazy))
        loads = [
            pltpu.make_async_copy(src, dst, some(1)[0])
            for src, dst in zip(own_ins[n_own:], loaded)
        ]
        at = places()
        copies, late = [], []
        for r, i, o in zip(riding, ride_ins, ride_outs):
            found = r.copies(at, i, o, *some(2))
            copies += found[: len(found) - r.late]
            late += found[len(found) - r.late :]
        for load in loads:
            load.start()
        greet(at)
        start_all(at, copies)

        def ready(*which):
            @pl.when(pl.program_id(0) == 0)
            def _():
                for n in which:
                    loads[n].wait()

        def step(*blocks):
            if not in_turn:
                ready(*range(len(loads)))
            n_in = n_own + len(seen)
            body(*([at] if place else []), *([ready] if in_turn else []), *blocks[:n_in], *loaded, *blocks[n_in:], *own_scratch)

        if shapes:
            pltpu.emit_pipeline(
                step, grid=(grid,), in_specs=ins + [spec for _, spec in seen], out_specs=outs
            )(*own_ins[:n_own], *(ride_outs[r][0] for r, _ in seen), *own_outs)
        finish_all(at, copies)
        start_all(at, late)
        finish_all(at, late)

    return pl.pallas_call(
        kernel,
        in_specs=[ANYWHERE] * (len(args) + len(extra_in)),
        out_specs=[ANYWHERE] * (len(shapes) + len(extra_out)),
        out_shape=shapes + extra_out,
        input_output_aliases=aliases,
        scratch_shapes=list(scratch)
        + [pltpu.VMEM(a.shape, a.dtype) for a in lazy]
        + [pltpu.SemaphoreType.DMA] * len(lazy)
        + [pltpu.SemaphoreType.DMA((r.count,)) for r in riding for _ in range(2)],
        compiler_params=pltpu.CompilerParams(
            vmem_limit_bytes=VMEM_BYTES, collective_id=ident, has_side_effects=True
        ),
        cost_estimate=estimate,
        name=name,
    )(*args, *extra_in)


def opening_kernel(tile, groups, width, cut, *refs):
    x, gain, shift, g, *weights = refs[:10]
    biases, frequency, refs = refs[10:14], refs[14], refs[15:]
    rows_full, g_full, first_full, second_full, q, k, v, active, hidden, cos, low, high = refs[:12]
    own, kept, first_kept, second_kept, w, bias, x_tile = refs[12:19]
    staged, (local, x_sem, out_sem, w_sent, w_got), sems = refs[19:24], refs[24:29], refs[29:]
    at = places()
    core, dp = at["core"], lax.axis_index("dp")
    peers = [{"dp": jnp.bitwise_xor(dp, step)} for step in range(1, groups)]
    share, depth = own.shape
    half = share // 2
    units = hidden.shape[1]
    lows, highs = (0, half), (half, share)
    greet(at, peers)

    across = second_kept.shape[1]
    mine = pl.ds(pl.multiple_of(dp * across, across), across)
    columns = [(0, width), (width, width), (2 * width, width), (3 * width, units)]
    loads = [
        pltpu.make_async_copy(src, first_kept.at[:, pl.ds(start, size)], local.at[i])
        for i, (src, (start, size)) in enumerate(zip(weights[:4], columns))
    ] + [
        pltpu.make_async_copy(weights[4], second_kept.at[pl.ds(0, width)], local.at[4]),
        pltpu.make_async_copy(weights[5], second_kept.at[pl.ds(width, units)], local.at[5]),
        pltpu.make_async_copy(g, kept, local.at[6]),
    ]
    stores = [
        pltpu.make_async_copy(first_kept, first_full.at[dp], local.at[0]),
        pltpu.make_async_copy(second_kept, second_full.at[:, mine], local.at[1]),
        pltpu.make_async_copy(kept, g_full.at[3, core], local.at[2]),
        pltpu.make_async_copy(own, rows_full.at[3, core], local.at[7]),
    ]
    spread = [
        [to_device(src, dst, w_sent.at[n, i], w_got.at[n, i], peer) for i, peer in enumerate(peers)]
        for n, (src, dst) in enumerate(
            ((first_kept, first_full.at[dp]), (second_kept, second_full.at[:, mine]))
        )
    ]
    plans = dict(
        n1_low=[(1, *lows)],
        n1_high=[(1, *highs), ("own", 0, share)],
        n2_low=[(2, *lows)],
        n2_high=[(2, *highs)],
        e2_low=[("first", *lows)],
        e2_high=[("first", *highs)],
        n3_low=[(3, *lows)],
        n3_high=[(3, *highs)],
        e1_low=[("second", *lows)],
        e1_high=[("second", *highs)],
        e0_low=[("third", *lows)],
        e0_high=[("third", *highs)],
        g_own=[("own", 0, share)],
        g1=[(1, 0, cut)],
    )
    moves = {
        name: Gather(*plan).copies(
            at, g_full if name[0] == "g" else rows_full, sems[2 * i], sems[2 * i + 1]
        )
        for i, (name, plan) in enumerate(plans.items())
    }

    def start(*names):
        for name in names:
            start_all(at, moves[name])

    def finish(*names):
        for name in names:
            finish_all(at, moves[name])

    for copy in loads:
        copy.start()

    @pl.loop(0, share // tile)
    def _(i):
        rows = pl.ds(pl.multiple_of(i * tile, tile), tile)
        values = x[rows, :].astype(F32)
        centered = values - jnp.mean(values, axis=1, keepdims=True)
        scale = lax.rsqrt(jnp.mean(centered * centered, axis=1, keepdims=True) + EPS)
        own[rows, :] = (
            centered * scale * gain[...].astype(F32) + shift[...].astype(F32)
        ).astype(BF16)

    stores[3].start()
    for copy in loads:
        copy.wait()
    for copy in spread[0]:
        copy.start()
    for copy in stores[:3]:
        copy.start()
    stores[3].wait()
    start("n1_low", "n1_high")

    lane = lax.broadcasted_iota(jnp.int32, (1, 128), 1) % HEAD_DIM
    position = lax.broadcasted_iota(jnp.int32, cos.shape, 0).astype(F32)
    angle = position * frequency[...]
    sine = jnp.sin(angle)
    cos[...] = jnp.where(lane < ROT, jnp.cos(angle), 1.0)
    low[...] = jnp.where(lane < ROT // 2, -sine, 0.0)
    high[...] = jnp.where(jnp.logical_and(lane >= ROT // 2, lane < ROT), sine, 0.0)
    for ref, (begin, size) in zip(biases, columns):
        bias[:, begin : begin + size] = ref[...].astype(F32)

    for copy in stores[:3]:
        copy.wait()
    start("g_own")
    for copy in spread[1]:
        copy.start()
    finish("n1_low")
    start("n2_low", "e2_low")
    finish("n1_high")
    start("n2_high", "e2_high")
    finish("n2_low")
    start("n3_low", "e1_low")
    for copy in spread[0]:
        copy.wait()
    fetch = [
        pltpu.make_async_copy(
            first_full.at[d], w.at[pl.ds(d * first_full.shape[1], first_full.shape[1])], local.at[d]
        )
        for d in range(groups)
    ]
    for copy in fetch:
        copy.start()
    for copy in fetch:
        copy.wait()

    outs = (q, k, v, active, hidden)

    def results(i):
        part = jnp.where(lax.rem(i, 2) == 0, core, 1 - core)
        slot = 3 - lax.div(i, 2)
        rows = pl.ds(pl.multiple_of((2 * slot + part) * share, share), share)
        return [
            pltpu.make_async_copy(src.at[lax.rem(i, 2)], dst.at[rows], out_sem.at[lax.rem(i, 2), n])
            for n, (src, dst) in enumerate(zip(staged, outs))
        ]

    @pl.loop(0, 8)
    def _(i):
        @pl.when(i == 2)
        def _():
            finish("n2_high")
            start("n3_high", "e1_high")
            finish("e2_low", "e2_high")

        @pl.when(i == 4)
        def _():
            finish("e1_low", "e1_high")

        @pl.when(i == 6)
        def _():
            finish("n3_low")
            start("e0_low")
            finish("n3_high")
            start("e0_high")
            finish("g_own")
            start("g1")

        @pl.when(i == 7)
        def _():
            finish("e0_low", "e0_high")

        part = jnp.where(lax.rem(i, 2) == 0, core, 1 - core)
        load = pltpu.make_async_copy(rows_full.at[3 - lax.div(i, 2), part], x_tile, x_sem)
        load.start()

        @pl.when(i >= 2)
        def _():
            for copy in results(i - 2):
                copy.wait()

        load.wait()
        here = pl.ds(pl.multiple_of(part * share, share), share)
        project_tile(
            width,
            x_tile,
            w,
            bias,
            cos.at[here],
            low.at[here],
            high.at[here],
            *(r.at[lax.rem(i, 2)] for r in staged),
        )
        for copy in results(i):
            copy.start()

    for i in (6, 7):
        for copy in results(i):
            copy.wait()
    finish("g1")
    for copy in spread[1]:
        copy.wait()


OPENING_PLANS = (2, 3, 2, 2, 2, 2, 1, 1, 1, 1, 1, 1, 1, 2)


def opening(ident, x, gain, shift, g, weights, biases, groups, length, cut, tile=64):
    rows, depth = x.shape
    width, units = weights[0].shape[1], weights[3].shape[1]
    total = 3 * width + units
    inner = width + units
    columns = weights[4].shape[1]
    everything = 8 * rows
    whole = pl.BlockSpec(memory_space=pltpu.VMEM)
    full = jax.ShapeDtypeStruct((4, 2, rows, depth), BF16)
    exponent = np.arange(ROT // 2, dtype=np.float32) * np.float32(2.0 / ROT)
    frequency = np.tile(np.power(np.float32(10000.0), -exponent), 8)[None, :]
    table = jax.ShapeDtypeStruct((length, 128), F32)
    narrow = jax.ShapeDtypeStruct((everything, width), BF16)
    return pl.pallas_call(
        functools.partial(opening_kernel, tile, groups, width, cut),
        in_specs=[whole] * 3 + [ANYWHERE] * 7 + [whole] * 5,
        out_specs=[ANYWHERE] * 9 + [whole] * 3,
        out_shape=[
            full,
            full,
            jax.ShapeDtypeStruct((groups, depth // groups, total), BF16),
            jax.ShapeDtypeStruct((inner, groups * columns), BF16),
            narrow,
            narrow,
            narrow,
            jax.ShapeDtypeStruct((everything, units), BF16),
            jax.ShapeDtypeStruct((everything, units), F32),
            table,
            table,
            table,
        ],
        scratch_shapes=[
            pltpu.VMEM((rows, depth), BF16),
            pltpu.VMEM((rows, depth), BF16),
            pltpu.VMEM((depth // groups, total), BF16),
            pltpu.VMEM((inner, columns), BF16),
            pltpu.VMEM((depth, total), BF16),
            pltpu.VMEM((1, total), F32),
            pltpu.VMEM((rows, depth), BF16),
            pltpu.VMEM((2, rows, width), BF16),
            pltpu.VMEM((2, rows, width), BF16),
            pltpu.VMEM((2, rows, width), BF16),
            pltpu.VMEM((2, rows, units), BF16),
            pltpu.VMEM((2, rows, units), F32),
            pltpu.SemaphoreType.DMA((8,)),
            pltpu.SemaphoreType.DMA,
            pltpu.SemaphoreType.DMA((2, 5)),
            pltpu.SemaphoreType.DMA((2, groups - 1)),
            pltpu.SemaphoreType.DMA((2, groups - 1)),
        ]
        + [pltpu.SemaphoreType.DMA((n,)) for n in OPENING_PLANS for _ in range(2)],
        compiler_params=pltpu.CompilerParams(
            vmem_limit_bytes=VMEM_BYTES, collective_id=ident, has_side_effects=True
        ),
        cost_estimate=cost(2 * everything * depth * total, 60 * rows * depth),
        name="opening",
    )(x, gain, shift, g, *weights, *biases, jnp.asarray(frequency))


def project_tile(width, x, w, bias, cos, low, high, q, k, v, active, hidden):
    rows = x[...]
    tables = (cos[...], low[...], high[...])
    q[...] = (
        rotated(nn(rows, w[:, :width]) + bias[:, :width], *tables).astype(BF16)
        * jnp.asarray(HEAD_DIM**-0.5, BF16)
    )
    k[...] = rotated(
        nn(rows, w[:, width : 2 * width]) + bias[:, width : 2 * width], *tables
    ).astype(BF16)
    v[...] = (nn(rows, w[:, 2 * width : 3 * width]) + bias[:, 2 * width : 3 * width]).astype(BF16)
    units = hidden.shape[1]
    step = min(256, units)
    for start in range(0, units, step):
        at = slice(3 * width + start, 3 * width + start + step)
        h = nn(rows, w[:, at]) + bias[:, at]
        hidden[:, start : start + step] = h
        active[:, start : start + step] = gelu(h).astype(BF16)


def project(x, w, bias, tables, width, units, length, riding=(), ident=None, tile=512):
    rows, depth = x.shape
    per = length // tile
    row = lambda n: pl.BlockSpec((tile, n), lambda i: (i, 0))
    table = pl.BlockSpec((tile, 128), lambda i: (i % per, 0))
    total = 3 * width + units
    return launch(
        functools.partial(project_tile, width),
        [x, w, bias, *tables],
        [
            row(depth),
            once((depth, total), lambda i: (0, 0)),
            once((1, total), lambda i: (0, 0)),
            table,
            table,
            table,
        ],
        [row(width), row(width), row(width), row(units), row(units)],
        [jax.ShapeDtypeStruct((rows, width), BF16)] * 3
        + [jax.ShapeDtypeStruct((rows, units), BF16), jax.ShapeDtypeStruct((rows, units), F32)],
        rows // tile,
        "project",
        cost(2 * rows * depth * total, 2 * depth * (rows + total) + rows * units * 6),
        riding=riding,
        ident=ident,
    )


def each_tile_kernel(body, *refs):
    body(*refs)


def each_tile(body, arrays, w, depth, name, tile=512):
    rows = arrays[0].shape[0]
    return pl.pallas_call(
        functools.partial(each_tile_kernel, body),
        grid=(rows // tile,),
        in_specs=[pl.BlockSpec((tile, a.shape[1]), lambda i: (i, 0)) for a in arrays]
        + [once(w.shape, lambda i, n=len(w.shape): (0,) * n)],
        out_specs=pl.BlockSpec((tile, depth), lambda i: (i, 0)),
        out_shape=jax.ShapeDtypeStruct((rows, depth), BF16),
        compiler_params=params(("arbitrary",)),
        cost_estimate=cost(2 * w.size * rows, 2 * rows * depth),
        name=name,
    )(*arrays, w)


def core_sum_body(body, count, pieces, n_in, at, *refs):
    ins, w, outs = refs[:n_in], refs[n_in], refs[n_in + 1 : n_in + 1 + count]
    sent, got, value, send_sem, got_sem = refs[n_in + 1 + count :]
    slot = pl.program_id(0)
    core = at["core"]
    share = sent.shape[1]
    piece = share // pieces

    def term(owner, i, to):
        rows = pl.ds(pl.multiple_of(owner * share + i * piece, piece), piece)
        body(*(r.at[rows, :] for r in ins), w, to)

    def copy(i):
        rows = pl.ds(i * piece, piece)
        return to_device(
            sent.at[slot, rows],
            got.at[slot, rows],
            send_sem.at[slot, i],
            got_sem.at[slot, i],
            {"tensor": at["partner"]},
        )

    for i in range(pieces):
        term(1 - core, i, sent.at[slot, pl.ds(i * piece, piece)])
        copy(i).start()
    for i in range(pieces):
        rows = pl.ds(i * piece, piece)
        term(core, i, value)
        copy(i).wait_recv()
        for n, out in enumerate(outs):

            @pl.when(slot == n)
            def _(out=out):
                out[rows, :] = (value[...] + got[slot, rows].astype(F32)).astype(BF16)

    for i in range(pieces):
        copy(i).wait_send()


def core_sum_parts(count, pieces, length, depth):
    share = length // 2
    out = pl.BlockSpec((share, depth), lambda i: (0, 0), pipeline_mode=pl.Buffered(1))
    return (
        [out] * count,
        [jax.ShapeDtypeStruct((share, depth), BF16)] * count,
        [
            pltpu.VMEM((count, share, depth), BF16),
            pltpu.VMEM((count, share, depth), BF16),
            pltpu.VMEM((share // pieces, depth), F32),
            pltpu.SemaphoreType.DMA((count, pieces)),
            pltpu.SemaphoreType.DMA((count, pieces)),
        ],
    )


def core_sum(body, ident, count, length, arrays, w, depth, name, pieces=2, riding=()):
    outs, shapes, scratch = core_sum_parts(count, pieces, length, depth)
    size = sum(a.shape[1] for a, _ in arrays)
    return launch(
        functools.partial(core_sum_body, body, count, pieces, len(arrays)),
        [a for a, _ in arrays],
        [pl.BlockSpec((length, a.shape[1]), lambda i, f=f: (f + i, 0)) for a, f in arrays],
        outs,
        shapes,
        count,
        name,
        cost(2 * count * length * size * depth, 2 * count * length * (size + depth) + 2 * size * depth),
        scratch=scratch,
        riding=riding,
        ident=ident,
        place=True,
        lazy=[w],
    )


def mix_body(attended, active, w, out):
    width, depth = attended.shape[1], w.shape[1]
    step = min(512, depth)
    for start in range(0, depth, step):
        at = slice(start, start + step)
        out[:, at] = (nn(attended[...], w[:width, at]) + nn(active[...], w[width:, at])).astype(
            out.dtype
        )


def unproject_body(qkv_grad, hidden_grad, w, out):
    three = qkv_grad.shape[1]
    depth = w.shape[0]
    step = min(512, depth)
    for start in range(0, depth, step):
        out[:, start : start + step] = (
            nt(qkv_grad[...], w[start : start + step, :three])
            + nt(hidden_grad[...], w[start : start + step, three:])
        ).astype(out.dtype)


def unmix_tile(hidden, g, w, attended_grad, hidden_grad, sums):
    width = attended_grad.shape[1]
    units = hidden.shape[1]

    @pl.when(pl.program_id(0) == 0)
    def _():
        sums[...] = jnp.zeros_like(sums)

    rows = g[...]
    attended_grad[...] = nt(rows, w[:width, :]).astype(BF16)
    step = min(256, units)
    for start in range(0, units, step):
        at = slice(start, start + step)
        back = nt(rows, w[width + start : width + start + step, :])
        low = (back * gelu_slope(hidden[:, at])).astype(BF16)
        hidden_grad[:, at] = low
        sums[:, at] += jnp.sum(low.astype(F32), axis=0, keepdims=True)


def unmix(g, w, hidden, width, first, count, length, riding=(), ident=None, tile=512):
    rows = count * length
    units = hidden.shape[1]
    inner, depth = w.shape
    per = length // tile
    row = lambda n: pl.BlockSpec((tile, n), lambda i: (i, 0))
    late = lambda n: pl.BlockSpec((tile, n), lambda i: (first * per + i, 0))
    seen = []
    if g is None:
        seen = [
            (0, pl.BlockSpec((None, None, tile, depth), lambda i: (first + i // 2, i % 2, 0, 0)))
        ]
    return launch(
        unmix_tile,
        [hidden] + ([] if g is None else [g]),
        [late(units)] + ([] if g is None else [late(depth)]),
        [row(width), row(units), pl.BlockSpec((1, units), lambda i: (0, 0))],
        [
            jax.ShapeDtypeStruct((rows, width), BF16),
            jax.ShapeDtypeStruct((rows, units), BF16),
            jax.ShapeDtypeStruct((1, units), F32),
        ],
        rows // tile,
        "unmix",
        cost(2 * rows * inner * depth, 2 * depth * (rows + inner) + rows * units * 6),
        riding=riding,
        ident=ident,
        lazy=[w],
        seen=seen,
    )


def outer_rows_kernel(ready, x, *refs):
    parts, out = refs[:-1], refs[-1]
    total, start = None, 0
    for n, part in enumerate(parts):
        ready(n)
        term = tn(x[start : start + part.shape[0], :], part[...])
        total = term if total is None else total + term
        start += part.shape[0]
    out[...] = total.astype(out.dtype)


def outer_rows(x, parts, riding=(), ident=None, tile=256, wait_for=()):
    rows, depth = x.shape
    n = parts[0].shape[1]
    return launch(
        outer_rows_kernel,
        [x],
        [pl.BlockSpec((rows, tile), lambda i: (0, i))],
        [pl.BlockSpec((tile, n), lambda i: (i, 0))],
        [jax.ShapeDtypeStruct((depth, n), BF16)],
        depth // tile,
        "outer_rows",
        cost(2 * rows * depth * n, 2 * (rows * (depth + n) + depth * n)),
        riding=riding,
        ident=ident,
        wait_for=wait_for,
        lazy=parts,
        in_turn=True,
    )


def outer_columns_kernel(ready, g, *refs):
    many, b, out = refs[:-2], refs[-2], refs[-1]
    width = many[0].shape[1]
    total, start = None, 0
    for n, a in enumerate(many):
        ready(n)
        term = tn(a[...], g[start : start + a.shape[0], :])
        total = term if total is None else total + term
        start += a.shape[0]
    out[0, :width, :] = total.astype(out.dtype)
    ready(len(many))
    out[0, width:, :] = tn(b[...], g[...]).astype(out.dtype)


def outer_columns(many, b, g, parts, riding=(), ident=None, tile=512):
    rows, depth = g.shape
    width, units = many[0].shape[1], b.shape[1]
    across = depth // parts
    tile = min(tile, across)
    per = across // tile
    return launch(
        outer_columns_kernel,
        [g],
        [pl.BlockSpec((rows, tile), lambda i: (0, i))],
        [pl.BlockSpec((1, width + units, tile), lambda i: (i // per, 0, i % per))],
        [jax.ShapeDtypeStruct((parts, width + units, across), BF16)],
        depth // tile,
        "outer_columns",
        cost(2 * rows * depth * (width + units), 2 * (rows * (depth + width + units) + depth * (width + units))),
        riding=riding,
        ident=ident,
        lazy=list(many) + [b],
        in_turn=True,
    )


def head_lanes(width, head):
    return lax.broadcasted_iota(jnp.int32, (1, width), 1) // HEAD_DIM == head


def attend_kernel(q, k, v, column_ids, row_ids, out, log_sums):
    length, width = q.shape
    heads = width // HEAD_DIM
    tile = min(SPAN, length)
    lanes = lax.broadcasted_iota(jnp.int32, (1, 128), 1)
    for begin in range(0, length, tile):
        end = min(length, begin + tile + SPAN)
        q_ids = column_ids[begin : begin + tile, :]
        blocked = row_ids[:, begin:end] > q_ids
        rows = q[begin : begin + tile, :]

        def one_head(head, carry):
            total, sums = carry
            mine = head_lanes(width, head)
            scores = nt(jnp.where(mine, rows, jnp.zeros_like(rows)), k[:end, :])
            tail = jnp.where(blocked, -1e9, scores[:, begin:])
            scores = jnp.concatenate([scores[:, :begin], tail], axis=1) if begin else tail
            highest = jnp.max(scores, axis=1, keepdims=True)
            powers = jnp.exp(scores - highest)
            amount = jnp.sum(powers, axis=1, keepdims=True)
            low = (powers * (1.0 / amount)).astype(BF16)
            total = jnp.where(mine, nn(low, v[:end, :]), total)
            sums = jnp.where(lanes == head, highest + jnp.log(amount), sums)
            return total, sums

        total, sums = jnp.zeros((tile, width), F32), jnp.zeros((tile, 128), F32)
        for head in range(heads):
            total, sums = one_head(head, (total, sums))
        out[begin : begin + tile, :] = total.astype(BF16)
        log_sums[:, begin : begin + tile] = sums.T[:8, :]


def attend(first, count, q, k, v, column_ids, row_ids, riding=(), ident=None):
    width = q.shape[1]
    length = row_ids.shape[2]
    rows, seqs = count * length, count
    heads = width // HEAD_DIM
    seq = pl.BlockSpec((length, width), lambda s: (first + s, 0))
    out = pl.BlockSpec((length, width), lambda s: (s, 0))
    return launch(
        attend_kernel,
        [q, k, v, column_ids, row_ids],
        [
            seq,
            seq,
            seq,
            pl.BlockSpec((length, 1), lambda s: (first + s, 0)),
            pl.BlockSpec((None, 1, length), lambda s: (first + s, 0, 0)),
        ],
        [out, pl.BlockSpec((8, length), lambda s: (0, s))],
        [jax.ShapeDtypeStruct((rows, width), BF16), jax.ShapeDtypeStruct((8, rows), F32)],
        seqs,
        "attend",
        cost(8 * seqs * heads * length * length * 256 * 0.8, 8 * rows * width, seqs * heads * length**2),
        riding=riding,
        ident=ident,
    )


def unattend_kernel(
    q, k, v, g, log_sums, column_ids, row_ids, cos, low, high, out, sums, key_total, value_total
):
    length, width = q.shape
    heads = width // HEAD_DIM
    tile = min(SPAN, length)
    tables = (cos[...], -low[...], -high[...])

    @pl.when(pl.program_id(0) == 0)
    def _():
        sums[...] = jnp.zeros_like(sums)

    key_total[...] = jnp.zeros_like(key_total)
    value_total[...] = jnp.zeros_like(value_total)

    def products(begin, head):
        end, at = min(length, begin + tile + SPAN), slice(begin, begin + tile)
        mine = head_lanes(width, head)
        q_rows, g_rows = q[at, :], g[at, :]
        q_head = jnp.where(mine, q_rows, jnp.zeros_like(q_rows))
        g_head = jnp.where(mine, g_rows, jnp.zeros_like(g_rows))
        return q_head, g_head, nt(k[:end, :], q_head), nt(v[:end, :], g_head)

    steps = [(begin, head) for begin in range(0, length, tile) for head in range(heads)]
    ahead = products(*steps[0])
    query_total = None
    for n, (begin, head) in enumerate(steps):
        q_head, g_head, scores, prob_grad = ahead
        if n + 1 < len(steps):
            ahead = products(*steps[n + 1])
        end, at = min(length, begin + tile + SPAN), slice(begin, begin + tile)
        blocked = column_ids[begin:end, :] > row_ids[:, at]
        tail = jnp.where(blocked, -1e9, scores[begin:, :])
        scores = jnp.concatenate([scores[:begin, :], tail], axis=0) if begin else tail
        probs = jnp.exp(scores - log_sums[head : head + 1, at])
        value_total[:end, :] += nn(probs.astype(BF16), g_head)
        inner = jnp.sum(prob_grad * probs, axis=0, keepdims=True)
        score_grad = (probs * (prob_grad - inner)).astype(BF16)
        key_total[:end, :] += nn(score_grad, q_head)
        part = tn(score_grad, k[:end, :])
        query_total = jnp.where(
            head_lanes(width, head), part, query_total if head else jnp.zeros_like(part)
        )
        if head == heads - 1:
            turned = rotated(query_total * HEAD_DIM**-0.5, *(t[at, :] for t in tables)).astype(BF16)
            out[at, :width] = turned
            sums[:, :width] += jnp.sum(turned.astype(F32), axis=0, keepdims=True)
    turned = rotated(key_total[...], *tables).astype(BF16)
    out[:, width : 2 * width] = turned
    sums[:, width : 2 * width] += jnp.sum(turned.astype(F32), axis=0, keepdims=True)
    turned = value_total[...].astype(BF16)
    out[:, 2 * width :] = turned
    sums[:, 2 * width :] += jnp.sum(turned.astype(F32), axis=0, keepdims=True)


def unattend(first, count, q, k, v, g, g_first, log_sums, sums_first, column_ids, row_ids, tables, riding=(), ident=None, wait_for=()):
    width = q.shape[1]
    length = row_ids.shape[2]
    rows, seqs = count * length, count
    heads = width // HEAD_DIM
    seq = pl.BlockSpec((length, width), lambda s: (first + s, 0))
    table = once((length, 128), lambda s: (0, 0))
    return launch(
        unattend_kernel,
        [q, k, v, g, log_sums, column_ids, row_ids, *tables],
        [
            seq,
            seq,
            seq,
            pl.BlockSpec((length, width), lambda s: (g_first + s, 0)),
            pl.BlockSpec((8, length), lambda s: (0, sums_first + s)),
            pl.BlockSpec((length, 1), lambda s: (first + s, 0)),
            pl.BlockSpec((None, 1, length), lambda s: (first + s, 0, 0)),
            table,
            table,
            table,
        ],
        [
            pl.BlockSpec((length, 3 * width), lambda s: (s, 0)),
            pl.BlockSpec((1, 3 * width), lambda s: (0, 0)),
        ],
        [jax.ShapeDtypeStruct((rows, 3 * width), BF16), jax.ShapeDtypeStruct((1, 3 * width), F32)],
        count,
        "unattend",
        cost(20 * seqs * heads * length * length * 256 * 0.8, 14 * rows * width, seqs * heads * length**2),
        scratch=[pltpu.VMEM((length, width), F32), pltpu.VMEM((length, width), F32)],
        riding=riding,
        ident=ident,
        wait_for=wait_for,
    )


def attend_mix_body(count, pieces, at, q, k, v, column_ids, row_ids, active, w, out, log_sums, *refs):
    attend_kernel(q, k, v, column_ids, row_ids, out, log_sums)
    core_sum_body(mix_body, count, pieces, 2, at, out, active, w, *refs)


def attend_mix(first, count, q, k, v, column_ids, row_ids, active, w, riding, ident, pieces=2):
    width, units = q.shape[1], active.shape[1]
    length = row_ids.shape[2]
    depth = w.shape[1]
    rows, heads = count * length, width // HEAD_DIM
    here = lambda n: pl.BlockSpec((length, n), lambda s: (first + s, 0))
    outs, shapes, scratch = core_sum_parts(count, pieces, length, depth)
    return launch(
        functools.partial(attend_mix_body, count, pieces),
        [q, k, v, column_ids, row_ids, active],
        [
            here(width),
            here(width),
            here(width),
            here(1),
            pl.BlockSpec((None, 1, length), lambda s: (first + s, 0, 0)),
            here(units),
        ],
        [pl.BlockSpec((length, width), lambda s: (s, 0)), pl.BlockSpec((8, length), lambda s: (0, s))]
        + outs,
        [jax.ShapeDtypeStruct((rows, width), BF16), jax.ShapeDtypeStruct((8, rows), F32)] + shapes,
        count,
        "attend_mix",
        cost(8 * rows * heads * length * 256 * 0.8, 8 * rows * width, rows * heads * length),
        scratch=scratch,
        riding=riding,
        ident=ident,
        place=True,
        lazy=[w],
    )


def unattend_unproject_body(pieces, at, *refs):
    operands, hidden_grad, w, (out, sums, part), scratch = (
        refs[:10],
        refs[10],
        refs[11],
        refs[12:15],
        refs[15:],
    )
    unattend_kernel(*operands, out, sums, *scratch[:2])
    core_sum_body(unproject_body, 1, pieces, 2, at, out, hidden_grad, w, part, *scratch[2:])


def unattend_unproject(
    at, q, k, v, g, g_at, log_sums, sums_at, column_ids, row_ids, tables, hidden_grad, hidden_at, w, riding, ident, pieces=2
):
    width, units = q.shape[1], hidden_grad.shape[1]
    length = row_ids.shape[2]
    depth = w.shape[0]
    heads = width // HEAD_DIM
    here = lambda n, at: pl.BlockSpec((length, n), lambda s: (at, 0))
    table = pl.BlockSpec((length, 128), lambda s: (0, 0))
    outs, shapes, scratch = core_sum_parts(1, pieces, length, depth)
    return launch(
        functools.partial(unattend_unproject_body, pieces),
        [q, k, v, g, log_sums, column_ids, row_ids, *tables, hidden_grad],
        [
            here(width, at),
            here(width, at),
            here(width, at),
            here(width, g_at),
            pl.BlockSpec((8, length), lambda s: (0, sums_at)),
            here(1, at),
            pl.BlockSpec((None, 1, length), lambda s: (at, 0, 0)),
            table,
            table,
            table,
            here(units, hidden_at),
        ],
        [
            pl.BlockSpec((length, 3 * width), lambda s: (0, 0)),
            pl.BlockSpec((1, 3 * width), lambda s: (0, 0)),
        ]
        + outs,
        [
            jax.ShapeDtypeStruct((length, 3 * width), BF16),
            jax.ShapeDtypeStruct((1, 3 * width), F32),
        ]
        + shapes,
        1,
        "unattend_unproject",
        cost(20 * heads * length * length * 256 * 0.8, 14 * length * width, heads * length**2),
        scratch=[pltpu.VMEM((length, width), F32), pltpu.VMEM((length, width), F32)] + scratch,
        riding=riding,
        ident=ident,
        place=True,
        lazy=[w],
    )


def nothing():
    pass


def add_up(*parts):
    total = parts[0].astype(F32)
    for part in parts[1:]:
        total = total + part.astype(F32)
    return total.astype(BF16)


def after(values, *others):
    return lax.optimization_barrier((values,) + others)[0]


def sum_everywhere_kernel(groups, members, gain, shift, bias, qkv, up, wide, narrow, buf, in_dp, in_tensor, send_dp, got_dp, send_tensor, got_tensor):
    dp, tensor = lax.axis_index("dp"), lax.axis_index("tensor")
    mesh = pl.DeviceIdType.MESH
    barrier = pltpu.get_barrier_semaphore()
    for step in range(1, groups):
        pl.semaphore_signal(barrier, inc=1, device_id={"dp": lax.rem(dp + step, groups)}, device_id_type=mesh)
    for step in range(1, members):
        pl.semaphore_signal(barrier, inc=1, device_id={"tensor": lax.rem(tensor + step, members)}, device_id_type=mesh)
    pl.semaphore_wait(barrier, groups + members - 2)
    lanes = buf.shape[2] // 4
    for k, ref in enumerate((gain, shift, bias)):
        for r in range(8):
            buf[0, r : r + 1, k * lanes : (k + 1) * lanes] = ref[:, r * lanes : (r + 1) * lanes]
    row = 0
    buf[0, :, 3 * lanes :] = jnp.zeros((8, lanes), F32)
    for ref in (qkv, up):
        for start in range(0, ref.shape[1], lanes):
            buf[0, row : row + 1, 3 * lanes :] = ref[:, start : start + lanes]
            row += 1

    def exchange(axis, me, size, source, into, send, got):
        copies = []
        for step in range(1, size):
            copies.append(
                pltpu.make_async_remote_copy(
                    src_ref=source,
                    dst_ref=into.at[step - 1],
                    send_sem=send.at[step - 1],
                    recv_sem=got.at[step - 1],
                    device_id={axis: lax.rem(me + step, size)},
                    device_id_type=mesh,
                )
            )
        for copy in copies:
            copy.start()
        for copy in copies:
            copy.wait()

    exchange("dp", dp, groups, buf.at[0], in_dp, send_dp, got_dp)
    total = buf[0]
    for step in range(groups - 1):
        total = total + in_dp[step]
    row = 0
    for start in range(0, narrow.shape[1], lanes):
        narrow[:, start : start + lanes] = total[row : row + 1, 3 * lanes :]
        row += 1
    buf[1] = total
    exchange("tensor", tensor, members, buf.at[1], in_tensor, send_tensor, got_tensor)
    total = buf[1]
    for step in range(members - 1):
        total = total + in_tensor[step]
    for k in range(3):
        for r in range(8):
            wide[k : k + 1, r * lanes : (r + 1) * lanes] = total[r : r + 1, k * lanes : (k + 1) * lanes]


def sum_everywhere(ident, groups, members, gain, shift, bias, qkv, up):
    depth = gain.shape[1]
    whole = pl.BlockSpec(memory_space=pltpu.VMEM)
    return pl.pallas_call(
        functools.partial(sum_everywhere_kernel, groups, members),
        in_specs=[whole] * 5,
        out_specs=[whole] * 2,
        out_shape=[
            jax.ShapeDtypeStruct((8, depth), F32),
            jax.ShapeDtypeStruct((1, qkv.shape[1] + up.shape[1]), F32),
        ],
        scratch_shapes=[
            pltpu.VMEM((2, 8, depth // 2), F32),
            pltpu.VMEM((groups - 1, 8, depth // 2), F32),
            pltpu.VMEM((members - 1, 8, depth // 2), F32),
            pltpu.SemaphoreType.DMA((groups - 1,)),
            pltpu.SemaphoreType.DMA((groups - 1,)),
            pltpu.SemaphoreType.DMA((members - 1,)),
            pltpu.SemaphoreType.DMA((members - 1,)),
        ],
        compiler_params=pltpu.CompilerParams(collective_id=ident, has_side_effects=True),
        name="sum_everywhere",
    )(gain, shift, bias, qkv, up)


def per_device(
    inputs,
    block_ids,
    norm_gain,
    norm_bias,
    query_weight,
    query_bias,
    key_weight,
    key_bias,
    value_weight,
    value_bias,
    out_weight,
    out_bias,
    up_weight,
    up_bias,
    down_weight,
    down_bias,
    grad_out,
):
    seqs, length = block_ids.shape
    share, depth = inputs.shape
    width = query_weight.shape[1]
    units = up_weight.shape[1]
    groups, members = lax.axis_size("dp"), lax.axis_size("tensor")
    gain, shift = norm_gain.astype(F32)[None, :], norm_bias.astype(F32)[None, :]
    paired = groups == 4 and members == 8 and seqs == 4 and 2 * share == length
    me = lax.axis_index("tensor")
    if paired:
        chip = me // 2
        order = jnp.arange(3, -1, -1, dtype=jnp.int32) ^ chip
        inner = ((chip == 1) | (chip == 2)).astype(jnp.int32)
    else:
        order = jnp.arange(seqs, dtype=jnp.int32)

    ids = block_ids[order]
    column_ids = ids.reshape(seqs * length, 1)
    row_ids = ids.reshape(seqs, 1, length)
    pair = seqs // 2
    everything = seqs * length
    idents = iter(range(1, 100))

    if paired:
        kept = lambda values: jnp.where(inner == 1, values, jnp.zeros_like(values))
        cuts = lambda fraction: int(share * fraction) // 32 * 32
        g1 = cuts(0.25)
        rows, full, first_full, second_full, q, k, v, active, hidden, *tables = opening(
            next(idents),
            inputs,
            norm_gain[None, :],
            norm_bias[None, :],
            grad_out,
            [query_weight, key_weight, value_weight, up_weight, out_weight, down_weight],
            [b[None, :] for b in (query_bias, key_bias, value_bias, up_bias)],
            groups,
            length,
            g1,
        )
        rows = rows.reshape(everything, depth)
        first_full = first_full.reshape(depth, 3 * width + units)

        def unheads(at, count, g, g_at, sums, sums_at, riding, wait_for=()):
            return unattend(
                at,
                count,
                q,
                k,
                v,
                g,
                g_at,
                sums,
                sums_at,
                column_ids,
                row_ids,
                tables,
                riding=riding,
                ident=next(idents),
                wait_for=wait_for,
            )

        def unprojected(count, grads, riding):
            return core_sum(
                unproject_body,
                next(idents),
                count,
                length,
                grads,
                first_full,
                depth,
                "unproject",
                riding=riding,
            )

        def forward(at, riding):
            return attend_mix(
                at, pair, q, k, v, column_ids, row_ids, active, second_full, riding, next(idents)
            )

        far_attended, far_sums, *far, full = forward(0, [gathering(full, (1, g1, share))])

        near_attended, near_sums, *near, full, end = forward(
            pair,
            [gathering(full, (2, 0, share), ("first", 0, share)), sending(far[0], "in", 0, share)],
        )

        crossing = add_up(far[1], end)
        part = cuts(0.44)
        near_attended_grad, near_hidden_grad, near_up_sum, full, end, middle = unmix(
            None,
            second_full,
            hidden,
            width,
            pair,
            pair,
            length,
            riding=[
                gathering(full, (3, 0, part), ("second", 0, share)),
                sending(far[1], "in", 0, part),
                sending(crossing, "middle", 0, part),
            ],
            ident=next(idents),
        )
        near_grad, near_sum, full, end, middle = unheads(
            pair,
            pair,
            near_attended_grad,
            0,
            near_sums,
            0,
            [
                gathering(
                    full, (3, part, share), ("third", 0, part), late=[("third", part, share)]
                ),
                sending(far[1], "in", part, share, end),
                sending(crossing, "middle", part, share, middle),
            ],
        )
        upstream = full.reshape(everything, depth)

        to_side = add_up(near[0], kept(middle))
        to_middle = add_up(far[0], end)
        mine = near[1]
        part = cuts(0.4)

        def outward(lo, hi, side=None, middle=None):
            return [sending(to_side, "side", lo, hi, side), sending(to_middle, "middle", lo, hi, middle)]

        far_attended_grad, far_hidden_grad, far_up_sum, side, middle = unmix(
            upstream,
            second_full,
            hidden,
            width,
            0,
            pair,
            length,
            riding=outward(0, part),
            ident=next(idents),
        )
        up_sum = near_up_sum + far_up_sum

        def backward(at, riding, wait_for=()):
            return unattend_unproject(
                at,
                q,
                k,
                v,
                far_attended_grad,
                at,
                far_sums,
                at,
                column_ids,
                row_ids,
                tables,
                far_hidden_grad,
                at,
                first_full,
                riding + [Riding([a], [], False, 1, lambda *_: []) for a in wait_for],
                next(idents),
            )

        grads_0, sum_0, far_0, side, middle = backward(0, outward(part, share, side, middle))
        output_terms = [mine, side, middle]

        part = cuts(0.45)
        up_part, end = outer_rows(
            rows,
            [far_hidden_grad, near_hidden_grad],
            riding=[sending(far_0, "in", 0, part)],
            ident=next(idents),
        )
        up_grad = lax.psum_scatter(up_part, "dp", scatter_dimension=0, tiled=True)
        grads_1, sum_1, far_1, end = backward(
            1, [sending(far_0, "in", part, share, end)], [up_part]
        )
    else:
        tables = rotary_tables(length)
        first = jnp.concatenate([query_weight, key_weight, value_weight, up_weight], axis=1)
        second = jnp.concatenate([out_weight, down_weight], axis=0)
        bias = jnp.concatenate([query_bias, key_bias, value_bias, up_bias]).astype(F32)[None, :]
        first_full = lax.all_gather(first, "dp", axis=0, tiled=True)
        second_full = lax.all_gather(second, "dp", axis=1, tiled=True)
        rows = lax.all_gather(norm(inputs, gain, shift), "tensor", axis=0, tiled=True)
        upstream = lax.all_gather(grad_out, "tensor", axis=0, tiled=True)
        q, k, v, active, hidden = project(rows, first_full, bias, tables, width, units, length)
        attended, log_sums = attend(0, seqs, q, k, v, column_ids, row_ids)
        whole = each_tile(mix_body, [attended, active], second_full, depth, "mix")
        output_terms = [lax.psum_scatter(whole, "tensor", scatter_dimension=0, tiled=True)]
        attended_grad, hidden_grad, up_sum = unmix(
            upstream, second_full, hidden, width, 0, seqs, length
        )
    if paired:
        crossing = add_up(far_1, end)
        part = cuts(0.58)
        second_part, end, middle = outer_columns(
            [far_attended, near_attended],
            active,
            upstream,
            groups,
            riding=[sending(far_1, "in", 0, part), sending(crossing, "middle", 0, part)],
            ident=next(idents),
        )
        second_grad = lax.psum_scatter(second_part, "dp", scatter_dimension=0)
        *near, end, middle = unprojected(
            pair,
            [(near_grad, 0), (near_hidden_grad, 0)],
            [
                sending(far_1, "in", part, share, end),
                sending(crossing, "middle", part, share, middle),
            ],
        )
        qkv_sum = sum_0 + sum_1 + near_sum
        to_side = add_up(near[0], kept(middle))
        to_middle = add_up(far_0, end)
        part = cuts(0.44)
        first_part, side, middle = outer_rows(
            rows,
            [grads_0, grads_1, near_grad],
            riding=[sending(to_side, "side", 0, part), sending(to_middle, "middle", 0, part)],
            ident=next(idents),
            wait_for=[up_grad],
        )
        first_grad = lax.psum_scatter(first_part, "dp", scatter_dimension=0, tiled=True)
        side, middle = launch(
            nothing,
            [],
            [],
            [],
            [],
            1,
            "finish",
            cost(1e9, 1e6),
            riding=[
                sending(to_side, "side", part, share, side),
                sending(to_middle, "middle", part, share, middle),
            ],
            ident=next(idents),
            wait_for=[first_part],
        )
        terms = [near[1], side, middle]
    else:
        inner = jnp.ones((), jnp.int32)
        qkv_grad, qkv_sum = unattend(
            0, seqs, q, k, v, attended_grad, 0, log_sums, 0, column_ids, row_ids, tables
        )
        whole = each_tile(unproject_body, [qkv_grad, hidden_grad], first_full, depth, "unproject")
        terms = [lax.psum_scatter(whole, "tensor", scatter_dimension=0, tiled=True)]
        (second_part,) = outer_columns([attended], active, upstream, groups)
        (first_part,) = outer_rows(rows, [qkv_grad])
        (up_part,) = outer_rows(rows, [hidden_grad])
        second_grad = lax.psum_scatter(second_part, "dp", scatter_dimension=0)
        first_grad = lax.psum_scatter(first_part, "dp", scatter_dimension=0, tiled=True)
        up_grad = lax.psum_scatter(up_part, "dp", scatter_dimension=0, tiled=True)

    first_grad = first_grad.astype(F32)
    input_grad, output, gain_part, shift_part, out_grad, down_grad, up_grad = closing(
        inner[None],
        inputs,
        grad_out,
        gain,
        out_bias[None, :],
        down_bias[None, :],
        second_grad,
        up_grad,
        width,
        terms,
        output_terms,
    )
    bias_part = jnp.sum(grad_out, axis=0, dtype=F32)[None, :]
    if paired and groups == 4:
        wide, narrow = sum_everywhere(
            next(idents), groups, members, gain_part, shift_part, bias_part, qkv_sum, up_sum
        )
        gain_grad, shift_grad, outer_bias_grad = wide[0], wide[1], wide[2]
        qkv_sum, up_sum = narrow[0, : 3 * width], narrow[0, 3 * width :]
    else:
        gain_grad, shift_grad, outer_bias_grad = lax.psum(
            (gain_part[0], shift_part[0], bias_part[0]), ("dp", "tensor")
        )
        qkv_sum, up_sum = lax.psum((qkv_sum[0], up_sum[0]), "dp")
    return (
        output,
        input_grad,
        gain_grad,
        shift_grad,
        first_grad[:, :width],
        qkv_sum[:width],
        first_grad[:, width : 2 * width],
        qkv_sum[width : 2 * width],
        first_grad[:, 2 * width :],
        qkv_sum[2 * width :],
        out_grad,
        outer_bias_grad,
        up_grad,
        up_sum,
        down_grad,
        outer_bias_grad,
    )


def solution(mesh):
    tokens = P(("dp", "tensor"), None)
    down = P("dp", "tensor")
    across = P("tensor", "dp")
    part = P("tensor")
    return jax.shard_map(
        per_device,
        mesh=mesh,
        in_specs=(
            tokens,
            P("dp", None),
            P(),
            P(),
            down,
            part,
            down,
            part,
            down,
            part,
            across,
            P(),
            down,
            part,
            across,
            P(),
            tokens,
        ),
        out_specs=(
            tokens,
            tokens,
            P(),
            P(),
            down,
            part,
            down,
            part,
            down,
            part,
            across,
            P(),
            down,
            part,
            across,
            P(),
        ),
        check_vma=False,
    )
```

```python
import functools

import jax
import jax.numpy as jnp
import numpy as np
from jax import lax
from jax.experimental import pallas as pl
from jax.experimental.pallas import tpu as pltpu
from jax.sharding import PartitionSpec as P

HEAD_DIM = 64
ROT = 32
SPAN = 256
EPS = 1e-05
F32 = jnp.float32
BF16 = jnp.bfloat16
VMEM_BYTES = 60 * 2**20


def nn(a, b):
    return jnp.dot(a, b, preferred_element_type=F32)


def nt(a, b):
    return lax.dot_general(a, b, (((1,), (1,)), ((), ())), preferred_element_type=F32)


def tn(a, b):
    return lax.dot_general(a, b, (((0,), (0,)), ((), ())), preferred_element_type=F32)


def params(semantics):
    return pltpu.CompilerParams(dimension_semantics=semantics, vmem_limit_bytes=VMEM_BYTES)


def cost(flops, bytes_accessed, transcendentals=0):
    return pl.CostEstimate(
        flops=int(flops) // 10,
        bytes_accessed=int(bytes_accessed) // 10,
        transcendentals=int(transcendentals) // 10,
    )


def once(shape, index_map):
    return pl.BlockSpec(shape, index_map, pipeline_mode=pl.Buffered(1))


def rotary_tables(length):
    halves = ROT // 2
    exponent = jnp.arange(halves, dtype=F32) * (2.0 / ROT)
    frequency = jnp.power(10000.0, -exponent)
    angles = jnp.arange(length, dtype=F32)[:, None] * frequency[None, :]
    cos, sin = jnp.cos(angles), jnp.sin(angles)
    zero = jnp.zeros((length, halves), F32)
    rest = HEAD_DIM - ROT
    head = lambda a, b, fill: jnp.concatenate([a, b, jnp.full((length, rest), fill, F32)], axis=1)
    return tuple(
        jnp.concatenate([t, t], axis=1)
        for t in (head(cos, cos, 1.0), head(-sin, zero, 0.0), head(zero, sin, 0.0))
    )


def rotated(values, cos, low, high):
    halves = ROT // 2
    pieces = []
    for start in range(0, values.shape[1], 128):
        u = values[:, start : start + 128]
        pieces.append(
            u * cos + pltpu.roll(u, 128 - halves, 1) * low + pltpu.roll(u, halves, 1) * high
        )
    return pieces[0] if len(pieces) == 1 else jnp.concatenate(pieces, axis=1)


GELU_A = 0.7978845608028654
GELU_B = 0.044715


def gelu(v):
    return 0.5 * v * (1.0 + jnp.tanh(GELU_A * (v + GELU_B * (v * v * v))))


def gelu_slope(v):
    square = v * v
    half = 0.5 + 0.5 * jnp.tanh(v * (GELU_A + GELU_A * GELU_B * square))
    return half + (half - half * half) * (v * (2.0 * GELU_A + 6.0 * GELU_A * GELU_B * square))


def norm_kernel(x, gain, shift, out):
    values = x[...].astype(F32)
    centered = values - jnp.mean(values, axis=1, keepdims=True)
    scale = lax.rsqrt(jnp.mean(centered * centered, axis=1, keepdims=True) + EPS)
    out[...] = (centered * scale * gain[...] + shift[...]).astype(BF16)


def norm(x, gain, shift, tile=128):
    rows, depth = x.shape
    row = pl.BlockSpec((tile, depth), lambda i: (i, 0))
    one = once((1, depth), lambda i: (0, 0))
    return pl.pallas_call(
        norm_kernel,
        grid=(rows // tile,),
        in_specs=[row, one, one],
        out_specs=row,
        out_shape=jax.ShapeDtypeStruct((rows, depth), BF16),
        compiler_params=params(("arbitrary",)),
        cost_estimate=cost(10 * rows * depth, 4 * rows * depth),
        name="norm",
    )(x, gain, shift)


def closing_kernel(terms, flag, x, g, gain, bias, other_bias, second, up, *refs):
    parts, more, refs = refs[:terms], refs[terms : 2 * terms], refs[2 * terms :]
    input_grad, output, gain_sum, shift_sum, out_grad, down_grad, up_grad = refs

    @pl.when(pl.program_id(0) == 0)
    def _():
        gain_sum[...] = jnp.zeros_like(gain_sum)
        shift_sum[...] = jnp.zeros_like(shift_sum)
        width = out_grad.shape[0]
        out_grad[...] = second[:width, :].astype(F32)
        down_grad[...] = second[width:, :].astype(F32)

    def total(many):
        result = many[0][...].astype(F32)
        for part in many[1:]:
            term = part[...].astype(F32)
            if part is many[-1]:
                term = jnp.where(flag[0] == 1, term, 0.0)
            result = result + term
        return result

    up_grad[...] = up[...].astype(F32)
    values = x[...].astype(F32)
    output[...] = (
        values + total(more) + bias[...].astype(F32) + other_bias[...].astype(F32)
    ).astype(BF16)
    centered = values - jnp.mean(values, axis=1, keepdims=True)
    scale = lax.rsqrt(jnp.mean(centered * centered, axis=1, keepdims=True) + EPS)
    hat = centered * scale
    back = total(parts)
    gain_sum[...] += jnp.sum(back * hat, axis=0, keepdims=True)
    shift_sum[...] += jnp.sum(back, axis=0, keepdims=True)
    e = back * gain[...].astype(F32)
    inner = (
        e - jnp.mean(e, axis=1, keepdims=True) - hat * jnp.mean(e * hat, axis=1, keepdims=True)
    )
    input_grad[...] = (g[...].astype(F32) + inner * scale).astype(BF16)


def closing(flag, x, g, gain, bias, other_bias, second, up, width, parts, more, tile=128):
    rows, depth = x.shape
    row = pl.BlockSpec((tile, depth), lambda i, f: (i, 0))
    one = once((1, depth), lambda i, f: (0, 0))
    total = pl.BlockSpec((1, depth), lambda i, f: (0, 0))
    still = lambda shape: once(shape, lambda i, f: (0, 0))
    step = up.shape[0] // (rows // tile)
    ups = pl.BlockSpec((step, up.shape[1]), lambda i, f: (i, 0))
    inner, columns = second.shape
    return pl.pallas_call(
        functools.partial(closing_kernel, len(parts)),
        grid_spec=pltpu.PrefetchScalarGridSpec(
            num_scalar_prefetch=1,
            grid=(rows // tile,),
            in_specs=[row, row, one, one, one, still(second.shape), ups] + [row] * (2 * len(parts)),
            out_specs=[
                row,
                row,
                total,
                total,
                still((width, columns)),
                still((inner - width, columns)),
                ups,
            ],
        ),
        out_shape=[
            jax.ShapeDtypeStruct((rows, depth), BF16),
            jax.ShapeDtypeStruct((rows, depth), BF16),
            jax.ShapeDtypeStruct((1, depth), F32),
            jax.ShapeDtypeStruct((1, depth), F32),
            jax.ShapeDtypeStruct((width, columns), F32),
            jax.ShapeDtypeStruct((inner - width, columns), F32),
            jax.ShapeDtypeStruct(up.shape, F32),
        ],
        compiler_params=params(("arbitrary",)),
        cost_estimate=cost(30 * rows * depth, 14 * rows * depth),
        name="closing",
    )(flag, x, g, gain, bias, other_bias, second, up, *parts, *more)


MESH = pl.DeviceIdType.MESH
ANYWHERE = pl.BlockSpec(memory_space=pl.ANY)


def places():
    me = lax.axis_index("tensor")
    core, chip = lax.rem(me, 2), lax.div(me, 2)
    beside = chip + 1 - 2 * lax.rem(chip, 2)
    inner = jnp.logical_or(chip == 1, chip == 2)
    return dict(
        core=core,
        partner=me + 1 - 2 * core,
        beside=2 * beside + core,
        opposite=2 * (3 - chip) + core,
        inner=inner,
        outer=jnp.logical_not(inner),
        all=None,
    )


def greet(at, others=()):
    barrier = pltpu.get_barrier_semaphore()
    ids = [{"tensor": at[name]} for name in ("partner", "beside", "opposite")] + list(others)
    for device in ids:
        pl.semaphore_signal(barrier, inc=1, device_id=device, device_id_type=MESH)
    pl.semaphore_wait(barrier, len(ids))


def to_device(src, dst, sent, got, device):
    return pltpu.make_async_remote_copy(
        src_ref=src,
        dst_ref=dst,
        send_sem=sent,
        recv_sem=got,
        device_id=device,
        device_id_type=MESH,
    )


def under(condition, act):
    if condition is None:
        act()
    else:
        pl.when(condition)(act)


def start_all(at, copies):
    for sender, _, copy in copies:
        under(at[sender], copy.start)


def finish_all(at, copies):
    for sender, receiver, copy in copies:
        under(at[receiver], copy.wait_recv)
        under(at[sender], copy.wait_send)


class Gather:
    MOVES = {
        1: (("all", "all", 3, 2, "beside"), ("inner", "inner", 3, 0, "opposite")),
        2: (("inner", "inner", 2, 1, "opposite"), ("inner", "outer", 0, 1, "beside")),
        3: (("inner", "outer", 1, 0, "beside"),),
        "own": (("all", "all", 3, 3, "partner"),),
        "first": (("all", "all", 2, 2, "partner"), ("inner", "inner", 0, 0, "partner")),
        "second": (("all", "all", 1, 1, "partner"),),
        "third": (("outer", "outer", 0, 0, "partner"),),
    }

    def __init__(self, *moves):
        self.moves = [(m, lo, hi) for name, lo, hi in moves for m in self.MOVES[name]]
        self.count = len(self.moves)

    def copies(self, at, full, sent, got):
        found = []
        for i, ((sender, receiver, src, dst, target), lo, hi) in enumerate(self.moves):
            rows = pl.ds(lo, hi - lo)
            found.append(
                (
                    sender,
                    receiver,
                    to_device(
                        full.at[src, at["core"], rows],
                        full.at[dst, at["core"], rows],
                        sent.at[i],
                        got.at[i],
                        {"tensor": at[target]},
                    ),
                )
            )
        return found


class Riding:
    def __init__(self, ins, outs, aliased, count, copies, late=0):
        self.ins, self.outs, self.aliased, self.count, self.copies = ins, outs, aliased, count, copies
        self.late = late
        self.scratch, self.summed = [], None


def like(array):
    return jax.ShapeDtypeStruct(array.shape, array.dtype)


def gathering(full, *moves, late=()):
    plan = Gather(*moves, *late)

    def copies(at, ins, outs, sent, got):
        return plan.copies(at, outs[0], sent, got)

    return Riding([full], [like(full)], True, plan.count, copies, Gather(*late).count)


SENDS = {
    "in": ("outer", "inner", "beside"),
    "middle": ("inner", "inner", "opposite"),
    "side": ("all", "all", "beside"),
}


def sending(values, kind, lo, hi, into=None):
    sender, receiver, target = SENDS[kind]

    def copies(at, ins, outs, sent, got):
        rows = pl.ds(lo, hi - lo)
        copy = to_device(
            ins[0].at[rows], outs[0].at[rows], sent.at[0], got.at[0], {"tensor": at[target]}
        )
        return [(sender, receiver, copy)]

    return Riding([values] + ([] if into is None else [into]), [like(values)], into is not None, 1, copies)


def summing(base, plus, kind, lo, hi, into=None, inner_only=False):
    sender, receiver, target = SENDS[kind]

    def copies(at, ins, outs, sent, got, total, other, sem):
        copy = to_device(
            total, outs[0].at[pl.ds(lo, hi - lo)], sent.at[0], got.at[0], {"tensor": at[target]}
        )
        return [(sender, receiver, copy)]

    def summed(at, ins, total, other, sem):
        rows = pl.ds(lo, hi - lo)
        loads = [
            pltpu.make_async_copy(src.at[rows], dst, sem.at[n])
            for n, (src, dst) in enumerate(zip(ins[:2], (total, other)))
        ]

        def add():
            for load in loads:
                load.wait()

            @pl.loop(0, (hi - lo) // 32)
            def _(i):
                here = pl.ds(pl.multiple_of(i * 32, 32), 32)
                term = other[here, :].astype(F32)
                if inner_only:
                    term = jnp.where(at["inner"], term, jnp.zeros_like(term))
                total[here, :] = (total[here, :].astype(F32) + term).astype(BF16)

        return loads, add

    ride = Riding(
        [base, plus] + ([] if into is None else [into]), [like(base)], into is not None, 1, copies
    )
    part = pltpu.VMEM((hi - lo, base.shape[1]), BF16)
    ride.scratch, ride.summed = [part, part, pltpu.SemaphoreType.DMA((2,))], summed
    return ride


def launch(body, args, ins, outs, shapes, grid, name, estimate, scratch=(), riding=(), ident=None, place=False, wait_for=(), lazy=(), seen=(), in_turn=False):
    if ident is None:
        return pl.pallas_call(
            functools.partial(body, lambda *which: None) if in_turn else body,
            grid=(grid,),
            in_specs=ins + [once(a.shape, lambda i, n=len(a.shape): (0,) * n) for a in lazy],
            out_specs=outs,
            out_shape=shapes,
            scratch_shapes=list(scratch),
            compiler_params=params(("arbitrary",)),
            cost_estimate=estimate,
            name=name,
        )(*args, *lazy)
    args, n_own = list(args) + list(lazy), len(args)
    riding = list(riding) + [Riding([a], [], False, 1, lambda *_: []) for a in wait_for]
    extra_in = [a for r in riding for a in r.ins]
    extra_out = [o for r in riding for o in r.outs]
    aliases, n_in, n_out = {}, len(args), len(shapes)
    for r in riding:
        if r.aliased:
            aliases[n_in + len(r.ins) - 1] = n_out
        n_in, n_out = n_in + len(r.ins), n_out + len(r.outs)

    def kernel(*refs):
        take = iter(refs)
        some = lambda n: [next(take) for _ in range(n)]
        own_ins, ride_ins = some(len(args)), [some(len(r.ins)) for r in riding]
        own_outs, ride_outs = some(len(shapes)), [some(len(r.outs)) for r in riding]
        own_scratch = some(len(scratch))
        loaded = some(len(lazy))
        loads = [
            pltpu.make_async_copy(src, dst, some(1)[0])
            for src, dst in zip(own_ins[n_own:], loaded)
        ]
        at = places()
        copies, late, sums = [], [], []
        for r, i, o in zip(riding, ride_ins, ride_outs):
            sems, room = some(2), some(len(r.scratch))
            found = r.copies(at, i, o, *sems, *room)
            if r.summed is None:
                copies += found[: len(found) - r.late]
                late += found[len(found) - r.late :]
            else:
                sums.append((*r.summed(at, i, *room), found))
        for first, _, _ in sums:
            for load in first:
                load.start()
        for load in loads:
            load.start()
        greet(at)
        start_all(at, copies)
        for _, add, found in sums:
            add()
            start_all(at, found)
            copies += found

        def ready(*which):
            @pl.when(pl.program_id(0) == 0)
            def _():
                for n in which:
                    loads[n].wait()

        def step(*blocks):
            if not in_turn:
                ready(*range(len(loads)))
            n_in = n_own + len(seen)
            body(*([at] if place else []), *([ready] if in_turn else []), *blocks[:n_in], *loaded, *blocks[n_in:], *own_scratch)

        if shapes:
            pltpu.emit_pipeline(
                step, grid=(grid,), in_specs=ins + [spec for _, spec in seen], out_specs=outs
            )(*own_ins[:n_own], *(ride_outs[r][0] for r, _ in seen), *own_outs)
        finish_all(at, copies)
        start_all(at, late)
        finish_all(at, late)

    return pl.pallas_call(
        kernel,
        in_specs=[ANYWHERE] * (len(args) + len(extra_in)),
        out_specs=[ANYWHERE] * (len(shapes) + len(extra_out)),
        out_shape=shapes + extra_out,
        input_output_aliases=aliases,
        scratch_shapes=list(scratch)
        + [pltpu.VMEM(a.shape, a.dtype) for a in lazy]
        + [pltpu.SemaphoreType.DMA] * len(lazy)
        + [
            entry
            for r in riding
            for entry in [pltpu.SemaphoreType.DMA((r.count,))] * 2 + r.scratch
        ],
        compiler_params=pltpu.CompilerParams(
            vmem_limit_bytes=VMEM_BYTES, collective_id=ident, has_side_effects=True
        ),
        cost_estimate=estimate,
        name=name,
    )(*args, *extra_in)


def opening_kernel(tile, groups, width, cut, *refs):
    x, gain, shift, g, *weights = refs[:10]
    biases, frequency, refs = refs[10:14], refs[14], refs[15:]
    rows_full, g_full, first_full, second_full, q, k, v, active, hidden, cos, low, high = refs[:12]
    g_sum, refs = refs[12], refs[13:]
    own, kept, first_kept, second_kept, w, bias, x_tile = refs[:7]
    staged, (local, x_sem, out_sem, w_sent, w_got), sems = refs[7:12], refs[12:17], refs[17:]
    at = places()
    core, dp = at["core"], lax.axis_index("dp")
    peers = [{"dp": jnp.bitwise_xor(dp, step)} for step in range(1, groups)]
    share, depth = own.shape
    half = share // 2
    units = hidden.shape[1]
    lows, highs = (0, half), (half, share)
    greet(at, peers)

    across = second_kept.shape[1]
    mine = pl.ds(pl.multiple_of(dp * across, across), across)
    columns = [(0, width), (width, width), (2 * width, width), (3 * width, units)]
    loads = [
        pltpu.make_async_copy(src, first_kept.at[:, pl.ds(start, size)], local.at[i])
        for i, (src, (start, size)) in enumerate(zip(weights[:4], columns))
    ] + [
        pltpu.make_async_copy(weights[4], second_kept.at[pl.ds(0, width)], local.at[4]),
        pltpu.make_async_copy(weights[5], second_kept.at[pl.ds(width, units)], local.at[5]),
        pltpu.make_async_copy(g, kept, local.at[6]),
    ]
    stores = [
        pltpu.make_async_copy(first_kept, first_full.at[dp], local.at[0]),
        pltpu.make_async_copy(second_kept, second_full.at[:, mine], local.at[1]),
        pltpu.make_async_copy(kept, g_full.at[3, core], local.at[2]),
        pltpu.make_async_copy(own, rows_full.at[3, core], local.at[7]),
    ]
    spread = [
        [to_device(src, dst, w_sent.at[n, i], w_got.at[n, i], peer) for i, peer in enumerate(peers)]
        for n, (src, dst) in enumerate(
            ((first_kept, first_full.at[dp]), (second_kept, second_full.at[:, mine]))
        )
    ]
    plans = dict(
        n1_low=[(1, *lows)],
        n1_high=[(1, *highs), ("own", 0, share)],
        n2_low=[(2, *lows)],
        n2_high=[(2, *highs)],
        e2_low=[("first", *lows)],
        e2_high=[("first", *highs)],
        n3_low=[(3, *lows)],
        n3_high=[(3, *highs)],
        e1_low=[("second", *lows)],
        e1_high=[("second", *highs)],
        e0_low=[("third", *lows)],
        e0_high=[("third", *highs)],
        g_own=[("own", 0, share)],
        g1=[(1, 0, cut)],
    )
    moves = {
        name: Gather(*plan).copies(
            at, g_full if name[0] == "g" else rows_full, sems[2 * i], sems[2 * i + 1]
        )
        for i, (name, plan) in enumerate(plans.items())
    }

    def start(*names):
        for name in names:
            start_all(at, moves[name])

    def finish(*names):
        for name in names:
            finish_all(at, moves[name])

    for copy in loads:
        copy.start()

    @pl.loop(0, share // tile)
    def _(i):
        rows = pl.ds(pl.multiple_of(i * tile, tile), tile)
        values = x[rows, :].astype(F32)
        centered = values - jnp.mean(values, axis=1, keepdims=True)
        scale = lax.rsqrt(jnp.mean(centered * centered, axis=1, keepdims=True) + EPS)
        own[rows, :] = (
            centered * scale * gain[...].astype(F32) + shift[...].astype(F32)
        ).astype(BF16)

    stores[3].start()
    for copy in loads:
        copy.wait()
    for copy in spread[0]:
        copy.start()
    for copy in stores[:3]:
        copy.start()
    stores[3].wait()
    start("n1_low", "n1_high")

    lane = lax.broadcasted_iota(jnp.int32, (1, 128), 1) % HEAD_DIM
    position = lax.broadcasted_iota(jnp.int32, cos.shape, 0).astype(F32)
    angle = position * frequency[...]
    sine = jnp.sin(angle)
    cos[...] = jnp.where(lane < ROT, jnp.cos(angle), 1.0)
    low[...] = jnp.where(lane < ROT // 2, -sine, 0.0)
    high[...] = jnp.where(jnp.logical_and(lane >= ROT // 2, lane < ROT), sine, 0.0)
    for ref, (begin, size) in zip(biases, columns):
        bias[:, begin : begin + size] = ref[...].astype(F32)
    g_sum[...] = jnp.zeros_like(g_sum)

    @pl.loop(0, share // tile)
    def _(i):
        rows = pl.ds(pl.multiple_of(i * tile, tile), tile)
        g_sum[...] += jnp.sum(kept[rows, :].astype(F32), axis=0, keepdims=True)

    for copy in stores[:3]:
        copy.wait()
    start("g_own")
    for copy in spread[1]:
        copy.start()
    finish("n1_low")
    start("n2_low", "e2_low")
    finish("n1_high")
    start("n2_high", "e2_high")
    finish("n2_low")
    start("n3_low", "e1_low")
    for copy in spread[0]:
        copy.wait()
    fetch = [
        pltpu.make_async_copy(
            first_full.at[d], w.at[pl.ds(d * first_full.shape[1], first_full.shape[1])], local.at[d]
        )
        for d in range(groups)
    ]
    for copy in fetch:
        copy.start()
    for copy in fetch:
        copy.wait()

    outs = (q, k, v, active, hidden)

    def results(i):
        part = jnp.where(lax.rem(i, 2) == 0, core, 1 - core)
        slot = 3 - lax.div(i, 2)
        rows = pl.ds(pl.multiple_of((2 * slot + part) * share, share), share)
        return [
            pltpu.make_async_copy(src.at[lax.rem(i, 2)], dst.at[rows], out_sem.at[lax.rem(i, 2), n])
            for n, (src, dst) in enumerate(zip(staged, outs))
        ]

    @pl.loop(0, 8)
    def _(i):
        @pl.when(i == 2)
        def _():
            finish("n2_high")
            start("n3_high", "e1_high")
            finish("e2_low", "e2_high")

        @pl.when(i == 4)
        def _():
            finish("e1_low", "e1_high")

        @pl.when(i == 6)
        def _():
            finish("n3_low")
            start("e0_low")
            finish("n3_high")
            start("e0_high")
            finish("g_own")
            start("g1")

        @pl.when(i == 7)
        def _():
            finish("e0_low", "e0_high")

        part = jnp.where(lax.rem(i, 2) == 0, core, 1 - core)
        load = pltpu.make_async_copy(rows_full.at[3 - lax.div(i, 2), part], x_tile, x_sem)
        load.start()

        @pl.when(i >= 2)
        def _():
            for copy in results(i - 2):
                copy.wait()

        load.wait()
        here = pl.ds(pl.multiple_of(part * share, share), share)
        project_tile(
            width,
            x_tile,
            w,
            bias,
            cos.at[here],
            low.at[here],
            high.at[here],
            *(r.at[lax.rem(i, 2)] for r in staged),
        )
        for copy in results(i):
            copy.start()

    for i in (6, 7):
        for copy in results(i):
            copy.wait()
    finish("g1")
    for copy in spread[1]:
        copy.wait()


OPENING_PLANS = (2, 3, 2, 2, 2, 2, 1, 1, 1, 1, 1, 1, 1, 2)


def opening(ident, x, gain, shift, g, weights, biases, groups, length, cut, tile=64):
    rows, depth = x.shape
    width, units = weights[0].shape[1], weights[3].shape[1]
    total = 3 * width + units
    inner = width + units
    columns = weights[4].shape[1]
    everything = 8 * rows
    whole = pl.BlockSpec(memory_space=pltpu.VMEM)
    full = jax.ShapeDtypeStruct((4, 2, rows, depth), BF16)
    exponent = np.arange(ROT // 2, dtype=np.float32) * np.float32(2.0 / ROT)
    frequency = np.tile(np.power(np.float32(10000.0), -exponent), 8)[None, :]
    table = jax.ShapeDtypeStruct((length, 128), F32)
    narrow = jax.ShapeDtypeStruct((everything, width), BF16)
    return pl.pallas_call(
        functools.partial(opening_kernel, tile, groups, width, cut),
        in_specs=[whole] * 3 + [ANYWHERE] * 7 + [whole] * 5,
        out_specs=[ANYWHERE] * 9 + [whole] * 4,
        out_shape=[
            full,
            full,
            jax.ShapeDtypeStruct((groups, depth // groups, total), BF16),
            jax.ShapeDtypeStruct((inner, groups * columns), BF16),
            narrow,
            narrow,
            narrow,
            jax.ShapeDtypeStruct((everything, units), BF16),
            jax.ShapeDtypeStruct((everything, units), F32),
            table,
            table,
            table,
            jax.ShapeDtypeStruct((1, depth), F32),
        ],
        scratch_shapes=[
            pltpu.VMEM((rows, depth), BF16),
            pltpu.VMEM((rows, depth), BF16),
            pltpu.VMEM((depth // groups, total), BF16),
            pltpu.VMEM((inner, columns), BF16),
            pltpu.VMEM((depth, total), BF16),
            pltpu.VMEM((1, total), F32),
            pltpu.VMEM((rows, depth), BF16),
            pltpu.VMEM((2, rows, width), BF16),
            pltpu.VMEM((2, rows, width), BF16),
            pltpu.VMEM((2, rows, width), BF16),
            pltpu.VMEM((2, rows, units), BF16),
            pltpu.VMEM((2, rows, units), F32),
            pltpu.SemaphoreType.DMA((8,)),
            pltpu.SemaphoreType.DMA,
            pltpu.SemaphoreType.DMA((2, 5)),
            pltpu.SemaphoreType.DMA((2, groups - 1)),
            pltpu.SemaphoreType.DMA((2, groups - 1)),
        ]
        + [pltpu.SemaphoreType.DMA((n,)) for n in OPENING_PLANS for _ in range(2)],
        compiler_params=pltpu.CompilerParams(
            vmem_limit_bytes=VMEM_BYTES, collective_id=ident, has_side_effects=True
        ),
        cost_estimate=cost(2 * everything * depth * total, 60 * rows * depth),
        name="opening",
    )(x, gain, shift, g, *weights, *biases, jnp.asarray(frequency))


def project_tile(width, x, w, bias, cos, low, high, q, k, v, active, hidden):
    rows = x[...]
    tables = (cos[...], low[...], high[...])
    q[...] = (
        rotated(nn(rows, w[:, :width]) + bias[:, :width], *tables).astype(BF16)
        * jnp.asarray(HEAD_DIM**-0.5, BF16)
    )
    k[...] = rotated(
        nn(rows, w[:, width : 2 * width]) + bias[:, width : 2 * width], *tables
    ).astype(BF16)
    v[...] = (nn(rows, w[:, 2 * width : 3 * width]) + bias[:, 2 * width : 3 * width]).astype(BF16)
    units = hidden.shape[1]
    step = min(256, units)
    for start in range(0, units, step):
        at = slice(3 * width + start, 3 * width + start + step)
        h = nn(rows, w[:, at]) + bias[:, at]
        hidden[:, start : start + step] = h
        active[:, start : start + step] = gelu(h).astype(BF16)


def project(x, w, bias, tables, width, units, length, riding=(), ident=None, tile=512):
    rows, depth = x.shape
    per = length // tile
    row = lambda n: pl.BlockSpec((tile, n), lambda i: (i, 0))
    table = pl.BlockSpec((tile, 128), lambda i: (i % per, 0))
    total = 3 * width + units
    return launch(
        functools.partial(project_tile, width),
        [x, w, bias, *tables],
        [
            row(depth),
            once((depth, total), lambda i: (0, 0)),
            once((1, total), lambda i: (0, 0)),
            table,
            table,
            table,
        ],
        [row(width), row(width), row(width), row(units), row(units)],
        [jax.ShapeDtypeStruct((rows, width), BF16)] * 3
        + [jax.ShapeDtypeStruct((rows, units), BF16), jax.ShapeDtypeStruct((rows, units), F32)],
        rows // tile,
        "project",
        cost(2 * rows * depth * total, 2 * depth * (rows + total) + rows * units * 6),
        riding=riding,
        ident=ident,
    )


def each_tile_kernel(body, *refs):
    body(*refs)


def each_tile(body, arrays, w, depth, name, tile=512):
    rows = arrays[0].shape[0]
    return pl.pallas_call(
        functools.partial(each_tile_kernel, body),
        grid=(rows // tile,),
        in_specs=[pl.BlockSpec((tile, a.shape[1]), lambda i: (i, 0)) for a in arrays]
        + [once(w.shape, lambda i, n=len(w.shape): (0,) * n)],
        out_specs=pl.BlockSpec((tile, depth), lambda i: (i, 0)),
        out_shape=jax.ShapeDtypeStruct((rows, depth), BF16),
        compiler_params=params(("arbitrary",)),
        cost_estimate=cost(2 * w.size * rows, 2 * rows * depth),
        name=name,
    )(*arrays, w)


def core_sum_body(body, count, pieces, n_in, at, *refs):
    ins, w, outs = refs[:n_in], refs[n_in], refs[n_in + 1 : n_in + 1 + count]
    sent, got, value, send_sem, got_sem = refs[n_in + 1 + count :]
    slot = pl.program_id(0)
    core = at["core"]
    share = sent.shape[1]
    piece = share // pieces

    def term(owner, i, to):
        rows = pl.ds(pl.multiple_of(owner * share + i * piece, piece), piece)
        body(*(r.at[rows, :] for r in ins), w, to)

    def copy(i):
        rows = pl.ds(i * piece, piece)
        return to_device(
            sent.at[slot, rows],
            got.at[slot, rows],
            send_sem.at[slot, i],
            got_sem.at[slot, i],
            {"tensor": at["partner"]},
        )

    for i in range(pieces):
        term(1 - core, i, sent.at[slot, pl.ds(i * piece, piece)])
        copy(i).start()
    for i in range(pieces):
        rows = pl.ds(i * piece, piece)
        term(core, i, value)
        copy(i).wait_recv()
        for n, out in enumerate(outs):

            @pl.when(slot == n)
            def _(out=out):
                out[rows, :] = (value[...] + got[slot, rows].astype(F32)).astype(BF16)

    for i in range(pieces):
        copy(i).wait_send()


def core_sum_parts(count, pieces, length, depth):
    share = length // 2
    out = pl.BlockSpec((share, depth), lambda i: (0, 0), pipeline_mode=pl.Buffered(1))
    return (
        [out] * count,
        [jax.ShapeDtypeStruct((share, depth), BF16)] * count,
        [
            pltpu.VMEM((count, share, depth), BF16),
            pltpu.VMEM((count, share, depth), BF16),
            pltpu.VMEM((share // pieces, depth), F32),
            pltpu.SemaphoreType.DMA((count, pieces)),
            pltpu.SemaphoreType.DMA((count, pieces)),
        ],
    )


def core_sum(body, ident, count, length, arrays, w, depth, name, pieces=2, riding=()):
    outs, shapes, scratch = core_sum_parts(count, pieces, length, depth)
    size = sum(a.shape[1] for a, _ in arrays)
    return launch(
        functools.partial(core_sum_body, body, count, pieces, len(arrays)),
        [a for a, _ in arrays],
        [pl.BlockSpec((length, a.shape[1]), lambda i, f=f: (f + i, 0)) for a, f in arrays],
        outs,
        shapes,
        count,
        name,
        cost(2 * count * length * size * depth, 2 * count * length * (size + depth) + 2 * size * depth),
        scratch=scratch,
        riding=riding,
        ident=ident,
        place=True,
        lazy=[w],
    )


def mix_body(attended, active, w, out):
    width, depth = attended.shape[1], w.shape[1]
    step = min(512, depth)
    for start in range(0, depth, step):
        at = slice(start, start + step)
        out[:, at] = (nn(attended[...], w[:width, at]) + nn(active[...], w[width:, at])).astype(
            out.dtype
        )


def unproject_body(qkv_grad, hidden_grad, w, out):
    three = qkv_grad.shape[1]
    depth = w.shape[0]
    step = min(512, depth)
    for start in range(0, depth, step):
        out[:, start : start + step] = (
            nt(qkv_grad[...], w[start : start + step, :three])
            + nt(hidden_grad[...], w[start : start + step, three:])
        ).astype(out.dtype)


def unmix_tile(hidden, g, w, attended_grad, hidden_grad, sums):
    width = attended_grad.shape[1]
    units = hidden.shape[1]

    @pl.when(pl.program_id(0) == 0)
    def _():
        sums[...] = jnp.zeros_like(sums)

    rows = g[...]
    attended_grad[...] = nt(rows, w[:width, :]).astype(BF16)
    step = min(256, units)
    for start in range(0, units, step):
        at = slice(start, start + step)
        back = nt(rows, w[width + start : width + start + step, :])
        low = (back * gelu_slope(hidden[:, at])).astype(BF16)
        hidden_grad[:, at] = low
        sums[:, at] += jnp.sum(low.astype(F32), axis=0, keepdims=True)


def unmix(g, w, hidden, width, first, count, length, riding=(), ident=None, tile=512):
    rows = count * length
    units = hidden.shape[1]
    inner, depth = w.shape
    per = length // tile
    row = lambda n: pl.BlockSpec((tile, n), lambda i: (i, 0))
    late = lambda n: pl.BlockSpec((tile, n), lambda i: (first * per + i, 0))
    seen = []
    if g is None:
        seen = [
            (0, pl.BlockSpec((None, None, tile, depth), lambda i: (first + i // 2, i % 2, 0, 0)))
        ]
    return launch(
        unmix_tile,
        [hidden] + ([] if g is None else [g]),
        [late(units)] + ([] if g is None else [late(depth)]),
        [row(width), row(units), pl.BlockSpec((1, units), lambda i: (0, 0))],
        [
            jax.ShapeDtypeStruct((rows, width), BF16),
            jax.ShapeDtypeStruct((rows, units), BF16),
            jax.ShapeDtypeStruct((1, units), F32),
        ],
        rows // tile,
        "unmix",
        cost(2 * rows * inner * depth, 2 * depth * (rows + inner) + rows * units * 6),
        riding=riding,
        ident=ident,
        lazy=[w],
        seen=seen,
    )


def outer_rows_kernel(ready, x, *refs):
    parts, out = refs[:-1], refs[-1]
    total, start = None, 0
    for n, part in enumerate(parts):
        ready(n)
        term = tn(x[start : start + part.shape[0], :], part[...])
        total = term if total is None else total + term
        start += part.shape[0]
    out[...] = total.astype(out.dtype)


def outer_rows(x, parts, riding=(), ident=None, tile=256, wait_for=()):
    rows, depth = x.shape
    n = parts[0].shape[1]
    return launch(
        outer_rows_kernel,
        [x],
        [pl.BlockSpec((rows, tile), lambda i: (0, i))],
        [pl.BlockSpec((tile, n), lambda i: (i, 0))],
        [jax.ShapeDtypeStruct((depth, n), BF16)],
        depth // tile,
        "outer_rows",
        cost(2 * rows * depth * n, 2 * (rows * (depth + n) + depth * n)),
        riding=riding,
        ident=ident,
        wait_for=wait_for,
        lazy=parts,
        in_turn=True,
    )


def outer_columns_kernel(ready, g, *refs):
    many, b, out = refs[:-2], refs[-2], refs[-1]
    width = many[0].shape[1]
    total, start = None, 0
    for n, a in enumerate(many):
        ready(n)
        term = tn(a[...], g[start : start + a.shape[0], :])
        total = term if total is None else total + term
        start += a.shape[0]
    out[0, :width, :] = total.astype(out.dtype)
    ready(len(many))
    out[0, width:, :] = tn(b[...], g[...]).astype(out.dtype)


def outer_columns(many, b, g, parts, riding=(), ident=None, tile=512):
    rows, depth = g.shape
    width, units = many[0].shape[1], b.shape[1]
    across = depth // parts
    tile = min(tile, across)
    per = across // tile
    return launch(
        outer_columns_kernel,
        [g],
        [pl.BlockSpec((rows, tile), lambda i: (0, i))],
        [pl.BlockSpec((1, width + units, tile), lambda i: (i // per, 0, i % per))],
        [jax.ShapeDtypeStruct((parts, width + units, across), BF16)],
        depth // tile,
        "outer_columns",
        cost(2 * rows * depth * (width + units), 2 * (rows * (depth + width + units) + depth * (width + units))),
        riding=riding,
        ident=ident,
        lazy=list(many) + [b],
        in_turn=True,
    )


def head_lanes(width, head):
    return lax.broadcasted_iota(jnp.int32, (1, width), 1) // HEAD_DIM == head


def attend_kernel(q, k, v, column_ids, row_ids, out, log_sums):
    length, width = q.shape
    heads = width // HEAD_DIM
    tile = min(SPAN, length)
    lanes = lax.broadcasted_iota(jnp.int32, (1, 128), 1)
    for begin in range(0, length, tile):
        end = min(length, begin + tile + SPAN)
        q_ids = column_ids[begin : begin + tile, :]
        blocked = row_ids[:, begin:end] > q_ids
        rows = q[begin : begin + tile, :]

        def one_head(head, carry):
            total, sums = carry
            mine = head_lanes(width, head)
            scores = nt(jnp.where(mine, rows, jnp.zeros_like(rows)), k[:end, :])
            tail = jnp.where(blocked, -1e9, scores[:, begin:])
            scores = jnp.concatenate([scores[:, :begin], tail], axis=1) if begin else tail
            highest = jnp.max(scores, axis=1, keepdims=True)
            powers = jnp.exp(scores - highest)
            amount = jnp.sum(powers, axis=1, keepdims=True)
            low = (powers * (1.0 / amount)).astype(BF16)
            total = jnp.where(mine, nn(low, v[:end, :]), total)
            sums = jnp.where(lanes == head, highest + jnp.log(amount), sums)
            return total, sums

        total, sums = jnp.zeros((tile, width), F32), jnp.zeros((tile, 128), F32)
        for head in range(heads):
            total, sums = one_head(head, (total, sums))
        out[begin : begin + tile, :] = total.astype(BF16)
        log_sums[:, begin : begin + tile] = sums.T[:8, :]


def attend(first, count, q, k, v, column_ids, row_ids, riding=(), ident=None):
    width = q.shape[1]
    length = row_ids.shape[2]
    rows, seqs = count * length, count
    heads = width // HEAD_DIM
    seq = pl.BlockSpec((length, width), lambda s: (first + s, 0))
    out = pl.BlockSpec((length, width), lambda s: (s, 0))
    return launch(
        attend_kernel,
        [q, k, v, column_ids, row_ids],
        [
            seq,
            seq,
            seq,
            pl.BlockSpec((length, 1), lambda s: (first + s, 0)),
            pl.BlockSpec((None, 1, length), lambda s: (first + s, 0, 0)),
        ],
        [out, pl.BlockSpec((8, length), lambda s: (0, s))],
        [jax.ShapeDtypeStruct((rows, width), BF16), jax.ShapeDtypeStruct((8, rows), F32)],
        seqs,
        "attend",
        cost(8 * seqs * heads * length * length * 256 * 0.8, 8 * rows * width, seqs * heads * length**2),
        riding=riding,
        ident=ident,
    )


def unattend_kernel(
    q, k, v, g, log_sums, column_ids, row_ids, cos, low, high, out, sums, key_total, value_total
):
    length, width = q.shape
    heads = width // HEAD_DIM
    tile = min(SPAN, length)
    tables = (cos[...], -low[...], -high[...])

    @pl.when(pl.program_id(0) == 0)
    def _():
        sums[...] = jnp.zeros_like(sums)

    key_total[...] = jnp.zeros_like(key_total)
    value_total[...] = jnp.zeros_like(value_total)

    def products(begin, head):
        end, at = min(length, begin + tile + SPAN), slice(begin, begin + tile)
        mine = head_lanes(width, head)
        q_rows, g_rows = q[at, :], g[at, :]
        q_head = jnp.where(mine, q_rows, jnp.zeros_like(q_rows))
        g_head = jnp.where(mine, g_rows, jnp.zeros_like(g_rows))
        return q_head, g_head, nt(k[:end, :], q_head), nt(v[:end, :], g_head)

    steps = [(begin, head) for begin in range(0, length, tile) for head in range(heads)]
    ahead = products(*steps[0])
    query_total = None
    for n, (begin, head) in enumerate(steps):
        q_head, g_head, scores, prob_grad = ahead
        if n + 1 < len(steps):
            ahead = products(*steps[n + 1])
        end, at = min(length, begin + tile + SPAN), slice(begin, begin + tile)
        blocked = column_ids[begin:end, :] > row_ids[:, at]
        tail = jnp.where(blocked, -1e9, scores[begin:, :])
        scores = jnp.concatenate([scores[:begin, :], tail], axis=0) if begin else tail
        probs = jnp.exp(scores - log_sums[head : head + 1, at])
        value_total[:end, :] += nn(probs.astype(BF16), g_head)
        inner = jnp.sum(prob_grad * probs, axis=0, keepdims=True)
        score_grad = (probs * (prob_grad - inner)).astype(BF16)
        key_total[:end, :] += nn(score_grad, q_head)
        part = tn(score_grad, k[:end, :])
        query_total = jnp.where(
            head_lanes(width, head), part, query_total if head else jnp.zeros_like(part)
        )
        if head == heads - 1:
            turned = rotated(query_total * HEAD_DIM**-0.5, *(t[at, :] for t in tables)).astype(BF16)
            out[at, :width] = turned
            sums[:, :width] += jnp.sum(turned.astype(F32), axis=0, keepdims=True)
    turned = rotated(key_total[...], *tables).astype(BF16)
    out[:, width : 2 * width] = turned
    sums[:, width : 2 * width] += jnp.sum(turned.astype(F32), axis=0, keepdims=True)
    turned = value_total[...].astype(BF16)
    out[:, 2 * width :] = turned
    sums[:, 2 * width :] += jnp.sum(turned.astype(F32), axis=0, keepdims=True)


def unattend(first, count, q, k, v, g, g_first, log_sums, sums_first, column_ids, row_ids, tables, riding=(), ident=None, wait_for=()):
    width = q.shape[1]
    length = row_ids.shape[2]
    rows, seqs = count * length, count
    heads = width // HEAD_DIM
    seq = pl.BlockSpec((length, width), lambda s: (first + s, 0))
    table = once((length, 128), lambda s: (0, 0))
    return launch(
        unattend_kernel,
        [q, k, v, g, log_sums, column_ids, row_ids, *tables],
        [
            seq,
            seq,
            seq,
            pl.BlockSpec((length, width), lambda s: (g_first + s, 0)),
            pl.BlockSpec((8, length), lambda s: (0, sums_first + s)),
            pl.BlockSpec((length, 1), lambda s: (first + s, 0)),
            pl.BlockSpec((None, 1, length), lambda s: (first + s, 0, 0)),
            table,
            table,
            table,
        ],
        [
            pl.BlockSpec((length, 3 * width), lambda s: (s, 0)),
            pl.BlockSpec((1, 3 * width), lambda s: (0, 0)),
        ],
        [jax.ShapeDtypeStruct((rows, 3 * width), BF16), jax.ShapeDtypeStruct((1, 3 * width), F32)],
        count,
        "unattend",
        cost(20 * seqs * heads * length * length * 256 * 0.8, 14 * rows * width, seqs * heads * length**2),
        scratch=[pltpu.VMEM((length, width), F32), pltpu.VMEM((length, width), F32)],
        riding=riding,
        ident=ident,
        wait_for=wait_for,
    )


def attend_mix_body(count, pieces, at, q, k, v, column_ids, row_ids, active, w, out, log_sums, *refs):
    attend_kernel(q, k, v, column_ids, row_ids, out, log_sums)
    core_sum_body(mix_body, count, pieces, 2, at, out, active, w, *refs)


def attend_mix(first, count, q, k, v, column_ids, row_ids, active, w, riding, ident, pieces=2):
    width, units = q.shape[1], active.shape[1]
    length = row_ids.shape[2]
    depth = w.shape[1]
    rows, heads = count * length, width // HEAD_DIM
    here = lambda n: pl.BlockSpec((length, n), lambda s: (first + s, 0))
    outs, shapes, scratch = core_sum_parts(count, pieces, length, depth)
    return launch(
        functools.partial(attend_mix_body, count, pieces),
        [q, k, v, column_ids, row_ids, active],
        [
            here(width),
            here(width),
            here(width),
            here(1),
            pl.BlockSpec((None, 1, length), lambda s: (first + s, 0, 0)),
            here(units),
        ],
        [pl.BlockSpec((length, width), lambda s: (s, 0)), pl.BlockSpec((8, length), lambda s: (0, s))]
        + outs,
        [jax.ShapeDtypeStruct((rows, width), BF16), jax.ShapeDtypeStruct((8, rows), F32)] + shapes,
        count,
        "attend_mix",
        cost(8 * rows * heads * length * 256 * 0.8, 8 * rows * width, rows * heads * length),
        scratch=scratch,
        riding=riding,
        ident=ident,
        place=True,
        lazy=[w],
    )


def unattend_unproject_body(pieces, at, *refs):
    operands, hidden_grad, w, (out, sums, part), scratch = (
        refs[:10],
        refs[10],
        refs[11],
        refs[12:15],
        refs[15:],
    )
    unattend_kernel(*operands, out, sums, *scratch[:2])
    core_sum_body(unproject_body, 1, pieces, 2, at, out, hidden_grad, w, part, *scratch[2:])


def unattend_unproject(
    at, q, k, v, g, g_at, log_sums, sums_at, column_ids, row_ids, tables, hidden_grad, hidden_at, w, riding, ident, pieces=2
):
    width, units = q.shape[1], hidden_grad.shape[1]
    length = row_ids.shape[2]
    depth = w.shape[0]
    heads = width // HEAD_DIM
    here = lambda n, at: pl.BlockSpec((length, n), lambda s: (at, 0))
    table = pl.BlockSpec((length, 128), lambda s: (0, 0))
    outs, shapes, scratch = core_sum_parts(1, pieces, length, depth)
    return launch(
        functools.partial(unattend_unproject_body, pieces),
        [q, k, v, g, log_sums, column_ids, row_ids, *tables, hidden_grad],
        [
            here(width, at),
            here(width, at),
            here(width, at),
            here(width, g_at),
            pl.BlockSpec((8, length), lambda s: (0, sums_at)),
            here(1, at),
            pl.BlockSpec((None, 1, length), lambda s: (at, 0, 0)),
            table,
            table,
            table,
            here(units, hidden_at),
        ],
        [
            pl.BlockSpec((length, 3 * width), lambda s: (0, 0)),
            pl.BlockSpec((1, 3 * width), lambda s: (0, 0)),
        ]
        + outs,
        [
            jax.ShapeDtypeStruct((length, 3 * width), BF16),
            jax.ShapeDtypeStruct((1, 3 * width), F32),
        ]
        + shapes,
        1,
        "unattend_unproject",
        cost(20 * heads * length * length * 256 * 0.8, 14 * length * width, heads * length**2),
        scratch=[pltpu.VMEM((length, width), F32), pltpu.VMEM((length, width), F32)] + scratch,
        riding=riding,
        ident=ident,
        place=True,
        lazy=[w],
    )


def nothing():
    pass


def add_up(*parts):
    total = parts[0].astype(F32)
    for part in parts[1:]:
        total = total + part.astype(F32)
    return total.astype(BF16)


def after(values, *others):
    return lax.optimization_barrier((values,) + others)[0]


def sum_everywhere_kernel(groups, members, counts, *refs):
    vectors, refs = refs[:3], refs[3:]
    narrows = []
    for count in counts:
        narrows.append(refs[:count])
        refs = refs[count:]
    wide, narrow, buf, in_dp, in_tensor, send_dp, got_dp, send_tensor, got_tensor = refs
    dp, tensor = lax.axis_index("dp"), lax.axis_index("tensor")
    mesh = pl.DeviceIdType.MESH
    barrier = pltpu.get_barrier_semaphore()
    for step in range(1, groups):
        pl.semaphore_signal(barrier, inc=1, device_id={"dp": lax.rem(dp + step, groups)}, device_id_type=mesh)
    for step in range(1, members):
        pl.semaphore_signal(barrier, inc=1, device_id={"tensor": lax.rem(tensor + step, members)}, device_id_type=mesh)
    pl.semaphore_wait(barrier, groups + members - 2)
    lanes = buf.shape[2] // 4
    for k, ref in enumerate(vectors):
        for r in range(8):
            buf[0, r : r + 1, k * lanes : (k + 1) * lanes] = ref[:, r * lanes : (r + 1) * lanes]
    row = 0
    buf[0, :, 3 * lanes :] = jnp.zeros((8, lanes), F32)
    for many in narrows:
        for start in range(0, many[0].shape[1], lanes):
            term = many[0][:, start : start + lanes]
            for ref in many[1:]:
                term = term + ref[:, start : start + lanes]
            buf[0, row : row + 1, 3 * lanes :] = term
            row += 1

    def exchange(axis, me, size, source, into, send, got):
        copies = []
        for step in range(1, size):
            copies.append(
                pltpu.make_async_remote_copy(
                    src_ref=source,
                    dst_ref=into.at[step - 1],
                    send_sem=send.at[step - 1],
                    recv_sem=got.at[step - 1],
                    device_id={axis: lax.rem(me + step, size)},
                    device_id_type=mesh,
                )
            )
        for copy in copies:
            copy.start()
        for copy in copies:
            copy.wait()

    exchange("dp", dp, groups, buf.at[0], in_dp, send_dp, got_dp)
    total = buf[0]
    for step in range(groups - 1):
        total = total + in_dp[step]
    row = 0
    for start in range(0, narrow.shape[1], lanes):
        narrow[:, start : start + lanes] = total[row : row + 1, 3 * lanes :]
        row += 1
    buf[1] = total
    exchange("tensor", tensor, members, buf.at[1], in_tensor, send_tensor, got_tensor)
    total = buf[1]
    for step in range(members - 1):
        total = total + in_tensor[step]
    for k in range(3):
        for r in range(8):
            wide[k : k + 1, r * lanes : (r + 1) * lanes] = total[r : r + 1, k * lanes : (k + 1) * lanes]


def sum_everywhere(ident, groups, members, vectors, narrows):
    depth = vectors[0].shape[1]
    counts = [len(many) for many in narrows]
    whole = pl.BlockSpec(memory_space=pltpu.VMEM)
    return pl.pallas_call(
        functools.partial(sum_everywhere_kernel, groups, members, counts),
        in_specs=[whole] * (3 + sum(counts)),
        out_specs=[whole] * 2,
        out_shape=[
            jax.ShapeDtypeStruct((8, depth), F32),
            jax.ShapeDtypeStruct((1, sum(many[0].shape[1] for many in narrows)), F32),
        ],
        scratch_shapes=[
            pltpu.VMEM((2, 8, depth // 2), F32),
            pltpu.VMEM((groups - 1, 8, depth // 2), F32),
            pltpu.VMEM((members - 1, 8, depth // 2), F32),
            pltpu.SemaphoreType.DMA((groups - 1,)),
            pltpu.SemaphoreType.DMA((groups - 1,)),
            pltpu.SemaphoreType.DMA((members - 1,)),
            pltpu.SemaphoreType.DMA((members - 1,)),
        ],
        compiler_params=pltpu.CompilerParams(collective_id=ident, has_side_effects=True),
        name="sum_everywhere",
    )(*vectors, *(v for many in narrows for v in many))


def per_device(
    inputs,
    block_ids,
    norm_gain,
    norm_bias,
    query_weight,
    query_bias,
    key_weight,
    key_bias,
    value_weight,
    value_bias,
    out_weight,
    out_bias,
    up_weight,
    up_bias,
    down_weight,
    down_bias,
    grad_out,
):
    seqs, length = block_ids.shape
    share, depth = inputs.shape
    width = query_weight.shape[1]
    units = up_weight.shape[1]
    groups, members = lax.axis_size("dp"), lax.axis_size("tensor")
    gain, shift = norm_gain.astype(F32)[None, :], norm_bias.astype(F32)[None, :]
    paired = groups == 4 and members == 8 and seqs == 4 and 2 * share == length
    me = lax.axis_index("tensor")
    if paired:
        chip = me // 2
        order = jnp.arange(3, -1, -1, dtype=jnp.int32) ^ chip
        inner = ((chip == 1) | (chip == 2)).astype(jnp.int32)
    else:
        order = jnp.arange(seqs, dtype=jnp.int32)

    ids = block_ids[order]
    column_ids = ids.reshape(seqs * length, 1)
    row_ids = ids.reshape(seqs, 1, length)
    pair = seqs // 2
    everything = seqs * length
    idents = iter(range(1, 100))

    if paired:
        cuts = lambda fraction: int(share * fraction) // 32 * 32
        g1 = cuts(0.25)
        rows, full, first_full, second_full, q, k, v, active, hidden, *tables, bias_part = opening(
            next(idents),
            inputs,
            norm_gain[None, :],
            norm_bias[None, :],
            grad_out,
            [query_weight, key_weight, value_weight, up_weight, out_weight, down_weight],
            [b[None, :] for b in (query_bias, key_bias, value_bias, up_bias)],
            groups,
            length,
            g1,
        )
        rows = rows.reshape(everything, depth)
        first_full = first_full.reshape(depth, 3 * width + units)

        def unheads(at, count, g, g_at, sums, sums_at, riding, wait_for=()):
            return unattend(
                at,
                count,
                q,
                k,
                v,
                g,
                g_at,
                sums,
                sums_at,
                column_ids,
                row_ids,
                tables,
                riding=riding,
                ident=next(idents),
                wait_for=wait_for,
            )

        def unprojected(count, grads, riding):
            return core_sum(
                unproject_body,
                next(idents),
                count,
                length,
                grads,
                first_full,
                depth,
                "unproject",
                riding=riding,
            )

        def forward(at, riding):
            return attend_mix(
                at, pair, q, k, v, column_ids, row_ids, active, second_full, riding, next(idents)
            )

        far_attended, far_sums, *far, full = forward(0, [gathering(full, (1, g1, share))])

        near_attended, near_sums, *near, full, end = forward(
            pair,
            [gathering(full, (2, 0, share), ("first", 0, share)), sending(far[0], "in", 0, share)],
        )

        ends, part = end, cuts(0.44)
        near_attended_grad, near_hidden_grad, near_up_sum, full, end, middle = unmix(
            None,
            second_full,
            hidden,
            width,
            pair,
            pair,
            length,
            riding=[
                gathering(full, (3, 0, part), ("second", 0, share)),
                sending(far[1], "in", 0, part),
                summing(far[1], ends, "middle", 0, part),
            ],
            ident=next(idents),
        )
        near_grad, near_sum, full, end, middle = unheads(
            pair,
            pair,
            near_attended_grad,
            0,
            near_sums,
            0,
            [
                gathering(
                    full, (3, part, share), ("third", 0, part), late=[("third", part, share)]
                ),
                sending(far[1], "in", part, share, end),
                summing(far[1], ends, "middle", part, share, middle),
            ],
        )
        upstream = full.reshape(everything, depth)

        def outward(side_terms, middle_terms):
            def rides(lo, hi, side=None, middle=None):
                return [
                    summing(*side_terms, "side", lo, hi, side, inner_only=True),
                    summing(*middle_terms, "middle", lo, hi, middle),
                ]

            return rides

        send_out = outward((near[0], middle), (far[0], end))
        mine = near[1]
        part = cuts(0.4)

        far_attended_grad, far_hidden_grad, far_up_sum, side, middle = unmix(
            upstream,
            second_full,
            hidden,
            width,
            0,
            pair,
            length,
            riding=send_out(0, part),
            ident=next(idents),
        )

        def backward(at, riding, wait_for=()):
            return unattend_unproject(
                at,
                q,
                k,
                v,
                far_attended_grad,
                at,
                far_sums,
                at,
                column_ids,
                row_ids,
                tables,
                far_hidden_grad,
                at,
                first_full,
                riding + [Riding([a], [], False, 1, lambda *_: []) for a in wait_for],
                next(idents),
            )

        grads_0, sum_0, far_0, side, middle = backward(0, send_out(part, share, side, middle))
        output_terms = [mine, side, middle]

        part = cuts(0.45)
        up_part, end = outer_rows(
            rows,
            [far_hidden_grad, near_hidden_grad],
            riding=[sending(far_0, "in", 0, part)],
            ident=next(idents),
        )
        up_grad = lax.psum_scatter(up_part, "dp", scatter_dimension=0, tiled=True)
        grads_1, sum_1, far_1, end = backward(
            1, [sending(far_0, "in", part, share, end)], [up_part]
        )
    else:
        tables = rotary_tables(length)
        first = jnp.concatenate([query_weight, key_weight, value_weight, up_weight], axis=1)
        second = jnp.concatenate([out_weight, down_weight], axis=0)
        bias = jnp.concatenate([query_bias, key_bias, value_bias, up_bias]).astype(F32)[None, :]
        first_full = lax.all_gather(first, "dp", axis=0, tiled=True)
        second_full = lax.all_gather(second, "dp", axis=1, tiled=True)
        rows = lax.all_gather(norm(inputs, gain, shift), "tensor", axis=0, tiled=True)
        upstream = lax.all_gather(grad_out, "tensor", axis=0, tiled=True)
        q, k, v, active, hidden = project(rows, first_full, bias, tables, width, units, length)
        attended, log_sums = attend(0, seqs, q, k, v, column_ids, row_ids)
        whole = each_tile(mix_body, [attended, active], second_full, depth, "mix")
        output_terms = [lax.psum_scatter(whole, "tensor", scatter_dimension=0, tiled=True)]
        attended_grad, hidden_grad, up_sum = unmix(
            upstream, second_full, hidden, width, 0, seqs, length
        )
    if paired:
        ends, part = end, cuts(0.56)
        second_part, end, middle = outer_columns(
            [far_attended, near_attended],
            active,
            upstream,
            groups,
            riding=[sending(far_1, "in", 0, part), summing(far_1, ends, "middle", 0, part)],
            ident=next(idents),
        )
        second_grad = lax.psum_scatter(second_part, "dp", scatter_dimension=0)
        *near, end, middle = unprojected(
            pair,
            [(near_grad, 0), (near_hidden_grad, 0)],
            [
                sending(far_1, "in", part, share, end),
                summing(far_1, ends, "middle", part, share, middle),
            ],
        )
        send_out = outward((near[0], middle), (far_0, end))
        part = cuts(0.5)
        first_part, side, middle = outer_rows(
            rows,
            [grads_0, grads_1, near_grad],
            riding=send_out(0, part),
            ident=next(idents),
            wait_for=[up_grad],
        )
        first_grad = lax.psum_scatter(first_part, "dp", scatter_dimension=0, tiled=True)
        side, middle = launch(
            nothing,
            [],
            [],
            [],
            [],
            1,
            "finish",
            cost(1e9, 1e6),
            riding=send_out(part, share, side, middle),
            ident=next(idents),
            wait_for=[first_part],
        )
        terms = [near[1], side, middle]
    else:
        inner = jnp.ones((), jnp.int32)
        qkv_grad, qkv_sum = unattend(
            0, seqs, q, k, v, attended_grad, 0, log_sums, 0, column_ids, row_ids, tables
        )
        whole = each_tile(unproject_body, [qkv_grad, hidden_grad], first_full, depth, "unproject")
        terms = [lax.psum_scatter(whole, "tensor", scatter_dimension=0, tiled=True)]
        (second_part,) = outer_columns([attended], active, upstream, groups)
        (first_part,) = outer_rows(rows, [qkv_grad])
        (up_part,) = outer_rows(rows, [hidden_grad])
        second_grad = lax.psum_scatter(second_part, "dp", scatter_dimension=0)
        first_grad = lax.psum_scatter(first_part, "dp", scatter_dimension=0, tiled=True)
        up_grad = lax.psum_scatter(up_part, "dp", scatter_dimension=0, tiled=True)

    first_grad = first_grad.astype(F32)
    input_grad, output, gain_part, shift_part, out_grad, down_grad, up_grad = closing(
        inner[None],
        inputs,
        grad_out,
        norm_gain[None, :],
        out_bias[None, :],
        down_bias[None, :],
        second_grad,
        up_grad,
        width,
        terms,
        output_terms,
    )
    if paired:
        wide, narrow = sum_everywhere(
            next(idents),
            groups,
            members,
            [gain_part, shift_part, bias_part],
            [[sum_0, sum_1, near_sum], [near_up_sum, far_up_sum]],
        )
        gain_grad, shift_grad, outer_bias_grad = wide[0], wide[1], wide[2]
        qkv_sum, up_sum = narrow[0, : 3 * width], narrow[0, 3 * width :]
    else:
        gain_grad, shift_grad, outer_bias_grad = lax.psum(
            (gain_part[0], shift_part[0], jnp.sum(grad_out, axis=0, dtype=F32)), ("dp", "tensor")
        )
        qkv_sum, up_sum = lax.psum((qkv_sum[0], up_sum[0]), "dp")
    return (
        output,
        input_grad,
        gain_grad,
        shift_grad,
        first_grad[:, :width],
        qkv_sum[:width],
        first_grad[:, width : 2 * width],
        qkv_sum[width : 2 * width],
        first_grad[:, 2 * width :],
        qkv_sum[2 * width :],
        out_grad,
        outer_bias_grad,
        up_grad,
        up_sum,
        down_grad,
        outer_bias_grad,
    )


def solution(mesh):
    tokens = P(("dp", "tensor"), None)
    down = P("dp", "tensor")
    across = P("tensor", "dp")
    part = P("tensor")
    return jax.shard_map(
        per_device,
        mesh=mesh,
        in_specs=(
            tokens,
            P("dp", None),
            P(),
            P(),
            down,
            part,
            down,
            part,
            down,
            part,
            across,
            P(),
            down,
            part,
            across,
            P(),
            tokens,
        ),
        out_specs=(
            tokens,
            tokens,
            P(),
            P(),
            down,
            part,
            down,
            part,
            down,
            part,
            across,
            P(),
            down,
            part,
            across,
            P(),
        ),
        check_vma=False,
    )
```

```python
import functools
import types

import jax
import jax.numpy as jnp
import numpy as np
from jax import lax
from jax.experimental import pallas as pl
from jax.experimental.pallas import tpu as pltpu
from jax.sharding import PartitionSpec as P

HEAD_DIM = 64
ROT = 32
SPAN = 256
EPS = 1e-05
F32 = jnp.float32
DP, TENSOR = "dp", "tensor"
BF16 = jnp.bfloat16
VMEM_BYTES = 60 * 2**20


def nn(a, b):
    return jnp.dot(a, b, preferred_element_type=F32)


def nt(a, b):
    return lax.dot_general(a, b, (((1,), (1,)), ((), ())), preferred_element_type=F32)


def tn(a, b):
    return lax.dot_general(a, b, (((0,), (0,)), ((), ())), preferred_element_type=F32)


def params(semantics):
    return pltpu.CompilerParams(dimension_semantics=semantics, vmem_limit_bytes=VMEM_BYTES)


def cost(flops, bytes_accessed, transcendentals=0):
    return pl.CostEstimate(
        flops=int(flops) // 10,
        bytes_accessed=int(bytes_accessed) // 10,
        transcendentals=int(transcendentals) // 10,
    )


def once(shape, index_map):
    return pl.BlockSpec(shape, index_map, pipeline_mode=pl.Buffered(1))


def rotary_tables(length):
    halves = ROT // 2
    exponent = jnp.arange(halves, dtype=F32) * (2.0 / ROT)
    frequency = jnp.power(10000.0, -exponent)
    angles = jnp.arange(length, dtype=F32)[:, None] * frequency[None, :]
    cos, sin = jnp.cos(angles), jnp.sin(angles)
    zero = jnp.zeros((length, halves), F32)
    rest = HEAD_DIM - ROT
    head = lambda a, b, fill: jnp.concatenate([a, b, jnp.full((length, rest), fill, F32)], axis=1)
    return tuple(
        jnp.concatenate([t, t], axis=1)
        for t in (head(cos, cos, 1.0), head(-sin, zero, 0.0), head(zero, sin, 0.0))
    )


def rotated(values, cos, low, high):
    halves = ROT // 2
    pieces = []
    for start in range(0, values.shape[1], 128):
        u = values[:, start : start + 128]
        pieces.append(
            u * cos + pltpu.roll(u, 128 - halves, 1) * low + pltpu.roll(u, halves, 1) * high
        )
    return pieces[0] if len(pieces) == 1 else jnp.concatenate(pieces, axis=1)


GELU_A = 0.7978845608028654
GELU_B = 0.044715


def gelu(v):
    return 0.5 * v * (1.0 + jnp.tanh(GELU_A * (v + GELU_B * (v * v * v))))


def gelu_slope(v):
    square = v * v
    half = 0.5 + 0.5 * jnp.tanh(v * (GELU_A + GELU_A * GELU_B * square))
    return half + (half - half * half) * (v * (2.0 * GELU_A + 6.0 * GELU_A * GELU_B * square))


def norm_kernel(x, gain, shift, out):
    values = x[...].astype(F32)
    centered = values - jnp.mean(values, axis=1, keepdims=True)
    scale = lax.rsqrt(jnp.mean(centered * centered, axis=1, keepdims=True) + EPS)
    out[...] = (centered * scale * gain[...] + shift[...]).astype(BF16)


def norm(x, gain, shift, tile=128):
    rows, depth = x.shape
    row = pl.BlockSpec((tile, depth), lambda i: (i, 0))
    one = once((1, depth), lambda i: (0, 0))
    return pl.pallas_call(
        norm_kernel,
        grid=(rows // tile,),
        in_specs=[row, one, one],
        out_specs=row,
        out_shape=jax.ShapeDtypeStruct((rows, depth), BF16),
        compiler_params=params(("arbitrary",)),
        cost_estimate=cost(10 * rows * depth, 4 * rows * depth),
        name="norm",
    )(x, gain, shift)


def closing_kernel(terms, flag, x, g, gain, bias, other_bias, second, up, *refs):
    parts, more, refs = refs[:terms], refs[terms : 2 * terms], refs[2 * terms :]
    input_grad, output, gain_sum, shift_sum, out_grad, down_grad, up_grad = refs

    @pl.when(pl.program_id(0) == 0)
    def _():
        gain_sum[...] = jnp.zeros_like(gain_sum)
        shift_sum[...] = jnp.zeros_like(shift_sum)
        width = out_grad.shape[0]
        out_grad[...] = second[:width, :].astype(F32)
        down_grad[...] = second[width:, :].astype(F32)

    def total(many):
        result = many[0][...].astype(F32)
        for part in many[1:]:
            term = part[...].astype(F32)
            if part is many[-1]:
                term = jnp.where(flag[0] == 1, term, 0.0)
            result = result + term
        return result

    up_grad[...] = up[...].astype(F32)
    values = x[...].astype(F32)
    output[...] = (
        values + total(more) + bias[...].astype(F32) + other_bias[...].astype(F32)
    ).astype(BF16)
    centered = values - jnp.mean(values, axis=1, keepdims=True)
    scale = lax.rsqrt(jnp.mean(centered * centered, axis=1, keepdims=True) + EPS)
    hat = centered * scale
    back = total(parts)
    gain_sum[...] += jnp.sum(back * hat, axis=0, keepdims=True)
    shift_sum[...] += jnp.sum(back, axis=0, keepdims=True)
    e = back * gain[...].astype(F32)
    inner = (
        e - jnp.mean(e, axis=1, keepdims=True) - hat * jnp.mean(e * hat, axis=1, keepdims=True)
    )
    input_grad[...] = (g[...].astype(F32) + inner * scale).astype(BF16)


def closing(flag, x, g, gain, bias, other_bias, second, up, width, parts, more, tile=128):
    rows, depth = x.shape
    row = pl.BlockSpec((tile, depth), lambda i, f: (i, 0))
    one = once((1, depth), lambda i, f: (0, 0))
    total = pl.BlockSpec((1, depth), lambda i, f: (0, 0))
    still = lambda shape: once(shape, lambda i, f: (0, 0))
    step = up.shape[0] // (rows // tile)
    ups = pl.BlockSpec((step, up.shape[1]), lambda i, f: (i, 0))
    inner, columns = second.shape
    return pl.pallas_call(
        functools.partial(closing_kernel, len(parts)),
        grid_spec=pltpu.PrefetchScalarGridSpec(
            num_scalar_prefetch=1,
            grid=(rows // tile,),
            in_specs=[row, row, one, one, one, still(second.shape), ups] + [row] * (2 * len(parts)),
            out_specs=[
                row,
                row,
                total,
                total,
                still((width, columns)),
                still((inner - width, columns)),
                ups,
            ],
        ),
        out_shape=[
            jax.ShapeDtypeStruct((rows, depth), BF16),
            jax.ShapeDtypeStruct((rows, depth), BF16),
            jax.ShapeDtypeStruct((1, depth), F32),
            jax.ShapeDtypeStruct((1, depth), F32),
            jax.ShapeDtypeStruct((width, columns), F32),
            jax.ShapeDtypeStruct((inner - width, columns), F32),
            jax.ShapeDtypeStruct(up.shape, F32),
        ],
        compiler_params=params(("arbitrary",)),
        cost_estimate=cost(30 * rows * depth, 14 * rows * depth),
        name="closing",
    )(flag, x, g, gain, bias, other_bias, second, up, *parts, *more)


MESH = pl.DeviceIdType.MESH
ANYWHERE = pl.BlockSpec(memory_space=pl.ANY)


def places():
    me = lax.axis_index(TENSOR)
    core, chip = lax.rem(me, 2), lax.div(me, 2)
    beside = chip + 1 - 2 * lax.rem(chip, 2)
    inner = jnp.logical_or(chip == 1, chip == 2)
    return types.SimpleNamespace(
        core=core,
        partner=me + 1 - 2 * core,
        beside=2 * beside + core,
        opposite=2 * (3 - chip) + core,
        inner=inner,
        outer=jnp.logical_not(inner),
        all=None,
    )


def greet(at, others=()):
    barrier = pltpu.get_barrier_semaphore()
    ids = [{TENSOR: getattr(at, name)} for name in ("partner", "beside", "opposite")] + list(others)
    for device in ids:
        pl.semaphore_signal(barrier, inc=1, device_id=device, device_id_type=MESH)
    pl.semaphore_wait(barrier, len(ids))


def to_device(src, dst, sent, got, device):
    return pltpu.make_async_remote_copy(
        src_ref=src,
        dst_ref=dst,
        send_sem=sent,
        recv_sem=got,
        device_id=device,
        device_id_type=MESH,
    )


def under(condition, act):
    if condition is None:
        act()
    else:
        pl.when(condition)(act)


def start_all(at, copies):
    for sender, _, copy in copies:
        under(getattr(at, sender), copy.start)


def finish_all(at, copies):
    for sender, receiver, copy in copies:
        under(getattr(at, receiver), copy.wait_recv)
        under(getattr(at, sender), copy.wait_send)


class Gather:
    MOVES = {
        1: (("all", "all", 3, 2, "beside"), ("inner", "inner", 3, 0, "opposite")),
        2: (("inner", "inner", 2, 1, "opposite"), ("inner", "outer", 0, 1, "beside")),
        3: (("inner", "outer", 1, 0, "beside"),),
        "own": (("all", "all", 3, 3, "partner"),),
        "first": (("all", "all", 2, 2, "partner"), ("inner", "inner", 0, 0, "partner")),
        "second": (("all", "all", 1, 1, "partner"),),
        "third": (("outer", "outer", 0, 0, "partner"),),
    }

    def __init__(self, *moves):
        self.moves = [(m, lo, hi) for name, lo, hi in moves for m in self.MOVES[name]]
        self.count = len(self.moves)

    def copies(self, at, full, sent, got):
        found = []
        for i, ((sender, receiver, src, dst, target), lo, hi) in enumerate(self.moves):
            rows = pl.ds(lo, hi - lo)
            found.append(
                (
                    sender,
                    receiver,
                    to_device(
                        full.at[src, at.core, rows],
                        full.at[dst, at.core, rows],
                        sent.at[i],
                        got.at[i],
                        {TENSOR: getattr(at, target)},
                    ),
                )
            )
        return found


class Riding:
    def __init__(self, ins, outs, aliased, count, copies, late=0):
        self.ins, self.outs, self.aliased, self.count, self.copies = ins, outs, aliased, count, copies
        self.late = late
        self.scratch, self.summed = [], None
        self.early, self.middle = 0, 0


def like(array):
    return jax.ShapeDtypeStruct(array.shape, array.dtype)


def gathering(full, *moves, late=(), early=(), middle=()):
    plan = Gather(*early, *moves, *middle, *late)

    def copies(at, ins, outs, sent, got):
        return plan.copies(at, outs[0], sent, got)

    ride = Riding([full], [like(full)], True, plan.count, copies, Gather(*late).count)
    ride.early, ride.middle = Gather(*early).count, Gather(*middle).count
    return ride


SENDS = {
    "in": ("outer", "inner", "beside"),
    "middle": ("inner", "inner", "opposite"),
    "side": ("all", "all", "beside"),
}


def sending(values, kind, lo, hi, into=None):
    sender, receiver, target = SENDS[kind]

    def copies(at, ins, outs, sent, got):
        rows = pl.ds(lo, hi - lo)
        copy = to_device(
            ins[0].at[rows], outs[0].at[rows], sent.at[0], got.at[0], {TENSOR: getattr(at, target)}
        )
        return [(sender, receiver, copy)]

    return Riding([values] + ([] if into is None else [into]), [like(values)], into is not None, 1, copies)


def summing(base, plus, kind, lo, hi, into=None, inner_only=False):
    sender, receiver, target = SENDS[kind]

    def copies(at, ins, outs, sent, got, total, other, sem):
        copy = to_device(
            total, outs[0].at[pl.ds(lo, hi - lo)], sent.at[0], got.at[0], {TENSOR: getattr(at, target)}
        )
        return [(sender, receiver, copy)]

    def summed(at, ins, total, other, sem):
        rows = pl.ds(lo, hi - lo)
        loads = [
            pltpu.make_async_copy(src.at[rows], dst, sem.at[n])
            for n, (src, dst) in enumerate(zip(ins[:2], (total, other)))
        ]

        def add():
            for load in loads:
                load.wait()

            @pl.loop(0, (hi - lo) // 32)
            def _(i):
                here = pl.ds(pl.multiple_of(i * 32, 32), 32)
                term = other[here, :].astype(F32)
                if inner_only:
                    term = jnp.where(at.inner, term, jnp.zeros_like(term))
                total[here, :] = (total[here, :].astype(F32) + term).astype(BF16)

        return loads, add

    ride = Riding(
        [base, plus] + ([] if into is None else [into]), [like(base)], into is not None, 1, copies
    )
    part = pltpu.VMEM((hi - lo, base.shape[1]), BF16)
    ride.scratch, ride.summed = [part, part, pltpu.SemaphoreType.DMA((2,))], summed
    return ride


def launch(body, args, ins, outs, shapes, grid, name, estimate, scratch=(), riding=(), ident=None, place=False, wait_for=(), lazy=(), seen=(), in_turn=False):
    if ident is None:
        return pl.pallas_call(
            functools.partial(body, lambda *which: None) if in_turn else body,
            grid=(grid,),
            in_specs=ins + [once(a.shape, lambda i, n=len(a.shape): (0,) * n) for a in lazy],
            out_specs=outs,
            out_shape=shapes,
            scratch_shapes=list(scratch),
            compiler_params=params(("arbitrary",)),
            cost_estimate=estimate,
            name=name,
        )(*args, *lazy)
    stage = types.SimpleNamespace(
        body=body,
        args=args,
        ins=ins,
        outs=outs,
        shapes=shapes,
        grid=grid,
        estimate=estimate,
        scratch=scratch,
        place=place,
        lazy=lazy,
        seen=seen,
        in_turn=in_turn,
    )
    if ident == "defer":
        return stage
    return chain([stage], name, riding, ident, wait_for)


class Made:
    def __init__(self, stage, output):
        self.at = stage, output


def chain(stages, name, riding, ident, wait_for=()):
    riding = list(riding) + [Riding([a], [], False, 1, lambda *_: []) for a in wait_for]
    plain = [[a for a in st.args if not isinstance(a, Made)] for st in stages]
    operands = [a for st, own in zip(stages, plain) for a in own + list(st.lazy)]
    shapes = [o for st in stages for o in st.shapes]
    scratch = [x for st in stages for x in st.scratch]
    lazies = [a for st in stages for a in st.lazy]
    extra_in = [a for r in riding for a in r.ins]
    extra_out = [o for r in riding for o in r.outs]
    aliases, n_in, n_out = {}, len(operands), len(shapes)
    for r in riding:
        if r.aliased:
            aliases[n_in + len(r.ins) - 1] = n_out
        n_in, n_out = n_in + len(r.ins), n_out + len(r.outs)

    def kernel(*refs):
        take = iter(refs)
        some = lambda n: [next(take) for _ in range(n)]
        own_ins, lazy_ins = [], []
        for st, own in zip(stages, plain):
            own_ins.append(some(len(own)))
            lazy_ins.append(some(len(st.lazy)))
        ride_ins = [some(len(r.ins)) for r in riding]
        own_outs = [some(len(st.shapes)) for st in stages]
        ride_outs = [some(len(r.outs)) for r in riding]
        own_scratch = [some(len(st.scratch)) for st in stages]
        loaded = [some(len(st.lazy)) for st in stages]
        loads = [
            [pltpu.make_async_copy(src, dst, some(1)[0]) for src, dst in zip(srcs, dsts)]
            for srcs, dsts in zip(lazy_ins, loaded)
        ]
        at = places()
        copies, middle, late, sums, early = [], [], [], [], []
        for r, i, o in zip(riding, ride_ins, ride_outs):
            sems, room = some(2), some(len(r.scratch))
            found = r.copies(at, i, o, *sems, *room)
            if r.summed is None:
                stop = len(found) - r.late
                early += found[: r.early]
                copies += found[r.early : stop - r.middle]
                middle += found[stop - r.middle : stop]
                late += found[stop:]
            else:
                sums.append((*r.summed(at, i, *room), found))
        for first, _, _ in sums:
            for load in first:
                load.start()
        for many in loads:
            for load in many:
                load.start()
        greet(at)
        start_all(at, early)
        start_all(at, copies)
        for _, add, found in sums:
            add()
            start_all(at, found)
            copies += found

        for k, st in enumerate(stages):
            if k == 1 and middle:
                finish_all(at, early)
                start_all(at, middle)
                early, copies = [], copies + middle
            own = iter(own_ins[k])
            sources = [
                own_outs[a.at[0]][a.at[1]] if isinstance(a, Made) else next(own) for a in st.args
            ]

            def ready(*which, k=k):
                @pl.when(pl.program_id(0) == 0)
                def _():
                    for n in which:
                        loads[k][n].wait()

            def step(*blocks, k=k, st=st, ready=ready):
                if not st.in_turn:
                    ready(*range(len(loads[k])))
                n_blocks = len(st.args) + len(st.seen)
                st.body(
                    *([at] if st.place else []),
                    *([ready] if st.in_turn else []),
                    *blocks[:n_blocks],
                    *loaded[k],
                    *blocks[n_blocks:],
                    *own_scratch[k],
                )

            if st.shapes:
                pltpu.emit_pipeline(
                    step,
                    grid=(st.grid,),
                    in_specs=st.ins + [spec for _, spec in st.seen],
                    out_specs=st.outs,
                )(*sources, *(ride_outs[r][0] for r, _ in st.seen), *own_outs[k])
        finish_all(at, early)
        finish_all(at, copies)
        start_all(at, late)
        finish_all(at, late)

    return pl.pallas_call(
        kernel,
        in_specs=[ANYWHERE] * (len(operands) + len(extra_in)),
        out_specs=[ANYWHERE] * (len(shapes) + len(extra_out)),
        out_shape=shapes + extra_out,
        input_output_aliases=aliases,
        scratch_shapes=scratch
        + [pltpu.VMEM(a.shape, a.dtype) for a in lazies]
        + [pltpu.SemaphoreType.DMA] * len(lazies)
        + [
            entry
            for r in riding
            for entry in [pltpu.SemaphoreType.DMA((r.count,))] * 2 + r.scratch
        ],
        compiler_params=pltpu.CompilerParams(
            vmem_limit_bytes=VMEM_BYTES, collective_id=ident, has_side_effects=True
        ),
        cost_estimate=stages[0].estimate,
        name=name,
    )(*operands, *extra_in)


def opening_kernel(tile, groups, width, cut, *refs):
    x, gain, shift, g, *weights = refs[:10]
    biases, frequency, refs = refs[10:14], refs[14], refs[15:]
    rows_full, g_full, first_full, second_full, q, k, v, active, hidden, cos, low, high = refs[:12]
    g_sum, refs = refs[12], refs[13:]
    own, kept, first_kept, second_kept, w, bias, x_tile = refs[:7]
    staged, (local, x_sem, out_sem, w_sent, w_got), sems = refs[7:12], refs[12:17], refs[17:]
    at = places()
    core, dp = at.core, lax.axis_index(DP)
    peers = [{DP: jnp.bitwise_xor(dp, step)} for step in range(1, groups)]
    share, depth = own.shape
    half = share // 2
    units = hidden.shape[1]
    lows, highs = (0, half), (half, share)
    greet(at, peers)

    across = second_kept.shape[1]
    mine = pl.ds(pl.multiple_of(dp * across, across), across)
    columns = [(0, width), (width, width), (2 * width, width), (3 * width, units)]
    loads = [
        pltpu.make_async_copy(src, first_kept.at[:, pl.ds(start, size)], local.at[i])
        for i, (src, (start, size)) in enumerate(zip(weights[:4], columns))
    ] + [
        pltpu.make_async_copy(weights[4], second_kept.at[pl.ds(0, width)], local.at[4]),
        pltpu.make_async_copy(weights[5], second_kept.at[pl.ds(width, units)], local.at[5]),
        pltpu.make_async_copy(g, kept, local.at[6]),
    ]
    stores = [
        pltpu.make_async_copy(first_kept, first_full.at[dp], local.at[0]),
        pltpu.make_async_copy(second_kept, second_full.at[:, mine], local.at[1]),
        pltpu.make_async_copy(kept, g_full.at[3, core], local.at[2]),
        pltpu.make_async_copy(own, rows_full.at[3, core], local.at[7]),
    ]
    spread = [
        [to_device(src, dst, w_sent.at[n, i], w_got.at[n, i], peer) for i, peer in enumerate(peers)]
        for n, (src, dst) in enumerate(
            ((first_kept, first_full.at[dp]), (second_kept, second_full.at[:, mine]))
        )
    ]
    plans = dict(
        n1_low=[(1, *lows)],
        n1_high=[(1, *highs), ("own", 0, share)],
        n2_low=[(2, *lows)],
        n2_high=[(2, *highs)],
        e2_low=[("first", *lows)],
        e2_high=[("first", *highs)],
        n3_low=[(3, *lows)],
        n3_high=[(3, *highs)],
        e1_low=[("second", *lows)],
        e1_high=[("second", *highs)],
        e0_low=[("third", *lows)],
        e0_high=[("third", *highs)],
        g_own=[("own", 0, share)],
        g1=[(1, 0, cut)],
    )
    moves = {
        name: Gather(*plan).copies(
            at, g_full if name[0] == "g" else rows_full, sems[2 * i], sems[2 * i + 1]
        )
        for i, (name, plan) in enumerate(plans.items())
    }

    def start(*names):
        for name in names:
            start_all(at, moves[name])

    def finish(*names):
        for name in names:
            finish_all(at, moves[name])

    for copy in loads:
        copy.start()

    @pl.loop(0, share // tile)
    def _(i):
        rows = pl.ds(pl.multiple_of(i * tile, tile), tile)
        values = x[rows, :].astype(F32)
        centered = values - jnp.mean(values, axis=1, keepdims=True)
        scale = lax.rsqrt(jnp.mean(centered * centered, axis=1, keepdims=True) + EPS)
        own[rows, :] = (
            centered * scale * gain[...].astype(F32) + shift[...].astype(F32)
        ).astype(BF16)

    stores[3].start()
    for copy in loads:
        copy.wait()
    for copy in spread[0]:
        copy.start()
    for copy in stores[:3]:
        copy.start()
    stores[3].wait()
    start("n1_low", "n1_high")

    lane = lax.broadcasted_iota(jnp.int32, (1, 128), 1) % HEAD_DIM
    position = lax.broadcasted_iota(jnp.int32, cos.shape, 0).astype(F32)
    angle = position * frequency[...]
    sine = jnp.sin(angle)
    cos[...] = jnp.where(lane < ROT, jnp.cos(angle), 1.0)
    low[...] = jnp.where(lane < ROT // 2, -sine, 0.0)
    high[...] = jnp.where(jnp.logical_and(lane >= ROT // 2, lane < ROT), sine, 0.0)
    for ref, (begin, size) in zip(biases, columns):
        bias[:, begin : begin + size] = ref[...].astype(F32)
    g_sum[...] = jnp.zeros_like(g_sum)

    @pl.loop(0, share // tile)
    def _(i):
        rows = pl.ds(pl.multiple_of(i * tile, tile), tile)
        g_sum[...] += jnp.sum(kept[rows, :].astype(F32), axis=0, keepdims=True)

    for copy in stores[:3]:
        copy.wait()
    start("g_own")
    for copy in spread[1]:
        copy.start()
    finish("n1_low")
    start("n2_low", "e2_low")
    finish("n1_high")
    start("n2_high", "e2_high")
    finish("n2_low")
    start("n3_low", "e1_low")
    for copy in spread[0]:
        copy.wait()
    fetch = [
        pltpu.make_async_copy(
            first_full.at[d], w.at[pl.ds(d * first_full.shape[1], first_full.shape[1])], local.at[d]
        )
        for d in range(groups)
    ]
    for copy in fetch:
        copy.start()
    for copy in fetch:
        copy.wait()

    outs = (q, k, v, active, hidden)

    def results(i):
        part = jnp.where(lax.rem(i, 2) == 0, core, 1 - core)
        slot = 3 - lax.div(i, 2)
        rows = pl.ds(pl.multiple_of((2 * slot + part) * share, share), share)
        return [
            pltpu.make_async_copy(src.at[lax.rem(i, 2)], dst.at[rows], out_sem.at[lax.rem(i, 2), n])
            for n, (src, dst) in enumerate(zip(staged, outs))
        ]

    @pl.loop(0, 8)
    def _(i):
        @pl.when(i == 2)
        def _():
            finish("n2_high")
            start("n3_high", "e1_high")
            finish("e2_low", "e2_high")

        @pl.when(i == 4)
        def _():
            finish("e1_low", "e1_high")

        @pl.when(i == 6)
        def _():
            finish("n3_low")
            start("e0_low")
            finish("n3_high")
            start("e0_high")
            finish("g_own")
            start("g1")

        @pl.when(i == 7)
        def _():
            finish("e0_low", "e0_high")

        part = jnp.where(lax.rem(i, 2) == 0, core, 1 - core)
        load = pltpu.make_async_copy(rows_full.at[3 - lax.div(i, 2), part], x_tile, x_sem)
        load.start()

        @pl.when(i >= 2)
        def _():
            for copy in results(i - 2):
                copy.wait()

        load.wait()
        here = pl.ds(pl.multiple_of(part * share, share), share)
        project_tile(
            width,
            x_tile,
            w,
            bias,
            cos.at[here],
            low.at[here],
            high.at[here],
            *(r.at[lax.rem(i, 2)] for r in staged),
        )
        for copy in results(i):
            copy.start()

    for i in (6, 7):
        for copy in results(i):
            copy.wait()
    finish("g1")
    for copy in spread[1]:
        copy.wait()


OPENING_PLANS = (2, 3, 2, 2, 2, 2, 1, 1, 1, 1, 1, 1, 1, 2)


def opening(ident, x, gain, shift, g, weights, biases, groups, length, cut, tile=64):
    rows, depth = x.shape
    width, units = weights[0].shape[1], weights[3].shape[1]
    total = 3 * width + units
    inner = width + units
    columns = weights[4].shape[1]
    everything = 8 * rows
    whole = pl.BlockSpec(memory_space=pltpu.VMEM)
    full = jax.ShapeDtypeStruct((4, 2, rows, depth), BF16)
    exponent = np.arange(ROT // 2, dtype=np.float32) * np.float32(2.0 / ROT)
    frequency = np.tile(np.power(np.float32(10000.0), -exponent), 8)[None, :]
    table = jax.ShapeDtypeStruct((length, 128), F32)
    narrow = jax.ShapeDtypeStruct((everything, width), BF16)
    return pl.pallas_call(
        functools.partial(opening_kernel, tile, groups, width, cut),
        in_specs=[whole] * 3 + [ANYWHERE] * 7 + [whole] * 5,
        out_specs=[ANYWHERE] * 9 + [whole] * 4,
        out_shape=[
            full,
            full,
            jax.ShapeDtypeStruct((groups, depth // groups, total), BF16),
            jax.ShapeDtypeStruct((inner, groups * columns), BF16),
            narrow,
            narrow,
            narrow,
            jax.ShapeDtypeStruct((everything, units), BF16),
            jax.ShapeDtypeStruct((everything, units), F32),
            table,
            table,
            table,
            jax.ShapeDtypeStruct((1, depth), F32),
        ],
        scratch_shapes=[
            pltpu.VMEM((rows, depth), BF16),
            pltpu.VMEM((rows, depth), BF16),
            pltpu.VMEM((depth // groups, total), BF16),
            pltpu.VMEM((inner, columns), BF16),
            pltpu.VMEM((depth, total), BF16),
            pltpu.VMEM((1, total), F32),
            pltpu.VMEM((rows, depth), BF16),
            pltpu.VMEM((2, rows, width), BF16),
            pltpu.VMEM((2, rows, width), BF16),
            pltpu.VMEM((2, rows, width), BF16),
            pltpu.VMEM((2, rows, units), BF16),
            pltpu.VMEM((2, rows, units), F32),
            pltpu.SemaphoreType.DMA((8,)),
            pltpu.SemaphoreType.DMA,
            pltpu.SemaphoreType.DMA((2, 5)),
            pltpu.SemaphoreType.DMA((2, groups - 1)),
            pltpu.SemaphoreType.DMA((2, groups - 1)),
        ]
        + [pltpu.SemaphoreType.DMA((n,)) for n in OPENING_PLANS for _ in range(2)],
        compiler_params=pltpu.CompilerParams(
            vmem_limit_bytes=VMEM_BYTES, collective_id=ident, has_side_effects=True
        ),
        cost_estimate=cost(2 * everything * depth * total, 60 * rows * depth),
        name="opening",
    )(x, gain, shift, g, *weights, *biases, jnp.asarray(frequency))


def project_tile(width, x, w, bias, cos, low, high, q, k, v, active, hidden):
    rows = x[...]
    tables = (cos[...], low[...], high[...])
    q[...] = (
        rotated(nn(rows, w[:, :width]) + bias[:, :width], *tables).astype(BF16)
        * jnp.asarray(HEAD_DIM**-0.5, BF16)
    )
    k[...] = rotated(
        nn(rows, w[:, width : 2 * width]) + bias[:, width : 2 * width], *tables
    ).astype(BF16)
    v[...] = (nn(rows, w[:, 2 * width : 3 * width]) + bias[:, 2 * width : 3 * width]).astype(BF16)
    units = hidden.shape[1]
    step = min(256, units)
    for start in range(0, units, step):
        at = slice(3 * width + start, 3 * width + start + step)
        h = nn(rows, w[:, at]) + bias[:, at]
        hidden[:, start : start + step] = h
        active[:, start : start + step] = gelu(h).astype(BF16)


def project(x, w, bias, tables, width, units, length, riding=(), ident=None, tile=512):
    rows, depth = x.shape
    per = length // tile
    row = lambda n: pl.BlockSpec((tile, n), lambda i: (i, 0))
    table = pl.BlockSpec((tile, 128), lambda i: (i % per, 0))
    total = 3 * width + units
    return launch(
        functools.partial(project_tile, width),
        [x, w, bias, *tables],
        [
            row(depth),
            once((depth, total), lambda i: (0, 0)),
            once((1, total), lambda i: (0, 0)),
            table,
            table,
            table,
        ],
        [row(width), row(width), row(width), row(units), row(units)],
        [jax.ShapeDtypeStruct((rows, width), BF16)] * 3
        + [jax.ShapeDtypeStruct((rows, units), BF16), jax.ShapeDtypeStruct((rows, units), F32)],
        rows // tile,
        "project",
        cost(2 * rows * depth * total, 2 * depth * (rows + total) + rows * units * 6),
        riding=riding,
        ident=ident,
    )


def each_tile_kernel(body, *refs):
    body(*refs)


def each_tile(body, arrays, w, depth, name, tile=512):
    rows = arrays[0].shape[0]
    return pl.pallas_call(
        functools.partial(each_tile_kernel, body),
        grid=(rows // tile,),
        in_specs=[pl.BlockSpec((tile, a.shape[1]), lambda i: (i, 0)) for a in arrays]
        + [once(w.shape, lambda i, n=len(w.shape): (0,) * n)],
        out_specs=pl.BlockSpec((tile, depth), lambda i: (i, 0)),
        out_shape=jax.ShapeDtypeStruct((rows, depth), BF16),
        compiler_params=params(("arbitrary",)),
        cost_estimate=cost(2 * w.size * rows, 2 * rows * depth),
        name=name,
    )(*arrays, w)


def core_sum_body(body, count, pieces, n_in, at, *refs):
    ins, w, outs = refs[:n_in], refs[n_in], refs[n_in + 1 : n_in + 1 + count]
    sent, got, value, send_sem, got_sem = refs[n_in + 1 + count :]
    slot = pl.program_id(0)
    core = at.core
    share = sent.shape[1]
    piece = share // pieces

    def term(owner, i, to):
        rows = pl.ds(pl.multiple_of(owner * share + i * piece, piece), piece)
        body(*(r.at[rows, :] for r in ins), w, to)

    def copy(i):
        rows = pl.ds(i * piece, piece)
        return to_device(
            sent.at[slot, rows],
            got.at[slot, rows],
            send_sem.at[slot, i],
            got_sem.at[slot, i],
            {TENSOR: at.partner},
        )

    for i in range(pieces):
        term(1 - core, i, sent.at[slot, pl.ds(i * piece, piece)])
        copy(i).start()
    for i in range(pieces):
        rows = pl.ds(i * piece, piece)
        term(core, i, value)
        copy(i).wait_recv()
        for n, out in enumerate(outs):

            @pl.when(slot == n)
            def _(out=out):
                out[rows, :] = (value[...] + got[slot, rows].astype(F32)).astype(BF16)

    for i in range(pieces):
        copy(i).wait_send()


def core_sum_parts(count, pieces, length, depth):
    share = length // 2
    out = pl.BlockSpec((share, depth), lambda i: (0, 0), pipeline_mode=pl.Buffered(1))
    return (
        [out] * count,
        [jax.ShapeDtypeStruct((share, depth), BF16)] * count,
        [
            pltpu.VMEM((count, share, depth), BF16),
            pltpu.VMEM((count, share, depth), BF16),
            pltpu.VMEM((share // pieces, depth), F32),
            pltpu.SemaphoreType.DMA((count, pieces)),
            pltpu.SemaphoreType.DMA((count, pieces)),
        ],
    )


def core_sum(body, ident, count, length, arrays, w, depth, name, pieces=2, riding=()):
    outs, shapes, scratch = core_sum_parts(count, pieces, length, depth)
    size = sum(a.shape[1] for a, _ in arrays)
    return launch(
        functools.partial(core_sum_body, body, count, pieces, len(arrays)),
        [a for a, _ in arrays],
        [pl.BlockSpec((length, a.shape[1]), lambda i, f=f: (f + i, 0)) for a, f in arrays],
        outs,
        shapes,
        count,
        name,
        cost(2 * count * length * size * depth, 2 * count * length * (size + depth) + 2 * size * depth),
        scratch=scratch,
        riding=riding,
        ident=ident,
        place=True,
        lazy=[w],
    )


def mix_body(attended, active, w, out):
    width, depth = attended.shape[1], w.shape[1]
    step = min(512, depth)
    for start in range(0, depth, step):
        at = slice(start, start + step)
        out[:, at] = (nn(attended[...], w[:width, at]) + nn(active[...], w[width:, at])).astype(
            out.dtype
        )


def unproject_body(qkv_grad, hidden_grad, w, out):
    three = qkv_grad.shape[1]
    depth = w.shape[0]
    step = min(512, depth)
    for start in range(0, depth, step):
        out[:, start : start + step] = (
            nt(qkv_grad[...], w[start : start + step, :three])
            + nt(hidden_grad[...], w[start : start + step, three:])
        ).astype(out.dtype)


def unmix_tile(hidden, g, w, attended_grad, hidden_grad, sums):
    width = attended_grad.shape[1]
    units = hidden.shape[1]

    @pl.when(pl.program_id(0) == 0)
    def _():
        sums[...] = jnp.zeros_like(sums)

    rows = g[...]
    attended_grad[...] = nt(rows, w[:width, :]).astype(BF16)
    step = min(256, units)
    for start in range(0, units, step):
        at = slice(start, start + step)
        back = nt(rows, w[width + start : width + start + step, :])
        low = (back * gelu_slope(hidden[:, at])).astype(BF16)
        hidden_grad[:, at] = low
        sums[:, at] += jnp.sum(low.astype(F32), axis=0, keepdims=True)


def unmix(g, w, hidden, width, first, count, length, riding=(), ident=None, tile=512):
    rows = count * length
    units = hidden.shape[1]
    inner, depth = w.shape
    per = length // tile
    row = lambda n: pl.BlockSpec((tile, n), lambda i: (i, 0))
    late = lambda n: pl.BlockSpec((tile, n), lambda i: (first * per + i, 0))
    seen = []
    if g is None:
        seen = [
            (0, pl.BlockSpec((None, None, tile, depth), lambda i: (first + i // 2, i % 2, 0, 0)))
        ]
    return launch(
        unmix_tile,
        [hidden] + ([] if g is None else [g]),
        [late(units)] + ([] if g is None else [late(depth)]),
        [row(width), row(units), pl.BlockSpec((1, units), lambda i: (0, 0))],
        [
            jax.ShapeDtypeStruct((rows, width), BF16),
            jax.ShapeDtypeStruct((rows, units), BF16),
            jax.ShapeDtypeStruct((1, units), F32),
        ],
        rows // tile,
        "unmix",
        cost(2 * rows * inner * depth, 2 * depth * (rows + inner) + rows * units * 6),
        riding=riding,
        ident=ident,
        lazy=[w],
        seen=seen,
    )


def outer_rows_kernel(ready, x, *refs):
    parts, out = refs[:-1], refs[-1]
    total, start = None, 0
    for n, part in enumerate(parts):
        ready(n)
        term = tn(x[start : start + part.shape[0], :], part[...])
        total = term if total is None else total + term
        start += part.shape[0]
    out[...] = total.astype(out.dtype)


def outer_rows(x, parts, riding=(), ident=None, tile=256, wait_for=()):
    rows, depth = x.shape
    n = parts[0].shape[1]
    return launch(
        outer_rows_kernel,
        [x],
        [pl.BlockSpec((rows, tile), lambda i: (0, i))],
        [pl.BlockSpec((tile, n), lambda i: (i, 0))],
        [jax.ShapeDtypeStruct((depth, n), BF16)],
        depth // tile,
        "outer_rows",
        cost(2 * rows * depth * n, 2 * (rows * (depth + n) + depth * n)),
        riding=riding,
        ident=ident,
        wait_for=wait_for,
        lazy=parts,
        in_turn=True,
    )


def outer_columns_kernel(ready, g, *refs):
    many, b, out = refs[:-2], refs[-2], refs[-1]
    width = many[0].shape[1]
    total, start = None, 0
    for n, a in enumerate(many):
        ready(n)
        term = tn(a[...], g[start : start + a.shape[0], :])
        total = term if total is None else total + term
        start += a.shape[0]
    out[0, :width, :] = total.astype(out.dtype)
    ready(len(many))
    out[0, width:, :] = tn(b[...], g[...]).astype(out.dtype)


def outer_columns(many, b, g, parts, riding=(), ident=None, tile=512):
    rows, depth = g.shape
    width, units = many[0].shape[1], b.shape[1]
    across = depth // parts
    tile = min(tile, across)
    per = across // tile
    return launch(
        outer_columns_kernel,
        [g],
        [pl.BlockSpec((rows, tile), lambda i: (0, i))],
        [pl.BlockSpec((1, width + units, tile), lambda i: (i // per, 0, i % per))],
        [jax.ShapeDtypeStruct((parts, width + units, across), BF16)],
        depth // tile,
        "outer_columns",
        cost(2 * rows * depth * (width + units), 2 * (rows * (depth + width + units) + depth * (width + units))),
        riding=riding,
        ident=ident,
        lazy=list(many) + [b],
        in_turn=True,
    )


def head_lanes(width, head):
    return lax.broadcasted_iota(jnp.int32, (1, width), 1) // HEAD_DIM == head


def attend_kernel(q, k, v, column_ids, row_ids, out, log_sums):
    length, width = q.shape
    heads = width // HEAD_DIM
    tile = min(SPAN, length)
    lanes = lax.broadcasted_iota(jnp.int32, (1, 128), 1)
    for begin in range(0, length, tile):
        end = min(length, begin + tile + SPAN)
        q_ids = column_ids[begin : begin + tile, :]
        blocked = row_ids[:, begin:end] > q_ids
        rows = q[begin : begin + tile, :]

        def one_head(head, carry):
            total, sums = carry
            mine = head_lanes(width, head)
            scores = nt(jnp.where(mine, rows, jnp.zeros_like(rows)), k[:end, :])
            tail = jnp.where(blocked, -1e9, scores[:, begin:])
            scores = jnp.concatenate([scores[:, :begin], tail], axis=1) if begin else tail
            highest = jnp.max(scores, axis=1, keepdims=True)
            powers = jnp.exp(scores - highest)
            amount = jnp.sum(powers, axis=1, keepdims=True)
            low = (powers * (1.0 / amount)).astype(BF16)
            total = jnp.where(mine, nn(low, v[:end, :]), total)
            sums = jnp.where(lanes == head, highest + jnp.log(amount), sums)
            return total, sums

        total, sums = jnp.zeros((tile, width), F32), jnp.zeros((tile, 128), F32)
        for head in range(heads):
            total, sums = one_head(head, (total, sums))
        out[begin : begin + tile, :] = total.astype(BF16)
        log_sums[:, begin : begin + tile] = sums.T[:8, :]


def attend(first, count, q, k, v, column_ids, row_ids, riding=(), ident=None):
    width = q.shape[1]
    length = row_ids.shape[2]
    rows, seqs = count * length, count
    heads = width // HEAD_DIM
    seq = pl.BlockSpec((length, width), lambda s: (first + s, 0))
    out = pl.BlockSpec((length, width), lambda s: (s, 0))
    return launch(
        attend_kernel,
        [q, k, v, column_ids, row_ids],
        [
            seq,
            seq,
            seq,
            pl.BlockSpec((length, 1), lambda s: (first + s, 0)),
            pl.BlockSpec((None, 1, length), lambda s: (first + s, 0, 0)),
        ],
        [out, pl.BlockSpec((8, length), lambda s: (0, s))],
        [jax.ShapeDtypeStruct((rows, width), BF16), jax.ShapeDtypeStruct((8, rows), F32)],
        seqs,
        "attend",
        cost(8 * seqs * heads * length * length * 256 * 0.8, 8 * rows * width, seqs * heads * length**2),
        riding=riding,
        ident=ident,
    )


def unattend_kernel(
    q, k, v, g, log_sums, column_ids, row_ids, cos, low, high, out, sums, key_total, value_total
):
    length, width = q.shape
    heads = width // HEAD_DIM
    tile = min(SPAN, length)
    tables = (cos[...], -low[...], -high[...])

    @pl.when(pl.program_id(0) == 0)
    def _():
        sums[...] = jnp.zeros_like(sums)

    key_total[...] = jnp.zeros_like(key_total)
    value_total[...] = jnp.zeros_like(value_total)

    def products(begin, head):
        end, at = min(length, begin + tile + SPAN), slice(begin, begin + tile)
        mine = head_lanes(width, head)
        q_rows, g_rows = q[at, :], g[at, :]
        q_head = jnp.where(mine, q_rows, jnp.zeros_like(q_rows))
        g_head = jnp.where(mine, g_rows, jnp.zeros_like(g_rows))
        return q_head, g_head, nt(k[:end, :], q_head), nt(v[:end, :], g_head)

    steps = [(begin, head) for begin in range(0, length, tile) for head in range(heads)]
    ahead = products(*steps[0])
    query_total = None
    for n, (begin, head) in enumerate(steps):
        q_head, g_head, scores, prob_grad = ahead
        if n + 1 < len(steps):
            ahead = products(*steps[n + 1])
        end, at = min(length, begin + tile + SPAN), slice(begin, begin + tile)
        blocked = column_ids[begin:end, :] > row_ids[:, at]
        tail = jnp.where(blocked, -1e9, scores[begin:, :])
        scores = jnp.concatenate([scores[:begin, :], tail], axis=0) if begin else tail
        probs = jnp.exp(scores - log_sums[head : head + 1, at])
        value_total[:end, :] += nn(probs.astype(BF16), g_head)
        inner = jnp.sum(prob_grad * probs, axis=0, keepdims=True)
        score_grad = (probs * (prob_grad - inner)).astype(BF16)
        key_total[:end, :] += nn(score_grad, q_head)
        part = tn(score_grad, k[:end, :])
        query_total = jnp.where(
            head_lanes(width, head), part, query_total if head else jnp.zeros_like(part)
        )
        if head == heads - 1:
            turned = rotated(query_total * HEAD_DIM**-0.5, *(t[at, :] for t in tables)).astype(BF16)
            out[at, :width] = turned
            sums[:, :width] += jnp.sum(turned.astype(F32), axis=0, keepdims=True)
    turned = rotated(key_total[...], *tables).astype(BF16)
    out[:, width : 2 * width] = turned
    sums[:, width : 2 * width] += jnp.sum(turned.astype(F32), axis=0, keepdims=True)
    turned = value_total[...].astype(BF16)
    out[:, 2 * width :] = turned
    sums[:, 2 * width :] += jnp.sum(turned.astype(F32), axis=0, keepdims=True)


def unattend(first, count, q, k, v, g, g_first, log_sums, sums_first, column_ids, row_ids, tables, riding=(), ident=None, wait_for=()):
    width = q.shape[1]
    length = row_ids.shape[2]
    rows, seqs = count * length, count
    heads = width // HEAD_DIM
    seq = pl.BlockSpec((length, width), lambda s: (first + s, 0))
    table = once((length, 128), lambda s: (0, 0))
    return launch(
        unattend_kernel,
        [q, k, v, g, log_sums, column_ids, row_ids, *tables],
        [
            seq,
            seq,
            seq,
            pl.BlockSpec((length, width), lambda s: (g_first + s, 0)),
            pl.BlockSpec((8, length), lambda s: (0, sums_first + s)),
            pl.BlockSpec((length, 1), lambda s: (first + s, 0)),
            pl.BlockSpec((None, 1, length), lambda s: (first + s, 0, 0)),
            table,
            table,
            table,
        ],
        [
            pl.BlockSpec((length, 3 * width), lambda s: (s, 0)),
            pl.BlockSpec((1, 3 * width), lambda s: (0, 0)),
        ],
        [jax.ShapeDtypeStruct((rows, 3 * width), BF16), jax.ShapeDtypeStruct((1, 3 * width), F32)],
        count,
        "unattend",
        cost(20 * seqs * heads * length * length * 256 * 0.8, 14 * rows * width, seqs * heads * length**2),
        scratch=[pltpu.VMEM((length, width), F32), pltpu.VMEM((length, width), F32)],
        riding=riding,
        ident=ident,
        wait_for=wait_for,
    )


def attend_mix_body(count, pieces, at, q, k, v, column_ids, row_ids, active, w, out, log_sums, *refs):
    attend_kernel(q, k, v, column_ids, row_ids, out, log_sums)
    core_sum_body(mix_body, count, pieces, 2, at, out, active, w, *refs)


def attend_mix(first, count, q, k, v, column_ids, row_ids, active, w, riding, ident, pieces=2):
    width, units = q.shape[1], active.shape[1]
    length = row_ids.shape[2]
    depth = w.shape[1]
    rows, heads = count * length, width // HEAD_DIM
    here = lambda n: pl.BlockSpec((length, n), lambda s: (first + s, 0))
    outs, shapes, scratch = core_sum_parts(count, pieces, length, depth)
    return launch(
        functools.partial(attend_mix_body, count, pieces),
        [q, k, v, column_ids, row_ids, active],
        [
            here(width),
            here(width),
            here(width),
            here(1),
            pl.BlockSpec((None, 1, length), lambda s: (first + s, 0, 0)),
            here(units),
        ],
        [pl.BlockSpec((length, width), lambda s: (s, 0)), pl.BlockSpec((8, length), lambda s: (0, s))]
        + outs,
        [jax.ShapeDtypeStruct((rows, width), BF16), jax.ShapeDtypeStruct((8, rows), F32)] + shapes,
        count,
        "attend_mix",
        cost(8 * rows * heads * length * 256 * 0.8, 8 * rows * width, rows * heads * length),
        scratch=scratch,
        riding=riding,
        ident=ident,
        place=True,
        lazy=[w],
    )


def unattend_unproject_body(pieces, at, *refs):
    operands, hidden_grad, w, (out, sums, part), scratch = (
        refs[:10],
        refs[10],
        refs[11],
        refs[12:15],
        refs[15:],
    )
    unattend_kernel(*operands, out, sums, *scratch[:2])
    core_sum_body(unproject_body, 1, pieces, 2, at, out, hidden_grad, w, part, *scratch[2:])


def unattend_unproject(
    at, q, k, v, g, g_at, log_sums, sums_at, column_ids, row_ids, tables, hidden_grad, hidden_at, w, riding, ident, pieces=2
):
    width = q.shape[1]
    units = w.shape[1] - 3 * width
    length = row_ids.shape[2]
    depth = w.shape[0]
    heads = width // HEAD_DIM
    here = lambda n, at: pl.BlockSpec((length, n), lambda s: (at, 0))
    table = pl.BlockSpec((length, 128), lambda s: (0, 0))
    outs, shapes, scratch = core_sum_parts(1, pieces, length, depth)
    return launch(
        functools.partial(unattend_unproject_body, pieces),
        [q, k, v, g, log_sums, column_ids, row_ids, *tables, hidden_grad],
        [
            here(width, at),
            here(width, at),
            here(width, at),
            here(width, g_at),
            pl.BlockSpec((8, length), lambda s: (0, sums_at)),
            here(1, at),
            pl.BlockSpec((None, 1, length), lambda s: (at, 0, 0)),
            table,
            table,
            table,
            here(units, hidden_at),
        ],
        [
            pl.BlockSpec((length, 3 * width), lambda s: (0, 0)),
            pl.BlockSpec((1, 3 * width), lambda s: (0, 0)),
        ]
        + outs,
        [
            jax.ShapeDtypeStruct((length, 3 * width), BF16),
            jax.ShapeDtypeStruct((1, 3 * width), F32),
        ]
        + shapes,
        1,
        "unattend_unproject",
        cost(20 * heads * length * length * 256 * 0.8, 14 * length * width, heads * length**2),
        scratch=[pltpu.VMEM((length, width), F32), pltpu.VMEM((length, width), F32)] + scratch,
        riding=riding,
        ident=ident,
        place=True,
        lazy=[w],
    )


def nothing():
    pass


def add_up(*parts):
    total = parts[0].astype(F32)
    for part in parts[1:]:
        total = total + part.astype(F32)
    return total.astype(BF16)


def after(values, *others):
    return lax.optimization_barrier((values,) + others)[0]


def sum_everywhere_kernel(groups, members, counts, *refs):
    vectors, refs = refs[:3], refs[3:]
    narrows = []
    for count in counts:
        narrows.append(refs[:count])
        refs = refs[count:]
    wide, narrow, buf, in_dp, in_tensor, send_dp, got_dp, send_tensor, got_tensor = refs
    dp, tensor = lax.axis_index(DP), lax.axis_index(TENSOR)
    mesh = pl.DeviceIdType.MESH
    barrier = pltpu.get_barrier_semaphore()
    for step in range(1, groups):
        pl.semaphore_signal(barrier, inc=1, device_id={DP: lax.rem(dp + step, groups)}, device_id_type=mesh)
    for step in range(1, members):
        pl.semaphore_signal(barrier, inc=1, device_id={TENSOR: lax.rem(tensor + step, members)}, device_id_type=mesh)
    pl.semaphore_wait(barrier, groups + members - 2)
    lanes = buf.shape[2] // 4
    for k, ref in enumerate(vectors):
        for r in range(8):
            buf[0, r : r + 1, k * lanes : (k + 1) * lanes] = ref[:, r * lanes : (r + 1) * lanes]
    row = 0
    buf[0, :, 3 * lanes :] = jnp.zeros((8, lanes), F32)
    for many in narrows:
        for start in range(0, many[0].shape[1], lanes):
            term = many[0][:, start : start + lanes]
            for ref in many[1:]:
                term = term + ref[:, start : start + lanes]
            buf[0, row : row + 1, 3 * lanes :] = term
            row += 1

    def exchange(axis, me, size, source, into, send, got):
        copies = []
        for step in range(1, size):
            copies.append(
                pltpu.make_async_remote_copy(
                    src_ref=source,
                    dst_ref=into.at[step - 1],
                    send_sem=send.at[step - 1],
                    recv_sem=got.at[step - 1],
                    device_id={axis: lax.rem(me + step, size)},
                    device_id_type=mesh,
                )
            )
        for copy in copies:
            copy.start()
        for copy in copies:
            copy.wait()

    exchange("dp", dp, groups, buf.at[0], in_dp, send_dp, got_dp)
    total = buf[0]
    for step in range(groups - 1):
        total = total + in_dp[step]
    row = 0
    for start in range(0, narrow.shape[1], lanes):
        narrow[:, start : start + lanes] = total[row : row + 1, 3 * lanes :]
        row += 1
    buf[1] = total
    kept = pl.ds(0, 3 * lanes)
    exchange("tensor", tensor, members, buf.at[1, :, kept], in_tensor, send_tensor, got_tensor)
    total = total[:, : 3 * lanes]
    for step in range(members - 1):
        total = total + in_tensor[step]
    for k in range(3):
        for r in range(8):
            wide[k : k + 1, r * lanes : (r + 1) * lanes] = total[r : r + 1, k * lanes : (k + 1) * lanes]


def sum_everywhere(ident, groups, members, vectors, narrows):
    depth = vectors[0].shape[1]
    counts = [len(many) for many in narrows]
    whole = pl.BlockSpec(memory_space=pltpu.VMEM)
    return pl.pallas_call(
        functools.partial(sum_everywhere_kernel, groups, members, counts),
        in_specs=[whole] * (3 + sum(counts)),
        out_specs=[whole] * 2,
        out_shape=[
            jax.ShapeDtypeStruct((8, depth), F32),
            jax.ShapeDtypeStruct((1, sum(many[0].shape[1] for many in narrows)), F32),
        ],
        scratch_shapes=[
            pltpu.VMEM((2, 8, depth // 2), F32),
            pltpu.VMEM((groups - 1, 8, depth // 2), F32),
            pltpu.VMEM((members - 1, 8, 3 * depth // 8), F32),
            pltpu.SemaphoreType.DMA((groups - 1,)),
            pltpu.SemaphoreType.DMA((groups - 1,)),
            pltpu.SemaphoreType.DMA((members - 1,)),
            pltpu.SemaphoreType.DMA((members - 1,)),
        ],
        compiler_params=pltpu.CompilerParams(collective_id=ident, has_side_effects=True),
        name="sum_everywhere",
    )(*vectors, *(v for many in narrows for v in many))


def per_device(
    inputs,
    block_ids,
    norm_gain,
    norm_bias,
    query_weight,
    query_bias,
    key_weight,
    key_bias,
    value_weight,
    value_bias,
    out_weight,
    out_bias,
    up_weight,
    up_bias,
    down_weight,
    down_bias,
    grad_out,
):
    seqs, length = block_ids.shape
    share, depth = inputs.shape
    width = query_weight.shape[1]
    units = up_weight.shape[1]
    groups, members = lax.axis_size("dp"), lax.axis_size("tensor")
    gain, shift = norm_gain.astype(F32)[None, :], norm_bias.astype(F32)[None, :]
    paired = groups == 4 and members == 8 and seqs == 4 and 2 * share == length
    me = lax.axis_index(TENSOR)
    if paired:
        chip = me // 2
        order = jnp.arange(3, -1, -1, dtype=jnp.int32) ^ chip
        inner = ((chip == 1) | (chip == 2)).astype(jnp.int32)
    else:
        order = jnp.arange(seqs, dtype=jnp.int32)

    ids = block_ids[order]
    column_ids = ids.reshape(seqs * length, 1)
    row_ids = ids.reshape(seqs, 1, length)
    pair = seqs // 2
    everything = seqs * length
    idents = iter(range(1, 100))

    if paired:
        cuts = lambda fraction: int(share * fraction) // 32 * 32
        g1 = cuts(0.25)
        rows, full, first_full, second_full, q, k, v, active, hidden, *tables, bias_part = opening(
            next(idents),
            inputs,
            norm_gain[None, :],
            norm_bias[None, :],
            grad_out,
            [query_weight, key_weight, value_weight, up_weight, out_weight, down_weight],
            [b[None, :] for b in (query_bias, key_bias, value_bias, up_bias)],
            groups,
            length,
            g1,
        )
        rows = rows.reshape(everything, depth)
        first_full = first_full.reshape(depth, 3 * width + units)

        def unheads(at, count, g, g_at, sums, sums_at, riding, wait_for=(), defer=False):
            return unattend(
                at,
                count,
                q,
                k,
                v,
                g,
                g_at,
                sums,
                sums_at,
                column_ids,
                row_ids,
                tables,
                riding=riding,
                ident="defer" if defer else next(idents),
                wait_for=wait_for,
            )

        def unprojected(count, grads, riding):
            return core_sum(
                unproject_body,
                next(idents),
                count,
                length,
                grads,
                first_full,
                depth,
                "unproject",
                riding=riding,
            )

        def forward(at, riding):
            return attend_mix(
                at, pair, q, k, v, column_ids, row_ids, active, second_full, riding, next(idents)
            )

        far_attended, far_sums, *far, full = forward(0, [gathering(full, (1, g1, share))])

        near_attended, near_sums, *near, full, end = forward(
            pair,
            [gathering(full, (2, 0, share), ("first", 0, share)), sending(far[0], "in", 0, share)],
        )

        ends, part = end, cuts(0.44)
        near_attended_grad, near_hidden_grad, near_up_sum, near_grad, near_sum, full, end, middle = chain(
            [
                unmix(None, second_full, hidden, width, pair, pair, length, ident="defer"),
                unheads(pair, pair, Made(0, 0), 0, near_sums, 0, [], defer=True),
            ],
            "unmix_unattend",
            [
                gathering(
                    full,
                    (3, part, share),
                    ("second", 0, share),
                    early=[(3, 0, part)],
                    middle=[("third", 0, part)],
                    late=[("third", part, share)],
                ),
                sending(far[1], "in", 0, share),
                summing(far[1], ends, "middle", 0, share),
            ],
            next(idents),
        )
        upstream = full.reshape(everything, depth)

        def outward(side_terms, middle_terms):
            def rides(lo, hi, side=None, middle=None):
                return [
                    summing(*side_terms, "side", lo, hi, side, inner_only=True),
                    summing(*middle_terms, "middle", lo, hi, middle),
                ]

            return rides

        send_out = outward((near[0], middle), (far[0], end))
        mine = near[1]
        part = cuts(0.4)

        def backward(at, g, hidden_grad, riding, ident, wait_for=()):
            return unattend_unproject(
                at,
                q,
                k,
                v,
                g,
                at,
                far_sums,
                at,
                column_ids,
                row_ids,
                tables,
                hidden_grad,
                at,
                first_full,
                riding + [Riding([a], [], False, 1, lambda *_: []) for a in wait_for],
                ident,
            )

        far_attended_grad, far_hidden_grad, far_up_sum, grads_0, sum_0, far_0, side, middle = chain(
            [
                unmix(upstream, second_full, hidden, width, 0, pair, length, ident="defer"),
                backward(0, Made(0, 0), Made(0, 1), [], "defer"),
            ],
            "unmix_unattend_unproject",
            send_out(0, share),
            next(idents),
        )
        output_terms = [mine, side, middle]

        part = cuts(0.5)
        second_part, end = outer_columns(
            [far_attended, near_attended],
            active,
            upstream,
            groups,
            riding=[sending(far_0, "in", 0, part)],
            ident=next(idents),
        )
        second_grad = lax.psum_scatter(second_part, DP, scatter_dimension=0)
        grads_1, sum_1, far_1, end = backward(
            1,
            far_attended_grad,
            far_hidden_grad,
            [sending(far_0, "in", part, share, end)],
            next(idents),
            [second_part],
        )
    else:
        tables = rotary_tables(length)
        first = jnp.concatenate([query_weight, key_weight, value_weight, up_weight], axis=1)
        second = jnp.concatenate([out_weight, down_weight], axis=0)
        bias = jnp.concatenate([query_bias, key_bias, value_bias, up_bias]).astype(F32)[None, :]
        first_full = lax.all_gather(first, "dp", axis=0, tiled=True)
        second_full = lax.all_gather(second, "dp", axis=1, tiled=True)
        rows = lax.all_gather(norm(inputs, gain, shift), "tensor", axis=0, tiled=True)
        upstream = lax.all_gather(grad_out, "tensor", axis=0, tiled=True)
        q, k, v, active, hidden = project(rows, first_full, bias, tables, width, units, length)
        attended, log_sums = attend(0, seqs, q, k, v, column_ids, row_ids)
        whole = each_tile(mix_body, [attended, active], second_full, depth, "mix")
        output_terms = [lax.psum_scatter(whole, TENSOR, scatter_dimension=0, tiled=True)]
        attended_grad, hidden_grad, up_sum = unmix(
            upstream, second_full, hidden, width, 0, seqs, length
        )
    if paired:
        ends, part = end, cuts(0.52)
        up_part, end, middle = outer_rows(
            rows,
            [far_hidden_grad, near_hidden_grad],
            riding=[sending(far_1, "in", 0, part), summing(far_1, ends, "middle", 0, part)],
            ident=next(idents),
        )
        up_grad = lax.psum_scatter(up_part, DP, scatter_dimension=0, tiled=True)
        *near, end, middle = unprojected(
            pair,
            [(near_grad, 0), (near_hidden_grad, 0)],
            [
                sending(far_1, "in", part, share, end),
                summing(far_1, ends, "middle", part, share, middle),
            ],
        )
        send_out = outward((near[0], middle), (far_0, end))
        part = cuts(0.5)
        first_part, side, middle = outer_rows(
            rows,
            [grads_0, grads_1, near_grad],
            riding=send_out(0, part),
            ident=next(idents),
            wait_for=[second_grad],
        )
        first_grad = lax.psum_scatter(first_part, DP, scatter_dimension=0, tiled=True)
        side, middle = launch(
            nothing,
            [],
            [],
            [],
            [],
            1,
            "finish",
            cost(1e9, 1e6),
            riding=send_out(part, share, side, middle),
            ident=next(idents),
            wait_for=[first_part],
        )
        terms = [near[1], side, middle]
    else:
        inner = jnp.ones((), jnp.int32)
        qkv_grad, qkv_sum = unattend(
            0, seqs, q, k, v, attended_grad, 0, log_sums, 0, column_ids, row_ids, tables
        )
        whole = each_tile(unproject_body, [qkv_grad, hidden_grad], first_full, depth, "unproject")
        terms = [lax.psum_scatter(whole, TENSOR, scatter_dimension=0, tiled=True)]
        (second_part,) = outer_columns([attended], active, upstream, groups)
        (first_part,) = outer_rows(rows, [qkv_grad])
        (up_part,) = outer_rows(rows, [hidden_grad])
        second_grad = lax.psum_scatter(second_part, DP, scatter_dimension=0)
        first_grad = lax.psum_scatter(first_part, DP, scatter_dimension=0, tiled=True)
        up_grad = lax.psum_scatter(up_part, DP, scatter_dimension=0, tiled=True)

    first_grad = first_grad.astype(F32)
    input_grad, output, gain_part, shift_part, out_grad, down_grad, up_grad = closing(
        inner[None],
        inputs,
        grad_out,
        norm_gain[None, :],
        out_bias[None, :],
        down_bias[None, :],
        second_grad,
        up_grad,
        width,
        terms,
        output_terms,
    )
    if paired:
        wide, narrow = sum_everywhere(
            next(idents),
            groups,
            members,
            [gain_part, shift_part, bias_part],
            [[sum_0, sum_1, near_sum], [near_up_sum, far_up_sum]],
        )
        gain_grad, shift_grad, outer_bias_grad = wide[0], wide[1], wide[2]
        qkv_sum, up_sum = narrow[0, : 3 * width], narrow[0, 3 * width :]
    else:
        gain_grad, shift_grad, outer_bias_grad = lax.psum(
            (gain_part[0], shift_part[0], jnp.sum(grad_out, axis=0, dtype=F32)), ("dp", "tensor")
        )
        qkv_sum, up_sum = lax.psum((qkv_sum[0], up_sum[0]), "dp")
    return (
        output,
        input_grad,
        gain_grad,
        shift_grad,
        first_grad[:, :width],
        qkv_sum[:width],
        first_grad[:, width : 2 * width],
        qkv_sum[width : 2 * width],
        first_grad[:, 2 * width :],
        qkv_sum[2 * width :],
        out_grad,
        outer_bias_grad,
        up_grad,
        up_sum,
        down_grad,
        outer_bias_grad,
    )


def solution(mesh):
    tokens = P(("dp", "tensor"), None)
    down = P("dp", "tensor")
    across = P("tensor", "dp")
    part = P("tensor")
    return jax.shard_map(
        per_device,
        mesh=mesh,
        in_specs=(
            tokens,
            P("dp", None),
            P(),
            P(),
            down,
            part,
            down,
            part,
            down,
            part,
            across,
            P(),
            down,
            part,
            across,
            P(),
            tokens,
        ),
        out_specs=(
            tokens,
            tokens,
            P(),
            P(),
            down,
            part,
            down,
            part,
            down,
            part,
            across,
            P(),
            down,
            part,
            across,
            P(),
        ),
        check_vma=False,
    )
```
